128 devices in a mesh: gz: 64 (over z, x_lo, y, core), gy: 2 (over x_hi).
Axes of the slice: x: 4 (x_hi: 2, x_lo: 2; x = x_hi * 2 + x_lo), y: 4, z: 4, core: 2. Of those that a mesh axis runs over, the one named last changes fastest.
Arguments:
- moving_image: float32 [2048, 128, 512], P('gz', 'gy'), may hold values from -6 to 6
- fixed_image: float32 [2048, 128, 512], P('gz', 'gy'), may hold values from -36 to 36
Outputs:
- solution: float32 [3, 128, 8, 32], P(None, 'gz')
- residual: float32 [3, 128, 8, 32], P(None, 'gz')
The draws below stay inside these ranges and needn't reach their ends.
All inputs are finite; a program needn't handle non-finite values.
Results may differ from the reference program's by a relative error of at most 0.0003.
Values sent between devices are 32-bit elements; how exact they have to be, the bound alone decides.
No kernel may reach another device: no remote copies, remote signals or barrier semaphores. Data moves between devices by JAX's collectives and lax.ppermute only.
A program may use at most 192 MiB of HBM per device.

```python
import jax
import jax.numpy as jnp
from jax import lax

KNOT = 16
ITERS = 2
NZ = 2048
NY = 128
NX = 512


def draw_fixed_image(key, part):
    position = jnp.arange(NZ, dtype=jnp.float32)
    growth = 3.0 * jnp.exp(jnp.log(3.0) * position / (NZ - 1))
    values = jnp.clip(jax.random.normal(key, (NZ, NY, NX), jnp.float32), -4.0, 4.0)
    return values * growth[:, None, None]


def steps_of(key, dims, cuts, low, high):
    def one(dim, parts):
        heights = jax.random.uniform(jax.random.fold_in(jax.random.fold_in(key, 6), dim), (parts,), jnp.float32, low / len(cuts), high / len(cuts))
        return jnp.repeat(jnp.exp(heights), dims[dim] // parts).reshape((-1,) + (1,) * (len(dims) - dim - 1))

    level = one(*cuts[0])
    for cut in cuts[1:]:
        level = level * one(*cut)
    return level


def noise(stream_key, extent, width, bound, split=(), kind=jnp.bfloat16):
    level = steps_of(stream_key, extent, split, -0.22, 0.18) if split else 1.0
    array = jax.random.normal(stream_key, extent, jnp.float32) * width * level
    return jnp.minimum(jnp.maximum(array, -bound), bound).astype(kind)


def setup_inputs(seed: int = 0) -> dict:
    key_of = jax.random.split(jax.random.key(seed), 3)
    moving_image = noise(key_of[0], (NZ, NY, NX), 1.0, 6.0, ((0, 64), (1, 2)), jnp.float32)
    fixed_image = draw_fixed_image(jax.random.fold_in(key_of[2], 71), 0)
    return {"moving_image": moving_image, "fixed_image": fixed_image}


data_weight = 1.0 / 256.0
smooth_weight = 0.1


def spline_weights(knot_len):
    t = (jnp.arange(knot_len, dtype=jnp.float32) + 0.5) / knot_len
    return jnp.stack([(1.0 - t) ** 3 / 6.0, (3.0 * t ** 3 - 6.0 * t ** 2 + 4.0) / 6.0, (-3.0 * t ** 3 + 3.0 * t ** 2 + 3.0 * t + 1.0) / 6.0, t ** 3 / 6.0])


def expand(coeffs, axis_pos, spline_table):
    turned = jnp.moveaxis(coeffs, axis_pos, -1)
    blocks = turned.shape[-1] - 3
    knot_len = spline_table.shape[1]
    summed = turned[..., 0:blocks, None] * spline_table[0]
    for j in range(1, 4):
        summed = summed + turned[..., j:j + blocks, None] * spline_table[j]
    summed = summed.reshape(turned.shape[:-1] + (blocks * knot_len,))
    return jnp.moveaxis(summed, -1, axis_pos)


def contract(spline_field, axis_pos, spline_table):
    turned = jnp.moveaxis(spline_field, axis_pos, -1)
    knot_len = spline_table.shape[1]
    blocks = turned.shape[-1] // knot_len
    pieces = turned.reshape(turned.shape[:-1] + (blocks, knot_len))
    widths = [(0, 0)] * (turned.ndim - 1)
    summed = jnp.zeros(turned.shape[:-1] + (blocks + 3,), spline_field.dtype)
    for j in range(4):
        folded = jnp.sum(pieces * spline_table[j], axis=-1)
        summed = summed + jnp.pad(folded, widths + [(j, 3 - j)])
    return jnp.moveaxis(summed, -1, axis_pos)


def central(extended, axis_pos):
    length = extended.shape[axis_pos] - 4

    def window(offset):
        return lax.slice_in_dim(extended, offset, offset + length, axis=axis_pos)

    return (8.0 * (window(3) - window(1)) - (window(4) - window(0))) / 12.0


def rim_pad(field_in, axis_pos):
    widths = [(0, 0)] * field_in.ndim
    widths[axis_pos] = (2, 2)
    return jnp.pad(field_in, widths)


def slab_gradient(moving_image, first_row, slab_depth):
    plane_count = moving_image.shape[0]
    center = lax.dynamic_slice_in_dim(moving_image, first_row, slab_depth, 0)
    lower_rim = lax.dynamic_slice_in_dim(moving_image, jnp.maximum(first_row - 2, 0), 2, 0)
    upper_rim = lax.dynamic_slice_in_dim(moving_image, jnp.minimum(first_row + slab_depth, plane_count - 2), 2, 0)
    lower_rim = jnp.where(first_row > 0, lower_rim, jnp.zeros_like(lower_rim))
    upper_rim = jnp.where(first_row + slab_depth < plane_count, upper_rim, jnp.zeros_like(upper_rim))
    extended = jnp.concatenate([lower_rim, center, upper_rim], 0)
    gradient = jnp.stack([central(extended, 0), central(rim_pad(center, 1), 1), central(rim_pad(center, 2), 2)])
    return center, gradient


def volume_pass(moving_image, fixed_image, coeffs, with_field, spline_table):
    slab_depth = 32
    slab_count = moving_image.shape[0] // slab_depth
    blocks = slab_depth // KNOT
    ctl_z = moving_image.shape[0] // KNOT
    ctl_y = moving_image.shape[1] // KNOT
    ctl_x = moving_image.shape[2] // KNOT
    padded = jnp.pad(coeffs, ((0, 0), (1, 2), (1, 2), (1, 2)))

    def slab_step(totals, slab_index):
        first_row = (slab_index * slab_depth).astype(jnp.int32)
        center, gradient = slab_gradient(moving_image, first_row, slab_depth)
        if with_field:
            pieces = lax.dynamic_slice_in_dim(padded, (slab_index * blocks).astype(jnp.int32), blocks + 3, 1)
            spline_field = expand(expand(expand(pieces, 1, spline_table), 2, spline_table), 3, spline_table)
            weights = jnp.sum(gradient * spline_field, 0)
        else:
            weights = center - lax.dynamic_slice_in_dim(fixed_image, first_row, slab_depth, 0)
        returned = contract(gradient * weights[None], 3, spline_table)[..., 1:ctl_x + 1]
        returned = contract(returned, 2, spline_table)[:, :, 1:ctl_y + 1]
        returned = contract(returned, 1, spline_table)
        where_to = (slab_index * blocks).astype(jnp.int32)
        current = lax.dynamic_slice_in_dim(totals, where_to, blocks + 3, 1)
        totals = lax.dynamic_update_slice_in_dim(totals, current + returned, where_to, 1)
        return totals, None

    start_totals = jnp.zeros((3, ctl_z + 3, ctl_y, ctl_x), jnp.float32)
    totals, unused = lax.scan(slab_step, start_totals, jnp.arange(slab_count, dtype=jnp.int32))
    return totals[:, 1:ctl_z + 1]


def smoothing(coeffs):
    padded = jnp.pad(coeffs, ((0, 0), (1, 1), (1, 1), (1, 1)))
    neighbours = padded[:, :-2, 1:-1, 1:-1] + padded[:, 2:, 1:-1, 1:-1]
    neighbours = neighbours + padded[:, 1:-1, :-2, 1:-1] + padded[:, 1:-1, 2:, 1:-1]
    neighbours = neighbours + padded[:, 1:-1, 1:-1, :-2] + padded[:, 1:-1, 1:-1, 2:]
    return 6.0 * coeffs - neighbours


def reference(moving_image, fixed_image):
    spline_table = spline_weights(KNOT)
    shape_ctl = (3, moving_image.shape[0] // KNOT, moving_image.shape[1] // KNOT, moving_image.shape[2] // KNOT)
    blank = jnp.zeros(shape_ctl, jnp.float32)
    right_side = -data_weight * volume_pass(moving_image, fixed_image, blank, False, spline_table)

    def hessian(coeffs):
        data_term = volume_pass(moving_image, fixed_image, coeffs, True, spline_table)
        return data_weight * data_term + smooth_weight * smoothing(coeffs)

    solution = jnp.zeros(shape_ctl, jnp.float32)
    residual = right_side
    direction = right_side
    norm_now = jnp.sum(residual * residual)
    for iteration in range(ITERS):
        image_vec = hessian(direction)
        step_size = norm_now / jnp.sum(direction * image_vec)
        solution = solution + step_size * direction
        residual = residual - step_size * image_vec
        norm_next = jnp.sum(residual * residual)
        direction = residual + (norm_next / norm_now) * direction
        norm_now = norm_next
    return solution, residual
```

```python
import functools

import jax
import jax.numpy as jnp
import ml_dtypes
import numpy as np
from jax import lax
from jax.experimental import pallas as pl
from jax.experimental.pallas import tpu as pltpu
from jax.sharding import PartitionSpec as P

KNOT = 16
data_weight = 1.0 / 256.0
smooth_weight = 0.1

BF = jnp.bfloat16
F32 = jnp.float32
NZ, NY, NX = 32, 64, 512
CHUNK = 8
STEPS = NZ // CHUNK
ROWS = CHUNK * NY
PLANES, CY, CX = 5, 8, 32
CTL = PLANES * CY
KPAD = 48


def split(array):
    high = array.astype(ml_dtypes.bfloat16)
    low = (array - high.astype(np.float64)).astype(ml_dtypes.bfloat16)
    return high, low


def tables():
    t = (np.arange(KNOT) + 0.5) / KNOT
    weights = np.stack(
        [
            (1 - t) ** 3 / 6,
            (3 * t**3 - 6 * t**2 + 4) / 6,
            (-3 * t**3 + 3 * t**2 + 3 * t + 1) / 6,
            t**3 / 6,
        ]
    )

    def along(blocks, first_block, points, first_point):
        out = np.zeros((blocks * KNOT, points))
        for block in range(blocks):
            for j in range(4):
                point = first_block + block + j - 1 - first_point
                if 0 <= point < points:
                    out[block * KNOT : (block + 1) * KNOT, point] = weights[j]
        return out

    along_z = along(NZ // KNOT, 0, PLANES, -1)
    halves = []
    for half in range(2):
        along_y = along(NY // KNOT, half * (NY // KNOT), CY, 0)
        halves.append(np.einsum("zp,yq->zypq", along_z, along_y).reshape(NZ * NY, CTL))
    high, low = split(np.stack(halves))
    widths = ((0, 0), (0, 0), (0, KPAD - CTL))
    high48, low48 = (np.pad(a, widths) for a in (high, low))
    out_table = np.concatenate([high48, low48, high48, low48], axis=2)
    back_table = np.concatenate([high, low], axis=2).transpose(0, 2, 1)
    along_x = along(NX // KNOT, 0, CX, 0)
    rows = np.zeros((128, 3 * NX))
    for c in range(3):
        rows[c * CX : (c + 1) * CX, c * NX : (c + 1) * NX] = along_x.T
    x_table = np.concatenate(split(rows), axis=0)
    return out_table, np.ascontiguousarray(back_table), x_table


def halves_of(value):
    high = value.astype(BF)
    return high, (value - high.astype(F32)).astype(BF)


def contracted(parts, back_ref, x_ref):
    both = lax.dot_general(
        parts[...], x_ref[...], (((1,), (1,)), ((), ())), preferred_element_type=F32
    )
    rows = both[:ROWS, :128] + (both[:ROWS, 128:] + both[ROWS:, :128])
    high, low = halves_of(rows)
    back = back_ref[0]
    terms = jnp.dot(back, high, preferred_element_type=F32)
    rest = jnp.dot(back[:CTL], low, preferred_element_type=F32)
    return terms[:CTL] + (terms[CTL:] + rest)


def put_parts(parts, z, c, value):
    high, low = halves_of(value)
    at = pl.multiple_of(z * NY, NY)
    parts[pl.ds(at, NY), c * NX : (c + 1) * NX] = high
    parts[pl.ds(ROWS + at, NY), c * NX : (c + 1) * NX] = low


def first_kernel(
    half, moving, z_low, z_high, fixed, y_rows, back, xt, grad, out, padded, parts, sems
):
    step = pl.program_id(0)

    def chunk_copy(j):
        return pltpu.make_async_copy(
            moving.at[pl.ds(j * CHUNK, CHUNK)],
            padded.at[pl.ds(2 + j * CHUNK, CHUNK), pl.ds(8, NY)],
            sems.at[j],
        )

    def low_copy():
        return pltpu.make_async_copy(
            z_low, padded.at[pl.ds(0, 2), pl.ds(8, NY)], sems.at[STEPS]
        )

    def high_copy():
        return pltpu.make_async_copy(
            z_high, padded.at[pl.ds(2 + NZ, 2), pl.ds(8, NY)], sems.at[STEPS + 1]
        )

    @pl.when(step == 0)
    def _():
        low_copy().start()
        for j in range(STEPS):
            chunk_copy(j).start()
        high_copy().start()
        low_copy().wait()
        chunk_copy(0).wait()
        out[...] = jnp.zeros_like(out)

    for j in range(1, STEPS):

        @pl.when(step == j - 1)
        def _(j=j):
            chunk_copy(j).wait()

    @pl.when(step == STEPS - 1)
    def _():
        high_copy().wait()

    upper = half[0] == 0
    lane = lax.broadcasted_iota(jnp.int32, (NY, NX), 1)

    def plane(z, carry):
        at = 2 + step * CHUNK + z
        rows = y_rows[z]
        blank = jnp.zeros_like(rows)
        padded[at, 6:8, :] = jnp.where(upper, blank, rows)
        padded[at, 72:74, :] = jnp.where(upper, rows, blank)
        center = padded[at, 8:72, :]

        def at_z(k):
            return padded[at + k, 8:72, :]

        def at_y(k):
            return padded[at, 8 + k : 72 + k, :]

        def at_x(k):
            moved = pltpu.roll(center, (-k) % NX, 1)
            inside = lane < NX - k if k > 0 else lane >= -k
            return jnp.where(inside, moved, 0.0)

        difference = center - fixed[z]
        for c, near in enumerate((at_z, at_y, at_x)):
            slope = 8.0 * (near(1) - near(-1)) - (near(2) - near(-2))
            grad[c, z] = slope
            put_parts(parts, z, c, slope * difference)
        return carry

    lax.fori_loop(0, CHUNK, plane, 0)
    out[...] += contracted(parts, back, xt)

    @pl.when(step == STEPS - 1)
    def _():
        out[...] = out[...] * (-data_weight / 12.0)


def hessian_kernel(
    half, ctl, base, grad, front, back, xt, out, sums, spread, field, parts, square
):
    step = pl.program_id(0)

    @pl.when(step == 0)
    def _():
        high, low = halves_of(ctl[...])
        first, second = xt[:128], xt[128:]
        value = jnp.dot(high, first, preferred_element_type=F32)
        value += jnp.dot(low, first, preferred_element_type=F32)
        value += jnp.dot(high, second, preferred_element_type=F32)
        value = jnp.concatenate([value, jnp.zeros((KPAD - CTL, 3 * NX), F32)], 0)
        high, low = halves_of(value)
        for j, part in enumerate((high, high, low, low)):
            spread[j * KPAD : (j + 1) * KPAD] = part
        out[...] = jnp.zeros_like(out)
        square[...] = jnp.zeros_like(square)

    field[...] = jnp.dot(front[0], spread[...], preferred_element_type=F32)

    def plane(z, carry):
        at = pl.multiple_of(z * NY, NY)
        rows = pl.ds(at, NY)
        slopes = [grad[c, z] for c in range(3)]
        weight = slopes[0] * field[rows, 0:NX]
        weight += slopes[1] * field[rows, NX : 2 * NX]
        weight += slopes[2] * field[rows, 2 * NX : 3 * NX]
        squared = weight * weight
        square[...] += jnp.sum(squared.reshape(NY // 8, 8, NX), axis=0)
        for c in range(3):
            put_parts(parts, z, c, slopes[c] * weight)
        return carry

    lax.fori_loop(0, CHUNK, plane, 0)
    out[...] += contracted(parts, back, xt)

    @pl.when(step == STEPS - 1)
    def _():
        scale = data_weight / 144.0
        whole = ctl[...]
        owned = whole[CY : 3 * CY]
        sub = lax.broadcasted_iota(jnp.int32, (2 * CY, 128), 0) % CY
        lane = lax.broadcasted_iota(jnp.int32, (2 * CY, 128), 1) % CX
        near = whole[0 : 2 * CY] + whole[2 * CY : 4 * CY]
        near += jnp.where(sub > 0, pltpu.roll(owned, 1, 0), 0.0)
        near += jnp.where(sub < CY - 1, pltpu.roll(owned, 2 * CY - 1, 0), 0.0)
        near += jnp.where(lane > 0, pltpu.roll(owned, 1, 1), 0.0)
        near += jnp.where(lane < CX - 1, pltpu.roll(owned, 127, 1), 0.0)
        smooth = (0.5 * smooth_weight) * (6.0 * owned - near)
        out[...] = out[...] * scale
        out[CY : 3 * CY] += smooth
        first = base[...]

        def total(value):
            return jnp.sum(jnp.sum(value, axis=0, keepdims=True), axis=1, keepdims=True)

        whole_square = total(square[...]) * scale + total(smooth * owned)
        lines = [
            0.5 * total(first * first),
            0.5 * total(first * owned),
            0.5 * total(owned * owned),
            whole_square,
        ]
        which = lax.broadcasted_iota(jnp.int32, (8, 128), 0)
        tile = jnp.zeros((8, 128), F32)
        for j, line in enumerate(lines):
            tile = jnp.where(which == j, line, tile)
        sums[...] = tile


def vmem_params():
    return pltpu.CompilerParams(
        dimension_semantics=("arbitrary",), vmem_limit_bytes=48 * 1024 * 1024
    )


def whole_spec(shape):
    return pl.BlockSpec(shape, lambda i, h: (0,) * len(shape))


BACK_SPEC = ((1, 2 * CTL, ROWS), lambda i, h: (h[0], 0, i))
GRAD_SPEC = ((3, CHUNK, NY, NX), lambda i, h: (0, i, 0, 0))


def first_pass(half, moving, z_low, z_high, fixed, y_rows, back_table, x_table):
    return pl.pallas_call(
        first_kernel,
        grid_spec=pltpu.PrefetchScalarGridSpec(
            num_scalar_prefetch=1,
            grid=(STEPS,),
            in_specs=[
                pl.BlockSpec(memory_space=pl.ANY),
                pl.BlockSpec(memory_space=pl.ANY),
                pl.BlockSpec(memory_space=pl.ANY),
                pl.BlockSpec((CHUNK, NY, NX), lambda i, h: (i, 0, 0)),
                pl.BlockSpec((CHUNK, 2, NX), lambda i, h: (i, 0, 0)),
                pl.BlockSpec(*BACK_SPEC),
                whole_spec((256, 3 * NX)),
            ],
            out_specs=[pl.BlockSpec(*GRAD_SPEC), whole_spec((CTL, 128))],
            scratch_shapes=[
                pltpu.VMEM((NZ + 4, NY + 16, NX), F32),
                pltpu.VMEM((2 * ROWS, 3 * NX), BF),
                pltpu.SemaphoreType.DMA((STEPS + 2,)),
            ],
        ),
        out_shape=[
            jax.ShapeDtypeStruct((3, NZ, NY, NX), F32),
            jax.ShapeDtypeStruct((CTL, 128), F32),
        ],
        compiler_params=vmem_params(),
        name="first",
    )(half, moving, z_low, z_high, fixed, y_rows, back_table, x_table)


def hessian_pass(half, ctl, base, grad, front_table, back_table, x_table):
    return pl.pallas_call(
        hessian_kernel,
        grid_spec=pltpu.PrefetchScalarGridSpec(
            num_scalar_prefetch=1,
            grid=(STEPS,),
            in_specs=[
                whole_spec((CTL, 128)),
                whole_spec((2 * CY, 128)),
                pl.BlockSpec(*GRAD_SPEC),
                pl.BlockSpec((1, ROWS, 4 * KPAD), lambda i, h: (h[0], i, 0)),
                pl.BlockSpec(*BACK_SPEC),
                whole_spec((256, 3 * NX)),
            ],
            out_specs=[whole_spec((CTL, 128)), whole_spec((8, 128))],
            scratch_shapes=[
                pltpu.VMEM((4 * KPAD, 3 * NX), BF),
                pltpu.VMEM((ROWS, 3 * NX), F32),
                pltpu.VMEM((2 * ROWS, 3 * NX), BF),
                pltpu.VMEM((8, NX), F32),
            ],
        ),
        out_shape=[
            jax.ShapeDtypeStruct((CTL, 128), F32),
            jax.ShapeDtypeStruct((8, 128), F32),
        ],
        compiler_params=vmem_params(),
        name="hessian",
    )(half, ctl, base, grad, front_table, back_table, x_table)


def passed_along(value, axis, steps):
    count = lax.axis_size(axis)
    initial, last = (max(0, -steps), min(count, count - steps))
    return lax.ppermute(value, axis, [(source, source + steps) for source in range(initial, last)])


def swapped(value):
    return lax.ppermute(value, "gy", [(0, 1), (1, 0)])


def owned_sum(whole):
    from_above = passed_along(whole[:CY], "gz", -1)
    from_below = passed_along(whole[3 * CY :], "gz", 1)
    owned = whole[CY : 3 * CY] + from_below
    return owned + jnp.pad(from_above, ((CY, 0), (0, 0)))


def with_rims(owned):
    lower = passed_along(owned[CY:], "gz", 1)
    upper = passed_along(owned, "gz", -1)
    return jnp.concatenate([lower, owned, upper], 0)


def local(moving, fixed):
    half_id = lax.axis_index("gy").astype(jnp.int32)
    half = half_id.reshape(1)
    front, back, xt = (jnp.asarray(a) for a in tables())

    z_low = passed_along(moving[-2:], "gz", 1)
    z_high = passed_along(moving[:2], "gz", -1)
    y_rows = swapped(jnp.where(half_id == 0, moving[:, -2:], moving[:, :2]))

    grad, part = first_pass(half, moving, z_low, z_high, fixed, y_rows, back, xt)
    b = owned_sum(part + swapped(part))
    part, _ = hessian_pass(half, with_rims(b), b, grad, front, back, xt)
    u = owned_sum(part + swapped(part))
    part, sums = hessian_pass(half, with_rims(u), b, grad, front, back, xt)
    both = jnp.concatenate([part, sums], 0)
    both = both + swapped(both)
    v = owned_sum(both[:CTL])
    sums = both[CTL:]
    for mask in (1, 2, 6, 8, 16, 48):
        sums = sums + lax.ppermute(sums, "gz", [(i, i ^ mask) for i in range(64)])

    bb, bu, uu, uv = (sums[j : j + 1] for j in range(4))
    a0 = bb / bu
    rr1 = bb - 2.0 * a0 * bu + a0 * a0 * uu
    beta = rr1 / bb
    more = 1.0 + beta
    a1 = rr1 / (more * more * bu - 2.0 * more * a0 * uu + a0 * a0 * uv)
    solution = a0 * b + a1 * (more * b - a0 * u)
    residual = (b - a0 * u) - a1 * (more * u - a0 * v)

    def placed(value):
        turned = value.reshape(2, CY, 128)[:, :, : 3 * CX].reshape(2, CY, 3, CX)
        return turned.transpose(2, 0, 1, 3)

    return placed(solution), placed(residual)


def solution(mesh):
    in_specs = (P("gz", "gy", None), P("gz", "gy", None))
    out_specs = (P(None, "gz", None, None), P(None, "gz", None, None))
    return jax.shard_map(local, mesh=mesh, in_specs=in_specs, out_specs=out_specs, check_vma=False)
```

```python
import functools

import jax
import jax.numpy as jnp
import ml_dtypes
import numpy as np
from jax import lax
from jax.experimental import pallas as pl
from jax.experimental.pallas import tpu as pltpu
from jax.sharding import PartitionSpec as P

KNOT = 16
data_weight = 1.0 / 256.0
smooth_weight = 0.1

BF = jnp.bfloat16
F32 = jnp.float32
NZ, NY, NX = 32, 64, 512
CHUNK = 8
STEPS = NZ // CHUNK
ROWS = CHUNK * NY
PLANES, CY, CX = 5, 8, 32
CTL = PLANES * CY
KPAD = 48


def split(array):
    high = array.astype(ml_dtypes.bfloat16)
    low = (array - high.astype(np.float64)).astype(ml_dtypes.bfloat16)
    return high, low


def tables():
    t = (np.arange(KNOT) + 0.5) / KNOT
    weights = np.stack(
        [
            (1 - t) ** 3 / 6,
            (3 * t**3 - 6 * t**2 + 4) / 6,
            (-3 * t**3 + 3 * t**2 + 3 * t + 1) / 6,
            t**3 / 6,
        ]
    )

    def along(blocks, first_block, points, first_point):
        out = np.zeros((blocks * KNOT, points))
        for block in range(blocks):
            for j in range(4):
                point = first_block + block + j - 1 - first_point
                if 0 <= point < points:
                    out[block * KNOT : (block + 1) * KNOT, point] = weights[j]
        return out

    along_z = along(NZ // KNOT, 0, PLANES, -1)
    halves = []
    for half in range(2):
        along_y = along(NY // KNOT, half * (NY // KNOT), CY, 0)
        halves.append(np.einsum("zp,yq->zypq", along_z, along_y).reshape(NZ * NY, CTL))
    high, low = split(np.stack(halves))
    widths = ((0, 0), (0, 0), (0, KPAD - CTL))
    high48, low48 = (np.pad(a, widths) for a in (high, low))
    out_table = np.concatenate([high48, low48, high48, low48], axis=2)
    back_table = np.concatenate([high, low], axis=2).transpose(0, 2, 1)
    along_x = along(NX // KNOT, 0, CX, 0)
    rows = np.zeros((128, 3 * NX))
    for c in range(3):
        rows[c * CX : (c + 1) * CX, c * NX : (c + 1) * NX] = along_x.T
    x_table = np.concatenate(split(rows), axis=0)
    return out_table, np.ascontiguousarray(back_table), x_table


def halves_of(value):
    high = value.astype(BF)
    return high, (value - high.astype(F32)).astype(BF)


def contracted(parts, back_ref, x_ref):
    both = lax.dot_general(
        parts[...], x_ref[...], (((1,), (1,)), ((), ())), preferred_element_type=F32
    )
    rows = both[:ROWS, :128] + (both[:ROWS, 128:] + both[ROWS:, :128])
    high, low = halves_of(rows)
    back = back_ref[0]
    terms = jnp.dot(back, high, preferred_element_type=F32)
    rest = jnp.dot(back[:CTL], low, preferred_element_type=F32)
    return terms[:CTL] + (terms[CTL:] + rest)


def put_parts(parts, z, c, value):
    high, low = halves_of(value)
    at = pl.multiple_of(z * NY, NY)
    parts[pl.ds(at, NY), c * NX : (c + 1) * NX] = high
    parts[pl.ds(ROWS + at, NY), c * NX : (c + 1) * NX] = low


def first_kernel(
    half, moving, z_low, z_high, fixed, y_rows, back, xt, grad, out, padded, parts, sems
):
    step = pl.program_id(0)

    def chunk_copy(j):
        return pltpu.make_async_copy(
            moving.at[pl.ds(j * CHUNK, CHUNK)],
            padded.at[pl.ds(2 + j * CHUNK, CHUNK), pl.ds(8, NY)],
            sems.at[j],
        )

    def low_copy():
        return pltpu.make_async_copy(
            z_low, padded.at[pl.ds(0, 2), pl.ds(8, NY)], sems.at[STEPS]
        )

    def high_copy():
        return pltpu.make_async_copy(
            z_high, padded.at[pl.ds(2 + NZ, 2), pl.ds(8, NY)], sems.at[STEPS + 1]
        )

    @pl.when(step == 0)
    def _():
        low_copy().start()
        for j in range(STEPS):
            chunk_copy(j).start()
        high_copy().start()
        low_copy().wait()
        chunk_copy(0).wait()
        out[...] = jnp.zeros_like(out)

    for j in range(1, STEPS):

        @pl.when(step == j - 1)
        def _(j=j):
            chunk_copy(j).wait()

    @pl.when(step == STEPS - 1)
    def _():
        high_copy().wait()

    upper = half[0] == 0
    lane = lax.broadcasted_iota(jnp.int32, (NY, NX), 1)

    def plane(z, carry):
        at = 2 + step * CHUNK + z
        rows = y_rows[z]
        blank = jnp.zeros_like(rows)
        padded[at, 6:8, :] = jnp.where(upper, blank, rows)
        padded[at, 72:74, :] = jnp.where(upper, rows, blank)
        center = padded[at, 8:72, :]

        def at_z(k):
            return padded[at + k, 8:72, :]

        def at_y(k):
            return padded[at, 8 + k : 72 + k, :]

        def at_x(k):
            moved = pltpu.roll(center, (-k) % NX, 1)
            inside = lane < NX - k if k > 0 else lane >= -k
            return jnp.where(inside, moved, 0.0)

        difference = center - fixed[z]
        for c, near in enumerate((at_z, at_y, at_x)):
            slope = 8.0 * (near(1) - near(-1)) - (near(2) - near(-2))
            grad[c, z] = slope
            put_parts(parts, z, c, slope * difference)
        return carry

    lax.fori_loop(0, CHUNK, plane, 0)
    out[...] += contracted(parts, back, xt)

    @pl.when(step == STEPS - 1)
    def _():
        out[...] = out[...] * (-data_weight / 12.0)


def hessian_kernel(
    half, ctl, base, grad, front, back, xt, out, sums, spread, field, parts, square
):
    step = pl.program_id(0)

    @pl.when(step == 0)
    def _():
        high, low = halves_of(ctl[...])
        first, second = xt[:128], xt[128:]
        value = jnp.dot(high, first, preferred_element_type=F32)
        value += jnp.dot(low, first, preferred_element_type=F32)
        value += jnp.dot(high, second, preferred_element_type=F32)
        value = jnp.concatenate([value, jnp.zeros((KPAD - CTL, 3 * NX), F32)], 0)
        high, low = halves_of(value)
        for j, part in enumerate((high, high, low, low)):
            spread[j * KPAD : (j + 1) * KPAD] = part
        out[...] = jnp.zeros_like(out)
        square[...] = jnp.zeros_like(square)

    field[...] = jnp.dot(front[0], spread[...], preferred_element_type=F32)

    def plane(z, carry):
        at = pl.multiple_of(z * NY, NY)
        rows = pl.ds(at, NY)
        slopes = [grad[c, z] for c in range(3)]
        weight = slopes[0] * field[rows, 0:NX]
        weight += slopes[1] * field[rows, NX : 2 * NX]
        weight += slopes[2] * field[rows, 2 * NX : 3 * NX]
        squared = weight * weight
        square[...] += jnp.sum(squared.reshape(NY // 8, 8, NX), axis=0)
        for c in range(3):
            put_parts(parts, z, c, slopes[c] * weight)
        return carry

    lax.fori_loop(0, CHUNK, plane, 0)
    out[...] += contracted(parts, back, xt)

    @pl.when(step == STEPS - 1)
    def _():
        scale = data_weight / 144.0
        whole = ctl[...]
        owned = whole[CY : 3 * CY]
        sub = lax.broadcasted_iota(jnp.int32, (2 * CY, 128), 0) % CY
        lane = lax.broadcasted_iota(jnp.int32, (2 * CY, 128), 1) % CX
        near = whole[0 : 2 * CY] + whole[2 * CY : 4 * CY]
        near += jnp.where(sub > 0, pltpu.roll(owned, 1, 0), 0.0)
        near += jnp.where(sub < CY - 1, pltpu.roll(owned, 2 * CY - 1, 0), 0.0)
        near += jnp.where(lane > 0, pltpu.roll(owned, 1, 1), 0.0)
        near += jnp.where(lane < CX - 1, pltpu.roll(owned, 127, 1), 0.0)
        smooth = (0.5 * smooth_weight) * (6.0 * owned - near)
        out[...] = out[...] * scale
        out[CY : 3 * CY] += smooth
        first = base[...]

        def total(value):
            return jnp.sum(jnp.sum(value, axis=0, keepdims=True), axis=1, keepdims=True)

        whole_square = total(square[...]) * scale + total(smooth * owned)
        lines = [
            0.5 * total(first * first),
            0.5 * total(first * owned),
            0.5 * total(owned * owned),
            whole_square,
        ]
        which = lax.broadcasted_iota(jnp.int32, (8, 128), 0)
        tile = jnp.zeros((8, 128), F32)
        for j, line in enumerate(lines):
            tile = jnp.where(which == j, line, tile)
        sums[...] = tile


def vmem_params():
    return pltpu.CompilerParams(
        dimension_semantics=("arbitrary",), vmem_limit_bytes=48 * 1024 * 1024
    )


def whole_spec(shape):
    return pl.BlockSpec(shape, lambda i, h: (0,) * len(shape))


BACK_SPEC = ((1, 2 * CTL, ROWS), lambda i, h: (h[0], 0, i))
GRAD_SPEC = ((3, CHUNK, NY, NX), lambda i, h: (0, i, 0, 0))


def first_pass(half, moving, z_low, z_high, fixed, y_rows, back_table, x_table):
    return pl.pallas_call(
        first_kernel,
        grid_spec=pltpu.PrefetchScalarGridSpec(
            num_scalar_prefetch=1,
            grid=(STEPS,),
            in_specs=[
                pl.BlockSpec(memory_space=pl.ANY),
                pl.BlockSpec(memory_space=pl.ANY),
                pl.BlockSpec(memory_space=pl.ANY),
                pl.BlockSpec((CHUNK, NY, NX), lambda i, h: (i, 0, 0)),
                pl.BlockSpec((CHUNK, 2, NX), lambda i, h: (i, 0, 0)),
                pl.BlockSpec(*BACK_SPEC),
                whole_spec((256, 3 * NX)),
            ],
            out_specs=[pl.BlockSpec(*GRAD_SPEC), whole_spec((CTL, 128))],
            scratch_shapes=[
                pltpu.VMEM((NZ + 4, NY + 16, NX), F32),
                pltpu.VMEM((2 * ROWS, 3 * NX), BF),
                pltpu.SemaphoreType.DMA((STEPS + 2,)),
            ],
        ),
        out_shape=[
            jax.ShapeDtypeStruct((3, NZ, NY, NX), F32),
            jax.ShapeDtypeStruct((CTL, 128), F32),
        ],
        compiler_params=vmem_params(),
        name="first",
    )(half, moving, z_low, z_high, fixed, y_rows, back_table, x_table)


def hessian_pass(half, ctl, base, grad, front_table, back_table, x_table):
    return pl.pallas_call(
        hessian_kernel,
        grid_spec=pltpu.PrefetchScalarGridSpec(
            num_scalar_prefetch=1,
            grid=(STEPS,),
            in_specs=[
                whole_spec((CTL, 128)),
                whole_spec((2 * CY, 128)),
                pl.BlockSpec(*GRAD_SPEC),
                pl.BlockSpec((1, ROWS, 4 * KPAD), lambda i, h: (h[0], i, 0)),
                pl.BlockSpec(*BACK_SPEC),
                whole_spec((256, 3 * NX)),
            ],
            out_specs=[whole_spec((CTL, 128)), whole_spec((8, 128))],
            scratch_shapes=[
                pltpu.VMEM((4 * KPAD, 3 * NX), BF),
                pltpu.VMEM((ROWS, 3 * NX), F32),
                pltpu.VMEM((2 * ROWS, 3 * NX), BF),
                pltpu.VMEM((8, NX), F32),
            ],
        ),
        out_shape=[
            jax.ShapeDtypeStruct((CTL, 128), F32),
            jax.ShapeDtypeStruct((8, 128), F32),
        ],
        compiler_params=vmem_params(),
        name="hessian",
    )(half, ctl, base, grad, front_table, back_table, x_table)


def passed_along(value, axis, steps):
    count = lax.axis_size(axis)
    initial, last = (max(0, -steps), min(count, count - steps))
    return lax.ppermute(value, axis, [(source, source + steps) for source in range(initial, last)])


def swapped(value):
    return lax.ppermute(value, "gy", [(0, 1), (1, 0)])


def paired(value, mask):
    count = lax.axis_size("gz")
    return lax.ppermute(value, "gz", [(i, i ^ mask) for i in range(count)])


def outer_paired(value):
    count = lax.axis_size("gz")
    pairs = [(i, i + 1) for i in range(1, count - 1, 2)]
    return lax.ppermute(value, "gz", pairs + [(j, i) for i, j in pairs])


def pair_sum(lower, own, other):
    first, second = jnp.where(lower, own, other), jnp.where(lower, other, own)
    widths = ((0, 2 * CY), (0, 0)), ((2 * CY, 0), (0, 0))
    return jnp.pad(first, widths[0]) + jnp.pad(second, widths[1])


def outer_terms(lower, seven):
    return outer_paired(jnp.where(lower, seven[: 3 * CY], seven[4 * CY :]))


def all_planes(lower, part):
    part = part + swapped(part)
    seven = pair_sum(lower, part, paired(part, 1))
    three = outer_terms(lower, seven)
    one = paired(jnp.where(lower, three[2 * CY :], three[:CY]), 1)
    low = jnp.concatenate([three, jnp.zeros((CY, 128), F32), one], 0) + seven[: 5 * CY]
    high = jnp.concatenate([one, jnp.zeros((CY, 128), F32), three], 0) + seven[2 * CY :]
    row = lax.broadcasted_iota(jnp.int32, (CTL, 128), 0)
    at = lax.axis_index("gz") * (2 * CY) - CY + row
    inside = (at >= 0) & (at < lax.axis_size("gz") * (2 * CY))
    return jnp.where(inside, jnp.where(lower, low, high), 0.0)


def local(moving, fixed):
    half_id = lax.axis_index("gy").astype(jnp.int32)
    half = half_id.reshape(1)
    lower = lax.axis_index("gz") % 2 == 0
    front, back, xt = (jnp.asarray(a) for a in tables())

    z_low = passed_along(moving[-2:], "gz", 1)
    z_high = passed_along(moving[:2], "gz", -1)
    y_rows = swapped(jnp.where(half_id == 0, moving[:, -2:], moving[:, :2]))

    grad, part = first_pass(half, moving, z_low, z_high, fixed, y_rows, back, xt)
    b_planes = all_planes(lower, part)
    b = b_planes[CY : 3 * CY]
    part, _ = hessian_pass(half, b_planes, b, grad, front, back, xt)
    u_planes = all_planes(lower, part)
    u = u_planes[CY : 3 * CY]
    part, sums = hessian_pass(half, u_planes, b, grad, front, back, xt)
    both = jnp.concatenate([part, sums], 0)
    both = both + swapped(both)
    other = paired(both, 1)
    seven = pair_sum(lower, both[:CTL], other[:CTL])
    sums = both[CTL:] + other[CTL:]
    three = outer_terms(lower, seven)
    sums = sums + paired(sums, 2)
    sums, three = lax.optimization_barrier((sums, three))
    for mask in (6, 8, 16, 48):
        sums = sums + paired(sums, mask)
    v_low = seven[CY : 3 * CY] + three[CY:]
    v_high = seven[3 * CY : 5 * CY] + jnp.pad(three[:CY], ((CY, 0), (0, 0)))
    v = jnp.where(lower, v_low, v_high)

    bb, bu, uu, uv = (sums[j : j + 1] for j in range(4))
    a0 = bb / bu
    rr1 = bb - 2.0 * a0 * bu + a0 * a0 * uu
    beta = rr1 / bb
    more = 1.0 + beta
    a1 = rr1 / (more * more * bu - 2.0 * more * a0 * uu + a0 * a0 * uv)
    solution = a0 * b + a1 * (more * b - a0 * u)
    residual = (b - a0 * u) - a1 * (more * u - a0 * v)

    def placed(value):
        turned = value.reshape(2, CY, 128)[:, :, : 3 * CX].reshape(2, CY, 3, CX)
        return turned.transpose(2, 0, 1, 3)

    return placed(solution), placed(residual)


def solution(mesh):
    in_specs = (P("gz", "gy", None), P("gz", "gy", None))
    out_specs = (P(None, "gz", None, None), P(None, "gz", None, None))
    return jax.shard_map(local, mesh=mesh, in_specs=in_specs, out_specs=out_specs, check_vma=False)
```

```python
import jax
import jax.numpy as jnp
import ml_dtypes
import numpy as np
from jax import lax
from jax.experimental import pallas as pl
from jax.experimental.pallas import tpu as pltpu
from jax.sharding import PartitionSpec as P

KNOT = 16
data_weight = 1.0 / 256.0
smooth_weight = 0.1

BF = jnp.bfloat16
F32 = jnp.float32
NZ, NY, NX = 32, 64, 512
ROWS = KNOT * NY
PLANES, CY, CX = 5, 8, 32
CTL = PLANES * CY
KPAD = 48
TILE = 16
WIDE = 128


def split(array):
    high = array.astype(ml_dtypes.bfloat16)
    low = (array - high.astype(np.float64)).astype(ml_dtypes.bfloat16)
    return high, low


def spline_weights():
    t = (np.arange(KNOT) + 0.5) / KNOT
    return np.stack(
        [
            (1 - t) ** 3 / 6,
            (3 * t**3 - 6 * t**2 + 4) / 6,
            (-3 * t**3 + 3 * t**2 + 3 * t + 1) / 6,
            t**3 / 6,
        ]
    )


def tables():
    weights = spline_weights()

    def along(blocks, first_block, points, first_point):
        out = np.zeros((blocks * KNOT, points))
        for block in range(blocks):
            for j in range(4):
                point = first_block + block + j - 1 - first_point
                if 0 <= point < points:
                    out[block * KNOT : (block + 1) * KNOT, point] = weights[j]
        return out

    along_z = along(NZ // KNOT, 0, PLANES, -1)
    halves = []
    for half in range(2):
        along_y = along(NY // KNOT, half * (NY // KNOT), CY, 0)
        halves.append(np.einsum("zp,yq->zypq", along_z, along_y).reshape(NZ * NY, CTL))
    high, low = split(np.stack(halves))
    widths = ((0, 0), (0, 0), (0, KPAD - CTL))
    high48, low48 = (np.pad(a, widths) for a in (high, low))
    out_table = np.concatenate([high48, low48, high48, low48], axis=2)
    backs = []
    for half in range(2):
        along_y = along(NY // KNOT, half * (NY // KNOT), CY, 0)
        backs.append(np.concatenate(split(np.kron(np.eye(PLANES), along_y).T), axis=0))
    back_table = np.stack(backs)
    along_x = along(NX // KNOT, 0, CX, 0)
    rows = np.zeros((128, 3 * NX))
    for c in range(3):
        rows[c * CX : (c + 1) * CX, c * NX : (c + 1) * NX] = along_x.T
    x_table = np.concatenate(split(rows), axis=0)
    return out_table, back_table, x_table


def halves_of(value):
    high = value.astype(BF)
    return high, (value - high.astype(F32)).astype(BF)


def block_terms(block, grad, weight_at, planes):
    weights = spline_weights()
    even = (weights[:2] + weights[:2, ::-1]) / 2
    odd = (weights[:2] - weights[:2, ::-1]) / 2

    def strip(y, carry):
        rows = pl.ds(pl.multiple_of(y * 8, 8), 8)
        for x in range(0, NX, WIDE):
            lanes = slice(x, x + WIDE)
            sums = [[[0.0, 0.0], [0.0, 0.0]] for _ in range(3)]
            for i in range(KNOT // 2):
                pair = []
                for z in (i, KNOT - 1 - i):
                    slopes = [grad[c, block * KNOT + z, rows, lanes] for c in range(3)]
                    weight, carry = weight_at(block * KNOT + z, y, lanes, slopes, carry)
                    pair.append([slope * weight for slope in slopes])
                for c in range(3):
                    both, apart = pair[0][c] + pair[1][c], pair[0][c] - pair[1][c]
                    for j in range(2):
                        sums[c][0][j] = sums[c][0][j] + float(even[j, i]) * both
                        sums[c][1][j] = sums[c][1][j] + float(odd[j, i]) * apart
            for c in range(3):
                (e0, e1), (o0, o1) = sums[c]
                at = slice(c * NX + x, c * NX + x + WIDE)
                for j, value in enumerate((e0 + o0, e1 + o1, e1 - o1, e0 - o0)):
                    if block == 0 or j == 3:
                        planes[block + j, rows, at] = value
                    else:
                        planes[block + j, rows, at] += value
        return carry

    return strip


def contracted(planes, back, x_table):
    high, low = halves_of(planes[...].reshape(PLANES * NY, 3 * NX))
    terms = jnp.dot(back, high, preferred_element_type=F32)
    rest = jnp.dot(back[:CTL], low, preferred_element_type=F32)
    high, low = halves_of(terms[:CTL] + (terms[CTL:] + rest))
    both = lax.dot_general(
        jnp.concatenate([high, low], 0),
        x_table[...],
        (((1,), (1,)), ((), ())),
        preferred_element_type=F32,
    )
    return both[:CTL, :128] + (both[:CTL, 128:] + both[CTL:, :128])


def first_kernel(half, moving, z_low, z_high, fixed, y_rows, back, xt, grad, out, planes):
    upper = half[0] == 0
    lane = lax.broadcasted_iota(jnp.int32, (TILE, NX), 1)

    def plane(z, near_planes):
        rows = y_rows[z]
        blank = jnp.zeros_like(rows)
        low_rows = jnp.where(upper, blank, rows)
        high_rows = jnp.where(upper, rows, blank)
        center = near_planes[2]
        for y in range(0, NY, TILE):
            here = slice(y, y + TILE)
            value = center[here]

            def at_z(k):
                return near_planes[2 + k][here]

            def at_y(k):
                first = y + k
                if first < 0:
                    return jnp.concatenate([low_rows[2 + first :], center[0 : TILE + first]], 0)
                if first + TILE > NY:
                    return jnp.concatenate([center[first:NY], high_rows[: first + TILE - NY]], 0)
                return center[first : first + TILE]

            def at_x(k):
                moved = pltpu.roll(value, (-k) % NX, 1)
                inside = lane < NX - k if k > 0 else lane >= -k
                return jnp.where(inside, moved, 0.0)

            for c, near in enumerate((at_z, at_y, at_x)):
                slope = 8.0 * (near(1) - near(-1)) - (near(2) - near(-2))
                grad[c, z, here] = slope

    def ref_of(z):
        if z < 0:
            return z_low.at[2 + z]
        if z >= NZ:
            return z_high.at[z - NZ]
        return moving.at[z]

    for z in (0, 1, NZ - 2, NZ - 1):
        plane(z, [ref_of(z + k) for k in range(-2, 3)])

    def body(z, carry):
        plane(z, [moving.at[z + k] for k in range(-2, 3)])
        return carry

    lax.fori_loop(2, NZ - 2, body, 0)

    def weight_at(z, y, lanes, slopes, carry):
        rows = pl.ds(pl.multiple_of(y * 8, 8), 8)
        return moving[z, rows, lanes] - fixed[z, rows, lanes], carry

    for block in range(NZ // KNOT):
        lax.fori_loop(0, NY // 8, block_terms(block, grad, weight_at, planes), 0)
    out[...] = contracted(planes, back[half[0]], xt) * (-data_weight / 12.0)


def hessian_kernel(half, ctl, base, grad, front, back, xt, out, sums, spread, field, planes):
    high, low = halves_of(ctl[...])
    first, second = xt[:128], xt[128:]
    value = jnp.dot(high, first, preferred_element_type=F32)
    value += jnp.dot(low, first, preferred_element_type=F32)
    value += jnp.dot(high, second, preferred_element_type=F32)
    value = jnp.concatenate([value, jnp.zeros((KPAD - CTL, 3 * NX), F32)], 0)
    high, low = halves_of(value)
    for j, part in enumerate((high, high, low, low)):
        spread[j * KPAD : (j + 1) * KPAD] = part
    square = jnp.zeros((8, WIDE), F32)

    for block in range(NZ // KNOT):
        at_rows = slice(block * ROWS, (block + 1) * ROWS)
        field[...] = jnp.dot(front[half[0], at_rows], spread[...], preferred_element_type=F32)

        def weight_at(z, y, lanes, slopes, carry):
            rows = pl.ds(pl.multiple_of(z % KNOT * NY + y * 8, 8), 8)
            weight = 0.0
            for c in range(3):
                at = slice(c * NX + lanes.start, c * NX + lanes.stop)
                weight = weight + slopes[c] * field[rows, at]
            return weight, carry + weight * weight

        strip = block_terms(block, grad, weight_at, planes)
        square = lax.fori_loop(0, NY // 8, strip, square)

    scale = data_weight / 144.0
    whole = ctl[...]
    owned = whole[CY : 3 * CY]
    sub = lax.broadcasted_iota(jnp.int32, (2 * CY, 128), 0) % CY
    lane = lax.broadcasted_iota(jnp.int32, (2 * CY, 128), 1) % CX
    near = whole[0 : 2 * CY] + whole[2 * CY : 4 * CY]
    near += jnp.where(sub > 0, pltpu.roll(owned, 1, 0), 0.0)
    near += jnp.where(sub < CY - 1, pltpu.roll(owned, 2 * CY - 1, 0), 0.0)
    near += jnp.where(lane > 0, pltpu.roll(owned, 1, 1), 0.0)
    near += jnp.where(lane < CX - 1, pltpu.roll(owned, 127, 1), 0.0)
    smooth = (0.5 * smooth_weight) * (6.0 * owned - near)
    out[...] = contracted(planes, back[half[0]], xt) * scale
    out[CY : 3 * CY] += smooth
    first = base[...]

    def total(value):
        return jnp.sum(jnp.sum(value, axis=0, keepdims=True), axis=1, keepdims=True)

    whole_square = total(square) * scale + total(smooth * owned)
    lines = [
        0.5 * total(first * first),
        0.5 * total(first * owned),
        0.5 * total(owned * owned),
        whole_square,
    ]
    which = lax.broadcasted_iota(jnp.int32, (8, 128), 0)
    tile = jnp.zeros((8, 128), F32)
    for j, line in enumerate(lines):
        tile = jnp.where(which == j, line, tile)
    sums[...] = tile


VMEM_SPEC = pl.BlockSpec(memory_space=pltpu.VMEM)
SMEM_SPEC = pl.BlockSpec(memory_space=pltpu.SMEM)
PARAMS = pltpu.CompilerParams(vmem_limit_bytes=24 * 1024 * 1024)


def first_pass(half, moving, z_low, z_high, fixed, y_rows, back_table, x_table):
    return pl.pallas_call(
        first_kernel,
        in_specs=[SMEM_SPEC] + [VMEM_SPEC] * 7,
        out_specs=[VMEM_SPEC] * 2,
        scratch_shapes=[pltpu.VMEM((PLANES, NY, 3 * NX), F32)],
        out_shape=[
            jax.ShapeDtypeStruct((3, NZ, NY, NX), F32),
            jax.ShapeDtypeStruct((CTL, 128), F32),
        ],
        compiler_params=PARAMS,
        name="first",
    )(half, moving, z_low, z_high, fixed, y_rows, back_table, x_table)


def hessian_pass(half, ctl, base, grad, front_table, back_table, x_table):
    return pl.pallas_call(
        hessian_kernel,
        in_specs=[SMEM_SPEC] + [VMEM_SPEC] * 6,
        out_specs=[VMEM_SPEC] * 2,
        scratch_shapes=[
            pltpu.VMEM((4 * KPAD, 3 * NX), BF),
            pltpu.VMEM((ROWS, 3 * NX), F32),
            pltpu.VMEM((PLANES, NY, 3 * NX), F32),
        ],
        out_shape=[
            jax.ShapeDtypeStruct((CTL, 128), F32),
            jax.ShapeDtypeStruct((8, 128), F32),
        ],
        compiler_params=PARAMS,
        name="hessian",
    )(half, ctl, base, grad, front_table, back_table, x_table)


def passed_along(value, axis, steps):
    count = lax.axis_size(axis)
    initial, last = (max(0, -steps), min(count, count - steps))
    return lax.ppermute(value, axis, [(source, source + steps) for source in range(initial, last)])


def swapped(value):
    return lax.ppermute(value, "gy", [(0, 1), (1, 0)])


def paired(value, mask):
    count = lax.axis_size("gz")
    return lax.ppermute(value, "gz", [(i, i ^ mask) for i in range(count)])


def outer_paired(value):
    count = lax.axis_size("gz")
    pairs = [(i, i + 1) for i in range(1, count - 1, 2)]
    return lax.ppermute(value, "gz", pairs + [(j, i) for i, j in pairs])


def pair_sum(lower, own, other):
    first, second = jnp.where(lower, own, other), jnp.where(lower, other, own)
    widths = ((0, 2 * CY), (0, 0)), ((2 * CY, 0), (0, 0))
    return jnp.pad(first, widths[0]) + jnp.pad(second, widths[1])


def outer_terms(lower, seven):
    return outer_paired(jnp.where(lower, seven[: 3 * CY], seven[4 * CY :]))


def all_planes(lower, part):
    part = part + swapped(part)
    seven = pair_sum(lower, part, paired(part, 1))
    three = outer_terms(lower, seven)
    one = paired(jnp.where(lower, three[2 * CY :], three[:CY]), 1)
    low = jnp.concatenate([three, jnp.zeros((CY, 128), F32), one], 0) + seven[: 5 * CY]
    high = jnp.concatenate([one, jnp.zeros((CY, 128), F32), three], 0) + seven[2 * CY :]
    row = lax.broadcasted_iota(jnp.int32, (CTL, 128), 0)
    at = lax.axis_index("gz") * (2 * CY) - CY + row
    inside = (at >= 0) & (at < lax.axis_size("gz") * (2 * CY))
    return jnp.where(inside, jnp.where(lower, low, high), 0.0)


def local(moving, fixed):
    half_id = lax.axis_index("gy").astype(jnp.int32)
    half = half_id.reshape(1)
    lower = lax.axis_index("gz") % 2 == 0
    front, back, xt = (jnp.asarray(a) for a in tables())

    z_low = passed_along(moving[-2:], "gz", 1)
    z_high = passed_along(moving[:2], "gz", -1)
    y_rows = swapped(jnp.where(half_id == 0, moving[:, -2:], moving[:, :2]))

    grad, part = first_pass(half, moving, z_low, z_high, fixed, y_rows, back, xt)
    b_planes = all_planes(lower, part)
    b = b_planes[CY : 3 * CY]
    part, _ = hessian_pass(half, b_planes, b, grad, front, back, xt)
    u_planes = all_planes(lower, part)
    u = u_planes[CY : 3 * CY]
    part, sums = hessian_pass(half, u_planes, b, grad, front, back, xt)
    both = jnp.concatenate([part, sums], 0)
    both = both + swapped(both)
    other = paired(both, 1)
    seven = pair_sum(lower, both[:CTL], other[:CTL])
    sums = both[CTL:] + other[CTL:]
    three = outer_terms(lower, seven)
    sums = sums + paired(sums, 2)
    sums, three = lax.optimization_barrier((sums, three))
    for mask in (6, 8, 16, 48):
        sums = sums + paired(sums, mask)
    v_low = seven[CY : 3 * CY] + three[CY:]
    v_high = seven[3 * CY : 5 * CY] + jnp.pad(three[:CY], ((CY, 0), (0, 0)))
    v = jnp.where(lower, v_low, v_high)

    bb, bu, uu, uv = (sums[j : j + 1] for j in range(4))
    a0 = bb / bu
    rr1 = bb - 2.0 * a0 * bu + a0 * a0 * uu
    beta = rr1 / bb
    more = 1.0 + beta
    a1 = rr1 / (more * more * bu - 2.0 * more * a0 * uu + a0 * a0 * uv)
    solution = a0 * b + a1 * (more * b - a0 * u)
    residual = (b - a0 * u) - a1 * (more * u - a0 * v)

    def placed(value):
        turned = value.reshape(2, CY, 128)[:, :, : 3 * CX].reshape(2, CY, 3, CX)
        return turned.transpose(2, 0, 1, 3)

    return placed(solution), placed(residual)


def solution(mesh):
    in_specs = (P("gz", "gy", None), P("gz", "gy", None))
    out_specs = (P(None, "gz", None, None), P(None, "gz", None, None))
    return jax.shard_map(local, mesh=mesh, in_specs=in_specs, out_specs=out_specs, check_vma=False)
```

```python
import jax
import jax.numpy as jnp
import ml_dtypes
import numpy as np
from jax import lax
from jax.experimental import pallas as pl
from jax.experimental.pallas import tpu as pltpu
from jax.sharding import PartitionSpec as P

KNOT = 16
data_weight = 1.0 / 256.0
smooth_weight = 0.1

BF = jnp.bfloat16
F32 = jnp.float32
NZ, NY, NX = 32, 64, 512
ROWS = KNOT * NY
PLANES, CY, CX = 5, 8, 32
CTL = PLANES * CY
KPAD = 48
TILE = 16
WIDE = 128
CHUNK = 8
STEPS = NZ // CHUNK
EDGES = (0, 1, NZ - 2, NZ - 1)


def split(array):
    high = array.astype(ml_dtypes.bfloat16)
    low = (array - high.astype(np.float64)).astype(ml_dtypes.bfloat16)
    return high, low


def spline_weights():
    t = (np.arange(KNOT) + 0.5) / KNOT
    return np.stack(
        [
            (1 - t) ** 3 / 6,
            (3 * t**3 - 6 * t**2 + 4) / 6,
            (-3 * t**3 + 3 * t**2 + 3 * t + 1) / 6,
            t**3 / 6,
        ]
    )


def tables():
    weights = spline_weights()

    def along(blocks, first_block, points, first_point):
        out = np.zeros((blocks * KNOT, points))
        for block in range(blocks):
            for j in range(4):
                point = first_block + block + j - 1 - first_point
                if 0 <= point < points:
                    out[block * KNOT : (block + 1) * KNOT, point] = weights[j]
        return out

    along_z = along(NZ // KNOT, 0, PLANES, -1)
    halves = []
    for half in range(2):
        along_y = along(NY // KNOT, half * (NY // KNOT), CY, 0)
        halves.append(np.einsum("zp,yq->zypq", along_z, along_y).reshape(NZ * NY, CTL))
    high, low = split(np.stack(halves))
    widths = ((0, 0), (0, 0), (0, KPAD - CTL))
    high48, low48 = (np.pad(a, widths) for a in (high, low))
    out_table = np.concatenate([high48, low48, high48, low48], axis=2)
    backs = []
    for half in range(2):
        along_y = along(NY // KNOT, half * (NY // KNOT), CY, 0)
        backs.append(np.concatenate(split(np.kron(np.eye(PLANES), along_y).T), axis=0))
    back_table = np.stack(backs)
    along_x = along(NX // KNOT, 0, CX, 0)
    rows = np.zeros((128, 3 * NX))
    for c in range(3):
        rows[c * CX : (c + 1) * CX, c * NX : (c + 1) * NX] = along_x.T
    x_table = np.concatenate(split(rows), axis=0)
    return out_table, back_table, x_table


def halves_of(value):
    high = value.astype(BF)
    return high, (value - high.astype(F32)).astype(BF)


def block_terms(block, grad, weight_at, planes):
    weights = spline_weights()
    even = (weights[:2] + weights[:2, ::-1]) / 2
    odd = (weights[:2] - weights[:2, ::-1]) / 2

    def strip(y, carry):
        rows = pl.ds(pl.multiple_of(y * 8, 8), 8)
        for x in range(0, NX, WIDE):
            lanes = slice(x, x + WIDE)
            sums = [[[0.0, 0.0], [0.0, 0.0]] for _ in range(3)]
            for i in range(KNOT // 2):
                pair = []
                for z in (i, KNOT - 1 - i):
                    slopes = [grad[c, block * KNOT + z, rows, lanes] for c in range(3)]
                    weight, carry = weight_at(block * KNOT + z, y, lanes, slopes, carry)
                    pair.append([slope * weight for slope in slopes])
                for c in range(3):
                    both, apart = pair[0][c] + pair[1][c], pair[0][c] - pair[1][c]
                    for j in range(2):
                        sums[c][0][j] = sums[c][0][j] + float(even[j, i]) * both
                        sums[c][1][j] = sums[c][1][j] + float(odd[j, i]) * apart
            for c in range(3):
                (e0, e1), (o0, o1) = sums[c]
                at = slice(c * NX + x, c * NX + x + WIDE)
                for j, value in enumerate((e0 + o0, e1 + o1, e1 - o1, e0 - o0)):
                    if block == 0 or j == 3:
                        planes[block + j, rows, at] = value
                    else:
                        planes[block + j, rows, at] += value
        return carry

    return strip


def contracted(planes, back, x_table):
    high, low = halves_of(planes[...].reshape(PLANES * NY, 3 * NX))
    terms = jnp.dot(back, high, preferred_element_type=F32)
    rest = jnp.dot(back[:CTL], low, preferred_element_type=F32)
    high, low = halves_of(terms[:CTL] + (terms[CTL:] + rest))
    both = lax.dot_general(
        jnp.concatenate([high, low], 0),
        x_table[...],
        (((1,), (1,)), ((), ())),
        preferred_element_type=F32,
    )
    return both[:CTL, :128] + (both[:CTL, 128:] + both[CTL:, :128])


def interior_kernel(
    half, moving_hbm, fixed_hbm, grad_hbm, planes, z_edges, y_edges, z_slopes, y_slopes, grad, moving, fixed, sems, out_sems
):
    def copies(j):
        part = pl.ds(j * CHUNK, CHUNK)
        return [
            pltpu.make_async_copy(source.at[part], target.at[part], sems.at[which, j])
            for which, (source, target) in enumerate(((moving_hbm, moving), (fixed_hbm, fixed)))
        ]

    for j in range(STEPS):
        copies(j)[0].start()
    for j in range(STEPS):
        copies(j)[1].start()
    lane = lax.broadcasted_iota(jnp.int32, (TILE, NX), 1)
    two = jnp.zeros((2, NX), F32)

    def plane(z, shifts):
        center = moving.at[z]
        for y in range(0, NY, TILE):
            here = slice(y, y + TILE)
            value = center[here]

            def at_z(k):
                return moving[z + k, here] if k in shifts else 0.0

            def at_y(k):
                first = y + k
                if first < 0:
                    return jnp.concatenate([two[: -first], center[0 : TILE + first]], 0)
                if first + TILE > NY:
                    return jnp.concatenate([center[first:NY], two[: first + TILE - NY]], 0)
                return center[first : first + TILE]

            def at_x(k):
                moved = pltpu.roll(value, (-k) % NX, 1)
                inside = lane < NX - k if k > 0 else lane >= -k
                return jnp.where(inside, moved, 0.0)

            for c, near in enumerate((at_z, at_y, at_x)):
                grad[c, z, here] = 8.0 * (near(1) - near(-1)) - (near(2) - near(-2))

    every = (-2, -1, 1, 2)

    def body(z, carry):
        plane(z, every)
        return carry

    bounds = [0] + [(j + 1) * CHUNK - 2 for j in range(STEPS - 1)] + [NZ]
    written = [
        pltpu.make_async_copy(grad.at[:, first:last], grad_hbm.at[:, first:last], out_sems.at[j])
        for j, (first, last) in enumerate(zip(bounds, bounds[1:]))
    ]
    for j in range(STEPS):
        copies(j)[0].wait()
        if j == 0:
            plane(0, (1, 2))
            plane(1, (-1, 1, 2))
        lax.fori_loop(max(2, j * CHUNK - 2), (j + 1) * CHUNK - 2, body, 0)
        if j == STEPS - 1:
            plane(NZ - 2, (-2, -1, 1))
            plane(NZ - 1, (-2, -1))
        written[j].start()
    for j in range(STEPS):
        copies(j)[1].wait()

    def weight_at(z, y, lanes, slopes, carry):
        rows = pl.ds(pl.multiple_of(y * 8, 8), 8)
        return moving[z, rows, lanes] - fixed[z, rows, lanes], carry

    for block in range(NZ // KNOT):
        lax.fori_loop(0, NY // 8, block_terms(block, grad, weight_at, planes), 0)
    for e, z in enumerate(EDGES):
        z_edges[e] = moving[z] - fixed[z]
        z_slopes[e] = grad[0, z]
    rows = pl.ds(pl.multiple_of((1 - half[0]) * (NY - 8), 8), 8)
    y_edges[...] = moving[:, rows, :] - fixed[:, rows, :]
    y_slopes[...] = grad[1, :, rows, :]
    for copy in written:
        copy.wait()


def edge_kernel(
    half,
    z_low,
    z_high,
    y_rows,
    z_edges,
    y_edges,
    z_slopes,
    y_slopes,
    back,
    xt,
    grad_in,
    planes_in,
    grad_hbm,
    out,
    planes,
    z_new,
    y_new,
    sems,
):
    del grad_in
    planes[...] = planes_in[...]
    weights = spline_weights()

    def strip(y, carry):
        rows = pl.ds(pl.multiple_of(y * 8, 8), 8)
        near, far = z_low[1, rows], z_low[0, rows]
        above, beyond = z_high[0, rows], z_high[1, rows]
        slopes = (far - 8.0 * near, near, -above, 8.0 * above - beyond)
        for e, z in enumerate(EDGES):
            z_new[e, rows] = z_slopes[e, rows] + slopes[e]
            term = slopes[e] * z_edges[e, rows]
            for j in range(4):
                at = z // KNOT + j
                planes[at, rows, 0:NX] += float(weights[j, z % KNOT]) * term
        return carry

    lax.fori_loop(0, NY // 8, strip, 0)
    copies = [
        pltpu.make_async_copy(z_new.at[pl.ds(e, 2)], grad_hbm.at[0, pl.ds(EDGES[e], 2)], sems.at[e // 2])
        for e in (0, 2)
    ]
    for copy in copies:
        copy.start()

    upper = half[0] == 0
    rows = pl.ds(pl.multiple_of((1 - half[0]) * (NY - 8), 8), 8)
    sub = lax.broadcasted_iota(jnp.int32, (8, NX), 0)

    def coefficient(when_upper, otherwise):
        def column(entries):
            value = jnp.zeros((8, NX), F32)
            for row, entry in entries.items():
                value = jnp.where(sub == row, entry, value)
            return value

        return jnp.where(upper, column(when_upper), column(otherwise))

    on_first = coefficient({6: -1.0, 7: 8.0}, {0: 1.0})
    on_second = coefficient({7: -1.0}, {0: -8.0, 1: 1.0})
    for block in range(NZ // KNOT):
        sums = [0.0] * 4
        for i in range(KNOT):
            z = block * KNOT + i
            slope = on_first * y_rows[z, 0:1] + on_second * y_rows[z, 1:2]
            y_new[z] = y_slopes[z] + slope
            term = slope * y_edges[z]
            sums = [total + float(weights[j, i]) * term for j, total in enumerate(sums)]
        for j, total in enumerate(sums):
            planes[block + j, rows, NX : 2 * NX] += total
    copies.append(pltpu.make_async_copy(y_new, grad_hbm.at[1, :, rows], sems.at[2]))
    copies[-1].start()
    out[...] = contracted(planes, back[half[0]], xt) * (-data_weight / 12.0)
    for copy in copies:
        copy.wait()


def hessian_kernel(
    half, ctl, base, grad_hbm, front, back, xt, out, sums, grad, spread, field, planes, sems
):
    copies = []
    for block in range(NZ // KNOT):
        part = pl.ds(block * KNOT, KNOT)
        copies.append(
            pltpu.make_async_copy(grad_hbm.at[:, part], grad.at[:, part], sems.at[block])
        )
        copies[-1].start()
    high, low = halves_of(ctl[...])
    first, second = xt[:128], xt[128:]
    value = jnp.dot(high, first, preferred_element_type=F32)
    value += jnp.dot(low, first, preferred_element_type=F32)
    value += jnp.dot(high, second, preferred_element_type=F32)
    value = jnp.concatenate([value, jnp.zeros((KPAD - CTL, 3 * NX), F32)], 0)
    high, low = halves_of(value)
    for j, part in enumerate((high, high, low, low)):
        spread[j * KPAD : (j + 1) * KPAD] = part
    square = jnp.zeros((8, WIDE), F32)

    for block in range(NZ // KNOT):
        at_rows = slice(block * ROWS, (block + 1) * ROWS)
        field[...] = jnp.dot(front[half[0], at_rows], spread[...], preferred_element_type=F32)

        def weight_at(z, y, lanes, slopes, carry):
            rows = pl.ds(pl.multiple_of(z % KNOT * NY + y * 8, 8), 8)
            weight = 0.0
            for c in range(3):
                at = slice(c * NX + lanes.start, c * NX + lanes.stop)
                weight = weight + slopes[c] * field[rows, at]
            return weight, carry + weight * weight

        copies[block].wait()
        strip = block_terms(block, grad, weight_at, planes)
        square = lax.fori_loop(0, NY // 8, strip, square)

    scale = data_weight / 144.0
    whole = ctl[...]
    owned = whole[CY : 3 * CY]
    sub = lax.broadcasted_iota(jnp.int32, (2 * CY, 128), 0) % CY
    lane = lax.broadcasted_iota(jnp.int32, (2 * CY, 128), 1) % CX
    near = whole[0 : 2 * CY] + whole[2 * CY : 4 * CY]
    near += jnp.where(sub > 0, pltpu.roll(owned, 1, 0), 0.0)
    near += jnp.where(sub < CY - 1, pltpu.roll(owned, 2 * CY - 1, 0), 0.0)
    near += jnp.where(lane > 0, pltpu.roll(owned, 1, 1), 0.0)
    near += jnp.where(lane < CX - 1, pltpu.roll(owned, 127, 1), 0.0)
    smooth = (0.5 * smooth_weight) * (6.0 * owned - near)
    out[...] = contracted(planes, back[half[0]], xt) * scale
    out[CY : 3 * CY] += smooth
    first = base[...]

    def total(value):
        return jnp.sum(jnp.sum(value, axis=0, keepdims=True), axis=1, keepdims=True)

    whole_square = total(square) * scale + total(smooth * owned)
    lines = [
        0.5 * total(first * first),
        0.5 * total(first * owned),
        0.5 * total(owned * owned),
        whole_square,
    ]
    which = lax.broadcasted_iota(jnp.int32, (8, 128), 0)
    tile = jnp.zeros((8, 128), F32)
    for j, line in enumerate(lines):
        tile = jnp.where(which == j, line, tile)
    sums[...] = tile


VMEM_SPEC = pl.BlockSpec(memory_space=pltpu.VMEM)
SMEM_SPEC = pl.BlockSpec(memory_space=pltpu.SMEM)
PARAMS = pltpu.CompilerParams(vmem_limit_bytes=52 * 1024 * 1024)
EDGE_PARAMS = pltpu.CompilerParams(vmem_limit_bytes=50 * 1024 * 1024)
INTERIOR_MIB = 48


GRAD_SHAPE = jax.ShapeDtypeStruct((3, NZ, NY, NX), F32)
PLANES_SHAPE = jax.ShapeDtypeStruct((PLANES, NY, 3 * NX), F32)
CTL_SHAPE = jax.ShapeDtypeStruct((CTL, 128), F32)


Z_SHAPE = (len(EDGES), NY, NX)
Y_SHAPE = (NZ, 8, NX)
HBM_SPEC = pl.BlockSpec(memory_space=pltpu.HBM)


def interior_pass(half, moving, fixed):
    return pl.pallas_call(
        interior_kernel,
        in_specs=[SMEM_SPEC] + [HBM_SPEC] * 2,
        out_specs=[HBM_SPEC] + [VMEM_SPEC] * 5,
        scratch_shapes=[
            pltpu.VMEM((3, NZ, NY, NX), F32),
            pltpu.VMEM((NZ, NY, NX), F32),
            pltpu.VMEM((NZ, NY, NX), F32),
            pltpu.SemaphoreType.DMA((2, STEPS)),
            pltpu.SemaphoreType.DMA((STEPS,)),
        ],
        out_shape=[GRAD_SHAPE, PLANES_SHAPE]
        + [jax.ShapeDtypeStruct(shape, F32) for shape in (Z_SHAPE, Y_SHAPE) * 2],
        compiler_params=pltpu.CompilerParams(vmem_limit_bytes=INTERIOR_MIB * 1024 * 1024),
        cost_estimate=pl.CostEstimate(flops=100_000_000, bytes_accessed=40_000_000, transcendentals=0),
        name="interior",
    )(half, moving, fixed)


def edge_pass(half, z_low, z_high, y_rows, edges, back_table, x_table, grad, planes):
    grad, part = pl.pallas_call(
        edge_kernel,
        in_specs=[SMEM_SPEC] + [VMEM_SPEC] * 9 + [HBM_SPEC, VMEM_SPEC],
        out_specs=[HBM_SPEC, VMEM_SPEC],
        out_shape=[GRAD_SHAPE, CTL_SHAPE],
        scratch_shapes=[
            pltpu.VMEM((PLANES, NY, 3 * NX), F32),
            pltpu.VMEM(Z_SHAPE, F32),
            pltpu.VMEM(Y_SHAPE, F32),
            pltpu.SemaphoreType.DMA((3,)),
        ],
        input_output_aliases={10: 0},
        compiler_params=EDGE_PARAMS,
        name="edge",
    )(half, z_low, z_high, y_rows, *edges, back_table, x_table, grad, planes)
    return grad, part


def hessian_pass(half, ctl, base, grad, front_table, back_table, x_table):
    return pl.pallas_call(
        hessian_kernel,
        in_specs=[SMEM_SPEC] + [VMEM_SPEC] * 2 + [HBM_SPEC] + [VMEM_SPEC] * 3,
        out_specs=[VMEM_SPEC] * 2,
        scratch_shapes=[
            pltpu.VMEM((3, NZ, NY, NX), F32),
            pltpu.VMEM((4 * KPAD, 3 * NX), BF),
            pltpu.VMEM((ROWS, 3 * NX), F32),
            pltpu.VMEM((PLANES, NY, 3 * NX), F32),
            pltpu.SemaphoreType.DMA((NZ // KNOT,)),
        ],
        out_shape=[
            jax.ShapeDtypeStruct((CTL, 128), F32),
            jax.ShapeDtypeStruct((8, 128), F32),
        ],
        compiler_params=PARAMS,
        name="hessian",
    )(half, ctl, base, grad, front_table, back_table, x_table)


def passed_along(value, axis, steps):
    count = lax.axis_size(axis)
    initial, last = (max(0, -steps), min(count, count - steps))
    return lax.ppermute(value, axis, [(source, source + steps) for source in range(initial, last)])


def swapped(value):
    return lax.ppermute(value, "gy", [(0, 1), (1, 0)])


def paired(value, mask):
    count = lax.axis_size("gz")
    return lax.ppermute(value, "gz", [(i, i ^ mask) for i in range(count)])


def outer_paired(value):
    count = lax.axis_size("gz")
    pairs = [(i, i + 1) for i in range(1, count - 1, 2)]
    return lax.ppermute(value, "gz", pairs + [(j, i) for i, j in pairs])


def pair_sum(lower, own, other):
    first, second = jnp.where(lower, own, other), jnp.where(lower, other, own)
    widths = ((0, 2 * CY), (0, 0)), ((2 * CY, 0), (0, 0))
    return jnp.pad(first, widths[0]) + jnp.pad(second, widths[1])


def outer_terms(lower, seven):
    return outer_paired(jnp.where(lower, seven[: 3 * CY], seven[4 * CY :]))


def all_planes(lower, part):
    part = part + swapped(part)
    seven = pair_sum(lower, part, paired(part, 1))
    three = outer_terms(lower, seven)
    one = paired(jnp.where(lower, three[2 * CY :], three[:CY]), 1)
    low = jnp.concatenate([three, jnp.zeros((CY, 128), F32), one], 0) + seven[: 5 * CY]
    high = jnp.concatenate([one, jnp.zeros((CY, 128), F32), three], 0) + seven[2 * CY :]
    row = lax.broadcasted_iota(jnp.int32, (CTL, 128), 0)
    at = lax.axis_index("gz") * (2 * CY) - CY + row
    inside = (at >= 0) & (at < lax.axis_size("gz") * (2 * CY))
    return jnp.where(inside, jnp.where(lower, low, high), 0.0)


def local(moving, fixed):
    half_id = lax.axis_index("gy").astype(jnp.int32)
    half = half_id.reshape(1)
    lower = lax.axis_index("gz") % 2 == 0
    front, back, xt = (jnp.asarray(a) for a in tables())

    z_low = passed_along(moving[-2:], "gz", 1)
    z_high = passed_along(moving[:2], "gz", -1)
    y_rows = swapped(jnp.where(half_id == 0, moving[:, -2:], moving[:, :2]))

    grad, planes, *edges = interior_pass(half, moving, fixed)
    grad, part = edge_pass(half, z_low, z_high, y_rows, edges, back, xt, grad, planes)
    b_planes = all_planes(lower, part)
    b = b_planes[CY : 3 * CY]
    part, _ = hessian_pass(half, b_planes, b, grad, front, back, xt)
    u_planes = all_planes(lower, part)
    u = u_planes[CY : 3 * CY]
    part, sums = hessian_pass(half, u_planes, b, grad, front, back, xt)
    both = jnp.concatenate([part, sums], 0)
    both = both + swapped(both)
    other = paired(both, 1)
    seven = pair_sum(lower, both[:CTL], other[:CTL])
    sums = both[CTL:] + other[CTL:]
    three = outer_terms(lower, seven)
    sums = sums + paired(sums, 2)
    sums, three = lax.optimization_barrier((sums, three))
    for mask in (6, 8, 16, 48):
        sums = sums + paired(sums, mask)
    v_low = seven[CY : 3 * CY] + three[CY:]
    v_high = seven[3 * CY : 5 * CY] + jnp.pad(three[:CY], ((CY, 0), (0, 0)))
    v = jnp.where(lower, v_low, v_high)

    bb, bu, uu, uv = (sums[j : j + 1] for j in range(4))
    a0 = bb / bu
    rr1 = bb - 2.0 * a0 * bu + a0 * a0 * uu
    beta = rr1 / bb
    more = 1.0 + beta
    a1 = rr1 / (more * more * bu - 2.0 * more * a0 * uu + a0 * a0 * uv)
    solution = a0 * b + a1 * (more * b - a0 * u)
    residual = (b - a0 * u) - a1 * (more * u - a0 * v)

    def placed(value):
        turned = value.reshape(2, CY, 128)[:, :, : 3 * CX].reshape(2, CY, 3, CX)
        return turned.transpose(2, 0, 1, 3)

    return placed(solution), placed(residual)


def solution(mesh):
    in_specs = (P("gz", "gy", None), P("gz", "gy", None))
    out_specs = (P(None, "gz", None, None), P(None, "gz", None, None))
    return jax.shard_map(local, mesh=mesh, in_specs=in_specs, out_specs=out_specs, check_vma=False)
```

```python
import jax
import jax.numpy as jnp
import ml_dtypes
import numpy as np
from jax import lax
from jax.experimental import pallas as pl
from jax.experimental.pallas import tpu as pltpu
from jax.sharding import PartitionSpec as P

KNOT = 16
data_weight = 1.0 / 256.0
smooth_weight = 0.1

BF = jnp.bfloat16
F32 = jnp.float32
NZ, NY, NX = 32, 64, 512
ROWS = KNOT * NY
PLANES, CY, CX = 5, 8, 32
CTL = PLANES * CY
KPAD = 48
TILE = 16
WIDE = 128
CHUNK = 8
STEPS = NZ // CHUNK
EDGES = (0, 1, NZ - 2, NZ - 1)


def split(array):
    high = array.astype(ml_dtypes.bfloat16)
    low = (array - high.astype(np.float64)).astype(ml_dtypes.bfloat16)
    return high, low


def spline_weights():
    t = (np.arange(KNOT) + 0.5) / KNOT
    return np.stack(
        [
            (1 - t) ** 3 / 6,
            (3 * t**3 - 6 * t**2 + 4) / 6,
            (-3 * t**3 + 3 * t**2 + 3 * t + 1) / 6,
            t**3 / 6,
        ]
    )


def tables():
    weights = spline_weights()

    def along(blocks, first_block, points, first_point):
        out = np.zeros((blocks * KNOT, points))
        for block in range(blocks):
            for j in range(4):
                point = first_block + block + j - 1 - first_point
                if 0 <= point < points:
                    out[block * KNOT : (block + 1) * KNOT, point] = weights[j]
        return out

    along_z = along(NZ // KNOT, 0, PLANES, -1)
    halves = []
    for half in range(2):
        along_y = along(NY // KNOT, half * (NY // KNOT), CY, 0)
        halves.append(np.einsum("zp,yq->zypq", along_z, along_y).reshape(NZ * NY, CTL))
    high, low = split(np.stack(halves))
    widths = ((0, 0), (0, 0), (0, KPAD - CTL))
    high48, low48 = (np.pad(a, widths) for a in (high, low))
    out_table = np.concatenate([high48, low48, high48, low48], axis=2)
    backs = []
    for half in range(2):
        along_y = along(NY // KNOT, half * (NY // KNOT), CY, 0)
        backs.append(np.concatenate(split(np.kron(np.eye(PLANES), along_y).T), axis=0))
    back_table = np.stack(backs)
    along_x = along(NX // KNOT, 0, CX, 0)
    rows = np.zeros((128, 3 * NX))
    for c in range(3):
        rows[c * CX : (c + 1) * CX, c * NX : (c + 1) * NX] = along_x.T
    x_table = np.concatenate(split(rows), axis=0)
    return out_table, back_table, x_table


def halves_of(value):
    high = value.astype(BF)
    return high, (value - high.astype(F32)).astype(BF)


def block_terms(block, grad, weight_at, planes):
    weights = spline_weights()
    even = (weights[:2] + weights[:2, ::-1]) / 2
    odd = (weights[:2] - weights[:2, ::-1]) / 2

    def strip(y, carry):
        rows = pl.ds(pl.multiple_of(y * 8, 8), 8)
        for x in range(0, NX, WIDE):
            lanes = slice(x, x + WIDE)
            sums = [[[0.0, 0.0], [0.0, 0.0]] for _ in range(3)]
            for i in range(KNOT // 2):
                pair = []
                for z in (i, KNOT - 1 - i):
                    slopes = [grad[c, block * KNOT + z, rows, lanes] for c in range(3)]
                    weight, carry = weight_at(block * KNOT + z, y, lanes, slopes, carry)
                    pair.append([slope * weight for slope in slopes])
                for c in range(3):
                    both, apart = pair[0][c] + pair[1][c], pair[0][c] - pair[1][c]
                    for j in range(2):
                        sums[c][0][j] = sums[c][0][j] + float(even[j, i]) * both
                        sums[c][1][j] = sums[c][1][j] + float(odd[j, i]) * apart
            for c in range(3):
                (e0, e1), (o0, o1) = sums[c]
                at = slice(c * NX + x, c * NX + x + WIDE)
                for j, value in enumerate((e0 + o0, e1 + o1, e1 - o1, e0 - o0)):
                    if block == 0 or j == 3:
                        planes[block + j, rows, at] = value
                    else:
                        planes[block + j, rows, at] += value
        return carry

    return strip


def contracted(planes, back, x_table):
    high, low = halves_of(planes[...].reshape(PLANES * NY, 3 * NX))
    terms = jnp.dot(back, high, preferred_element_type=F32)
    rest = jnp.dot(back[:CTL], low, preferred_element_type=F32)
    high, low = halves_of(terms[:CTL] + (terms[CTL:] + rest))
    both = lax.dot_general(
        jnp.concatenate([high, low], 0),
        x_table[...],
        (((1,), (1,)), ((), ())),
        preferred_element_type=F32,
    )
    return both[:CTL, :128] + (both[:CTL, 128:] + both[CTL:, :128])


def interior_kernel(
    half, moving_hbm, fixed_hbm, grad_hbm, planes, z_edges, y_edges, z_slopes, y_slopes, grad, moving, fixed, sems, out_sems
):
    def copies(j):
        part = pl.ds(j * CHUNK, CHUNK)
        return [
            pltpu.make_async_copy(source.at[part], target.at[part], sems.at[which, j])
            for which, (source, target) in enumerate(((moving_hbm, moving), (fixed_hbm, fixed)))
        ]

    for j in range(STEPS):
        copies(j)[0].start()
    for j in range(STEPS):
        copies(j)[1].start()
    lane = lax.broadcasted_iota(jnp.int32, (TILE, NX), 1)
    two = jnp.zeros((2, NX), F32)

    def plane(z, shifts):
        center = moving.at[z]
        for y in range(0, NY, TILE):
            here = slice(y, y + TILE)
            value = center[here]

            def at_z(k):
                return moving[z + k, here] if k in shifts else 0.0

            def at_y(k):
                first = y + k
                if first < 0:
                    return jnp.concatenate([two[: -first], center[0 : TILE + first]], 0)
                if first + TILE > NY:
                    return jnp.concatenate([center[first:NY], two[: first + TILE - NY]], 0)
                return center[first : first + TILE]

            def at_x(k):
                moved = pltpu.roll(value, (-k) % NX, 1)
                inside = lane < NX - k if k > 0 else lane >= -k
                return jnp.where(inside, moved, 0.0)

            for c, near in enumerate((at_z, at_y, at_x)):
                grad[c, z, here] = 8.0 * (near(1) - near(-1)) - (near(2) - near(-2))

    every = (-2, -1, 1, 2)

    def body(z, carry):
        plane(z, every)
        return carry

    bounds = [0] + [(j + 1) * CHUNK - 2 for j in range(STEPS - 1)] + [NZ]
    written = [
        pltpu.make_async_copy(grad.at[:, first:last], grad_hbm.at[:, first:last], out_sems.at[j])
        for j, (first, last) in enumerate(zip(bounds, bounds[1:]))
    ]
    for j in range(STEPS):
        copies(j)[0].wait()
        if j == 0:
            plane(0, (1, 2))
            plane(1, (-1, 1, 2))
        lax.fori_loop(max(2, j * CHUNK - 2), (j + 1) * CHUNK - 2, body, 0)
        if j == STEPS - 1:
            plane(NZ - 2, (-2, -1, 1))
            plane(NZ - 1, (-2, -1))
        written[j].start()
    for j in range(STEPS):
        copies(j)[1].wait()

    def weight_at(z, y, lanes, slopes, carry):
        rows = pl.ds(pl.multiple_of(y * 8, 8), 8)
        return moving[z, rows, lanes] - fixed[z, rows, lanes], carry

    for block in range(NZ // KNOT):
        lax.fori_loop(0, NY // 8, block_terms(block, grad, weight_at, planes), 0)
    for e, z in enumerate(EDGES):
        z_edges[e] = moving[z] - fixed[z]
        z_slopes[e] = grad[0, z]
    rows = pl.ds(pl.multiple_of((1 - half[0]) * (NY - 8), 8), 8)
    y_edges[...] = moving[:, rows, :] - fixed[:, rows, :]
    y_slopes[...] = grad[1, :, rows, :]
    for copy in written:
        copy.wait()


def edge_kernel(
    half,
    z_low,
    z_high,
    y_rows,
    z_edges,
    y_edges,
    z_slopes,
    y_slopes,
    back,
    xt,
    grad_in,
    planes_in,
    grad_hbm,
    out,
    planes,
    z_new,
    y_new,
    sems,
):
    del grad_in
    planes[...] = planes_in[...]
    weights = spline_weights()

    def strip(y, carry):
        rows = pl.ds(pl.multiple_of(y * 8, 8), 8)
        near, far = z_low[1, rows], z_low[0, rows]
        above, beyond = z_high[0, rows], z_high[1, rows]
        slopes = (far - 8.0 * near, near, -above, 8.0 * above - beyond)
        for e, z in enumerate(EDGES):
            z_new[e, rows] = z_slopes[e, rows] + slopes[e]
            term = slopes[e] * z_edges[e, rows]
            for j in range(4):
                at = z // KNOT + j
                planes[at, rows, 0:NX] += float(weights[j, z % KNOT]) * term
        return carry

    lax.fori_loop(0, NY // 8, strip, 0)
    copies = [
        pltpu.make_async_copy(z_new.at[pl.ds(e, 2)], grad_hbm.at[0, pl.ds(EDGES[e], 2)], sems.at[e // 2])
        for e in (0, 2)
    ]
    for copy in copies:
        copy.start()

    upper = half[0] == 0
    rows = pl.ds(pl.multiple_of((1 - half[0]) * (NY - 8), 8), 8)
    sub = lax.broadcasted_iota(jnp.int32, (8, NX), 0)

    def coefficient(when_upper, otherwise):
        def column(entries):
            value = jnp.zeros((8, NX), F32)
            for row, entry in entries.items():
                value = jnp.where(sub == row, entry, value)
            return value

        return jnp.where(upper, column(when_upper), column(otherwise))

    on_first = coefficient({6: -1.0, 7: 8.0}, {0: 1.0})
    on_second = coefficient({7: -1.0}, {0: -8.0, 1: 1.0})
    for block in range(NZ // KNOT):
        sums = [0.0] * 4
        for i in range(KNOT):
            z = block * KNOT + i
            slope = on_first * y_rows[z, 0:1] + on_second * y_rows[z, 1:2]
            y_new[z] = y_slopes[z] + slope
            term = slope * y_edges[z]
            sums = [total + float(weights[j, i]) * term for j, total in enumerate(sums)]
        for j, total in enumerate(sums):
            planes[block + j, rows, NX : 2 * NX] += total
    copies.append(pltpu.make_async_copy(y_new, grad_hbm.at[1, :, rows], sems.at[2]))
    copies[-1].start()
    out[...] = contracted(planes, back[half[0]], xt) * (-data_weight / 12.0)
    for copy in copies:
        copy.wait()


def hessian_kernel(
    half, ctl, base, grad_hbm, front, back, xt, out, sums, grad, spread, field, planes, sems
):
    copies = []
    for block in range(NZ // KNOT):
        for y in range(2):
            part = (slice(None), pl.ds(block * KNOT, KNOT), pl.ds(y * NY // 2, NY // 2))
            copies.append(
                pltpu.make_async_copy(grad_hbm.at[part], grad.at[part], sems.at[block, y])
            )
    for copy in copies:
        copy.start()
    high, low = halves_of(ctl[...])
    first, second = xt[:128], xt[128:]
    value = jnp.dot(high, first, preferred_element_type=F32)
    value += jnp.dot(low, first, preferred_element_type=F32)
    value += jnp.dot(high, second, preferred_element_type=F32)
    value = jnp.concatenate([value, jnp.zeros((KPAD - CTL, 3 * NX), F32)], 0)
    high, low = halves_of(value)
    for j, part in enumerate((high, high, low, low)):
        spread[j * KPAD : (j + 1) * KPAD] = part
    square = jnp.zeros((8, WIDE), F32)

    for block in range(NZ // KNOT):
        at_rows = slice(block * ROWS, (block + 1) * ROWS)
        field[...] = jnp.dot(front[half[0], at_rows], spread[...], preferred_element_type=F32)

        def weight_at(z, y, lanes, slopes, carry):
            rows = pl.ds(pl.multiple_of(z % KNOT * NY + y * 8, 8), 8)
            weight = 0.0
            for c in range(3):
                at = slice(c * NX + lanes.start, c * NX + lanes.stop)
                weight = weight + slopes[c] * field[rows, at]
            return weight, carry + weight * weight

        strip = block_terms(block, grad, weight_at, planes)
        for y in range(2):
            copies[2 * block + y].wait()
            square = lax.fori_loop(y * NY // 16, (y + 1) * NY // 16, strip, square)

    scale = data_weight / 144.0
    whole = ctl[...]
    owned = whole[CY : 3 * CY]
    sub = lax.broadcasted_iota(jnp.int32, (2 * CY, 128), 0) % CY
    lane = lax.broadcasted_iota(jnp.int32, (2 * CY, 128), 1) % CX
    near = whole[0 : 2 * CY] + whole[2 * CY : 4 * CY]
    near += jnp.where(sub > 0, pltpu.roll(owned, 1, 0), 0.0)
    near += jnp.where(sub < CY - 1, pltpu.roll(owned, 2 * CY - 1, 0), 0.0)
    near += jnp.where(lane > 0, pltpu.roll(owned, 1, 1), 0.0)
    near += jnp.where(lane < CX - 1, pltpu.roll(owned, 127, 1), 0.0)
    smooth = (0.5 * smooth_weight) * (6.0 * owned - near)
    out[...] = contracted(planes, back[half[0]], xt) * scale
    out[CY : 3 * CY] += smooth
    first = base[...]

    def total(value):
        return jnp.sum(jnp.sum(value, axis=0, keepdims=True), axis=1, keepdims=True)

    whole_square = total(square) * scale + total(smooth * owned)
    lines = [
        0.5 * total(first * first),
        0.5 * total(first * owned),
        0.5 * total(owned * owned),
        whole_square,
    ]
    which = lax.broadcasted_iota(jnp.int32, (8, 128), 0)
    tile = jnp.zeros((8, 128), F32)
    for j, line in enumerate(lines):
        tile = jnp.where(which == j, line, tile)
    sums[...] = tile


VMEM_SPEC = pl.BlockSpec(memory_space=pltpu.VMEM)
SMEM_SPEC = pl.BlockSpec(memory_space=pltpu.SMEM)
PARAMS = pltpu.CompilerParams(vmem_limit_bytes=48 * 1024 * 1024)
EDGE_PARAMS = pltpu.CompilerParams(vmem_limit_bytes=47 * 1024 * 1024)
INTERIOR_MIB = 48


GRAD_SHAPE = jax.ShapeDtypeStruct((3, NZ, NY, NX), F32)
PLANES_SHAPE = jax.ShapeDtypeStruct((PLANES, NY, 3 * NX), F32)
CTL_SHAPE = jax.ShapeDtypeStruct((CTL, 128), F32)


Z_SHAPE = (len(EDGES), NY, NX)
Y_SHAPE = (NZ, 8, NX)
HBM_SPEC = pl.BlockSpec(memory_space=pltpu.HBM)


def interior_pass(half, moving, fixed):
    return pl.pallas_call(
        interior_kernel,
        in_specs=[SMEM_SPEC] + [HBM_SPEC] * 2,
        out_specs=[HBM_SPEC] + [VMEM_SPEC] * 5,
        scratch_shapes=[
            pltpu.VMEM((3, NZ, NY, NX), F32),
            pltpu.VMEM((NZ, NY, NX), F32),
            pltpu.VMEM((NZ, NY, NX), F32),
            pltpu.SemaphoreType.DMA((2, STEPS)),
            pltpu.SemaphoreType.DMA((STEPS,)),
        ],
        out_shape=[GRAD_SHAPE, PLANES_SHAPE]
        + [jax.ShapeDtypeStruct(shape, F32) for shape in (Z_SHAPE, Y_SHAPE) * 2],
        compiler_params=pltpu.CompilerParams(vmem_limit_bytes=INTERIOR_MIB * 1024 * 1024),
        cost_estimate=pl.CostEstimate(flops=100_000_000, bytes_accessed=40_000_000, transcendentals=0),
        name="interior",
    )(half, moving, fixed)


def edge_pass(half, z_low, z_high, y_rows, edges, back_table, x_table, grad, planes):
    grad, part = pl.pallas_call(
        edge_kernel,
        in_specs=[SMEM_SPEC] + [VMEM_SPEC] * 9 + [HBM_SPEC, VMEM_SPEC],
        out_specs=[HBM_SPEC, VMEM_SPEC],
        out_shape=[GRAD_SHAPE, CTL_SHAPE],
        scratch_shapes=[
            pltpu.VMEM((PLANES, NY, 3 * NX), F32),
            pltpu.VMEM(Z_SHAPE, F32),
            pltpu.VMEM(Y_SHAPE, F32),
            pltpu.SemaphoreType.DMA((3,)),
        ],
        input_output_aliases={10: 0},
        compiler_params=EDGE_PARAMS,
        name="edge",
    )(half, z_low, z_high, y_rows, *edges, back_table, x_table, grad, planes)
    return grad, part


def hessian_pass(half, ctl, base, grad, front_table, back_table, x_table):
    return pl.pallas_call(
        hessian_kernel,
        in_specs=[SMEM_SPEC] + [VMEM_SPEC] * 2 + [HBM_SPEC] + [VMEM_SPEC] * 3,
        out_specs=[VMEM_SPEC] * 2,
        scratch_shapes=[
            pltpu.VMEM((3, NZ, NY, NX), F32),
            pltpu.VMEM((4 * KPAD, 3 * NX), BF),
            pltpu.VMEM((ROWS, 3 * NX), F32),
            pltpu.VMEM((PLANES, NY, 3 * NX), F32),
            pltpu.SemaphoreType.DMA((NZ // KNOT, 2)),
        ],
        out_shape=[
            jax.ShapeDtypeStruct((CTL, 128), F32),
            jax.ShapeDtypeStruct((8, 128), F32),
        ],
        compiler_params=PARAMS,
        name="hessian",
    )(half, ctl, base, grad, front_table, back_table, x_table)


def passed_along(value, axis, steps):
    count = lax.axis_size(axis)
    initial, last = (max(0, -steps), min(count, count - steps))
    return lax.ppermute(value, axis, [(source, source + steps) for source in range(initial, last)])


def swapped(value):
    return lax.ppermute(value, "gy", [(0, 1), (1, 0)])


def paired(value, mask):
    count = lax.axis_size("gz")
    return lax.ppermute(value, "gz", [(i, i ^ mask) for i in range(count)])


def stage(value, *masks):
    return value + sum(paired(value, mask) for mask in masks)


def outer_paired(value):
    count = lax.axis_size("gz")
    pairs = [(i, i + 1) for i in range(1, count - 1, 2)]
    return lax.ppermute(value, "gz", pairs + [(j, i) for i, j in pairs])


def pair_sum(lower, own, other):
    first, second = jnp.where(lower, own, other), jnp.where(lower, other, own)
    widths = ((0, 2 * CY), (0, 0)), ((2 * CY, 0), (0, 0))
    return jnp.pad(first, widths[0]) + jnp.pad(second, widths[1])


def outer_terms(lower, seven):
    return outer_paired(jnp.where(lower, seven[: 3 * CY], seven[4 * CY :]))


def all_planes(lower, part):
    part = part + swapped(part)
    seven = pair_sum(lower, part, paired(part, 1))
    three = outer_terms(lower, seven)
    one = paired(jnp.where(lower, three[2 * CY :], three[:CY]), 1)
    low = jnp.concatenate([three, jnp.zeros((CY, 128), F32), one], 0) + seven[: 5 * CY]
    high = jnp.concatenate([one, jnp.zeros((CY, 128), F32), three], 0) + seven[2 * CY :]
    row = lax.broadcasted_iota(jnp.int32, (CTL, 128), 0)
    at = lax.axis_index("gz") * (2 * CY) - CY + row
    inside = (at >= 0) & (at < lax.axis_size("gz") * (2 * CY))
    return jnp.where(inside, jnp.where(lower, low, high), 0.0)


def local(moving, fixed):
    half_id = lax.axis_index("gy").astype(jnp.int32)
    half = half_id.reshape(1)
    lower = lax.axis_index("gz") % 2 == 0
    front, back, xt = (jnp.asarray(a) for a in tables())

    z_low = passed_along(moving[-2:], "gz", 1)
    z_high = passed_along(moving[:2], "gz", -1)
    y_rows = swapped(jnp.where(half_id == 0, moving[:, -2:], moving[:, :2]))

    grad, planes, *edges = interior_pass(half, moving, fixed)
    grad, part = edge_pass(half, z_low, z_high, y_rows, edges, back, xt, grad, planes)
    b_planes = all_planes(lower, part)
    b = b_planes[CY : 3 * CY]
    part, _ = hessian_pass(half, b_planes, b, grad, front, back, xt)
    u_planes = all_planes(lower, part)
    u = u_planes[CY : 3 * CY]
    part, sums = hessian_pass(half, u_planes, b, grad, front, back, xt)
    both = jnp.concatenate([part, sums], 0)
    both = both + swapped(both)
    other = paired(both, 1)
    seven = pair_sum(lower, both[:CTL], other[:CTL])
    sums = both[CTL:] + other[CTL:]
    three = outer_terms(lower, seven)
    sums = stage(sums, 2, 4, 6)
    sums, three = lax.optimization_barrier((sums, three))
    sums = stage(stage(sums, 8), 16, 32, 48)
    v_low = seven[CY : 3 * CY] + three[CY:]
    v_high = seven[3 * CY : 5 * CY] + jnp.pad(three[:CY], ((CY, 0), (0, 0)))
    v = jnp.where(lower, v_low, v_high)

    bb, bu, uu, uv = (sums[j : j + 1] for j in range(4))
    a0 = bb / bu
    rr1 = bb - 2.0 * a0 * bu + a0 * a0 * uu
    beta = rr1 / bb
    more = 1.0 + beta
    a1 = rr1 / (more * more * bu - 2.0 * more * a0 * uu + a0 * a0 * uv)
    solution = a0 * b + a1 * (more * b - a0 * u)
    residual = (b - a0 * u) - a1 * (more * u - a0 * v)

    def placed(value):
        turned = value.reshape(2, CY, 128)[:, :, : 3 * CX].reshape(2, CY, 3, CX)
        return turned.transpose(2, 0, 1, 3)

    return placed(solution), placed(residual)


def solution(mesh):
    in_specs = (P("gz", "gy", None), P("gz", "gy", None))
    out_specs = (P(None, "gz", None, None), P(None, "gz", None, None))
    return jax.shard_map(local, mesh=mesh, in_specs=in_specs, out_specs=out_specs, check_vma=False)
```

```python
import jax
import jax.numpy as jnp
import ml_dtypes
import numpy as np
from jax import lax
from jax.experimental import pallas as pl
from jax.experimental.pallas import tpu as pltpu
from jax.sharding import PartitionSpec as P

KNOT = 16
data_weight = 1.0 / 256.0
smooth_weight = 0.1

BF = jnp.bfloat16
F32 = jnp.float32
NZ, NY, NX = 32, 64, 512
ROWS = KNOT * NY
PLANES, CY, CX = 5, 8, 32
CTL = PLANES * CY
KPAD = 48
TILE = 16
WIDE = 128
EDGES = (0, 1, NZ - 2, NZ - 1)


def split(array):
    high = array.astype(ml_dtypes.bfloat16)
    low = (array - high.astype(np.float64)).astype(ml_dtypes.bfloat16)
    return high, low


def spline_weights():
    t = (np.arange(KNOT) + 0.5) / KNOT
    return np.stack(
        [
            (1 - t) ** 3 / 6,
            (3 * t**3 - 6 * t**2 + 4) / 6,
            (-3 * t**3 + 3 * t**2 + 3 * t + 1) / 6,
            t**3 / 6,
        ]
    )


def tables():
    weights = spline_weights()

    def along(blocks, first_block, points, first_point):
        out = np.zeros((blocks * KNOT, points))
        for block in range(blocks):
            for j in range(4):
                point = first_block + block + j - 1 - first_point
                if 0 <= point < points:
                    out[block * KNOT : (block + 1) * KNOT, point] = weights[j]
        return out

    along_z = along(NZ // KNOT, 0, PLANES, -1)
    halves = []
    for half in range(2):
        along_y = along(NY // KNOT, half * (NY // KNOT), CY, 0)
        halves.append(np.einsum("zp,yq->zypq", along_z, along_y).reshape(NZ * NY, CTL))
    high, low = split(np.stack(halves))
    widths = ((0, 0), (0, 0), (0, KPAD - CTL))
    high48, low48 = (np.pad(a, widths) for a in (high, low))
    out_table = np.concatenate([high48, low48, high48, low48], axis=2)
    backs = []
    for half in range(2):
        along_y = along(NY // KNOT, half * (NY // KNOT), CY, 0)
        backs.append(np.concatenate(split(np.kron(np.eye(PLANES), along_y).T), axis=0))
    back_table = np.stack(backs)
    along_x = along(NX // KNOT, 0, CX, 0)
    rows = np.zeros((128, 3 * NX))
    for c in range(3):
        rows[c * CX : (c + 1) * CX, c * NX : (c + 1) * NX] = along_x.T
    x_table = np.concatenate(split(rows), axis=0)
    return out_table, back_table, x_table


def halves_of(value):
    high = value.astype(BF)
    return high, (value - high.astype(F32)).astype(BF)


def block_terms(block, grad, weight_at, planes):
    weights = spline_weights()
    even = (weights[:2] + weights[:2, ::-1]) / 2
    odd = (weights[:2] - weights[:2, ::-1]) / 2

    def strip(y, carry):
        rows = pl.ds(pl.multiple_of(y * 8, 8), 8)
        for x in range(0, NX, WIDE):
            lanes = slice(x, x + WIDE)
            sums = [[[0.0, 0.0], [0.0, 0.0]] for _ in range(3)]
            for i in range(KNOT // 2):
                pair = []
                for z in (i, KNOT - 1 - i):
                    slopes = [grad[c, block * KNOT + z, rows, lanes] for c in range(3)]
                    weight, carry = weight_at(block * KNOT + z, y, lanes, slopes, carry)
                    pair.append([slope * weight for slope in slopes])
                for c in range(3):
                    both, apart = pair[0][c] + pair[1][c], pair[0][c] - pair[1][c]
                    for j in range(2):
                        sums[c][0][j] = sums[c][0][j] + float(even[j, i]) * both
                        sums[c][1][j] = sums[c][1][j] + float(odd[j, i]) * apart
            for c in range(3):
                (e0, e1), (o0, o1) = sums[c]
                at = slice(c * NX + x, c * NX + x + WIDE)
                for j, value in enumerate((e0 + o0, e1 + o1, e1 - o1, e0 - o0)):
                    if block == 0 or j == 3:
                        planes[block + j, rows, at] = value
                    else:
                        planes[block + j, rows, at] += value
        return carry

    return strip


def contracted(planes, back, x_table):
    high, low = halves_of(planes[...].reshape(PLANES * NY, 3 * NX))
    terms = jnp.dot(back, high, preferred_element_type=F32)
    rest = jnp.dot(back[:CTL], low, preferred_element_type=F32)
    high, low = halves_of(terms[:CTL] + (terms[CTL:] + rest))
    both = lax.dot_general(
        jnp.concatenate([high, low], 0),
        x_table[...],
        (((1,), (1,)), ((), ())),
        preferred_element_type=F32,
    )
    return both[:CTL, :128] + (both[:CTL, 128:] + both[CTL:, :128])


def interior_kernel(half, moving, fixed, grad, planes, z_edges, y_edges):
    lane = lax.broadcasted_iota(jnp.int32, (TILE, NX), 1)
    two = jnp.zeros((2, NX), F32)

    def plane(z, shifts):
        center = moving.at[z]
        for y in range(0, NY, TILE):
            here = slice(y, y + TILE)
            value = center[here]

            def at_z(k):
                return moving[z + k, here] if k in shifts else 0.0

            def at_y(k):
                first = y + k
                if first < 0:
                    return jnp.concatenate([two[: -first], center[0 : TILE + first]], 0)
                if first + TILE > NY:
                    return jnp.concatenate([center[first:NY], two[: first + TILE - NY]], 0)
                return center[first : first + TILE]

            def at_x(k):
                moved = pltpu.roll(value, (-k) % NX, 1)
                inside = lane < NX - k if k > 0 else lane >= -k
                return jnp.where(inside, moved, 0.0)

            for c, near in enumerate((at_z, at_y, at_x)):
                grad[c, z, here] = 8.0 * (near(1) - near(-1)) - (near(2) - near(-2))

    every = (-2, -1, 1, 2)

    def body(z, carry):
        plane(z, every)
        return carry

    plane(0, (1, 2))
    plane(1, (-1, 1, 2))
    lax.fori_loop(2, NZ - 2, body, 0)
    plane(NZ - 2, (-2, -1, 1))
    plane(NZ - 1, (-2, -1))

    def weight_at(z, y, lanes, slopes, carry):
        rows = pl.ds(pl.multiple_of(y * 8, 8), 8)
        return moving[z, rows, lanes] - fixed[z, rows, lanes], carry

    for block in range(NZ // KNOT):
        lax.fori_loop(0, NY // 8, block_terms(block, grad, weight_at, planes), 0)
    for e, z in enumerate(EDGES):
        z_edges[e] = moving[z] - fixed[z]
    rows = pl.ds(pl.multiple_of((1 - half[0]) * (NY - 8), 8), 8)
    y_edges[...] = moving[:, rows, :] - fixed[:, rows, :]


def edge_kernel(
    half, z_low, z_high, y_rows, z_edges, y_edges, back, xt, grad_in, planes_in, grad, planes, out
):
    del grad_in, planes_in
    weights = spline_weights()

    def strip(y, carry):
        rows = pl.ds(pl.multiple_of(y * 8, 8), 8)
        near, far = z_low[1, rows], z_low[0, rows]
        above, beyond = z_high[0, rows], z_high[1, rows]
        slopes = (far - 8.0 * near, near, -above, 8.0 * above - beyond)
        for e, z in enumerate(EDGES):
            grad[0, z, rows] += slopes[e]
            term = slopes[e] * z_edges[e, rows]
            for j in range(4):
                at = z // KNOT + j
                planes[at, rows, 0:NX] += float(weights[j, z % KNOT]) * term
        return carry

    lax.fori_loop(0, NY // 8, strip, 0)

    upper = half[0] == 0
    rows = pl.ds(pl.multiple_of((1 - half[0]) * (NY - 8), 8), 8)
    sub = lax.broadcasted_iota(jnp.int32, (8, NX), 0)

    def coefficient(when_upper, otherwise):
        def column(entries):
            value = jnp.zeros((8, NX), F32)
            for row, entry in entries.items():
                value = jnp.where(sub == row, entry, value)
            return value

        return jnp.where(upper, column(when_upper), column(otherwise))

    on_first = coefficient({6: -1.0, 7: 8.0}, {0: 1.0})
    on_second = coefficient({7: -1.0}, {0: -8.0, 1: 1.0})
    for block in range(NZ // KNOT):
        sums = [0.0] * 4
        for i in range(KNOT):
            z = block * KNOT + i
            slope = on_first * y_rows[z, 0:1] + on_second * y_rows[z, 1:2]
            grad[1, z, rows] += slope
            term = slope * y_edges[z]
            sums = [total + float(weights[j, i]) * term for j, total in enumerate(sums)]
        for j, total in enumerate(sums):
            planes[block + j, rows, NX : 2 * NX] += total
    out[...] = contracted(planes, back[half[0]], xt) * (-data_weight / 12.0)


def hessian_kernel(half, ctl, base, grad, front, back, xt, out, sums, spread, field, planes):
    high, low = halves_of(ctl[...])
    first, second = xt[:128], xt[128:]
    value = jnp.dot(high, first, preferred_element_type=F32)
    value += jnp.dot(low, first, preferred_element_type=F32)
    value += jnp.dot(high, second, preferred_element_type=F32)
    value = jnp.concatenate([value, jnp.zeros((KPAD - CTL, 3 * NX), F32)], 0)
    high, low = halves_of(value)
    for j, part in enumerate((high, high, low, low)):
        spread[j * KPAD : (j + 1) * KPAD] = part
    square = jnp.zeros((8, WIDE), F32)

    for block in range(NZ // KNOT):
        at_rows = slice(block * ROWS, (block + 1) * ROWS)
        field[...] = jnp.dot(front[half[0], at_rows], spread[...], preferred_element_type=F32)

        def weight_at(z, y, lanes, slopes, carry):
            rows = pl.ds(pl.multiple_of(z % KNOT * NY + y * 8, 8), 8)
            weight = 0.0
            for c in range(3):
                at = slice(c * NX + lanes.start, c * NX + lanes.stop)
                weight = weight + slopes[c] * field[rows, at]
            return weight, carry + weight * weight

        strip = block_terms(block, grad, weight_at, planes)
        square = lax.fori_loop(0, NY // 8, strip, square, unroll=2)

    scale = data_weight / 144.0
    whole = ctl[...]
    owned = whole[CY : 3 * CY]
    sub = lax.broadcasted_iota(jnp.int32, (2 * CY, 128), 0) % CY
    lane = lax.broadcasted_iota(jnp.int32, (2 * CY, 128), 1) % CX
    near = whole[0 : 2 * CY] + whole[2 * CY : 4 * CY]
    near += jnp.where(sub > 0, pltpu.roll(owned, 1, 0), 0.0)
    near += jnp.where(sub < CY - 1, pltpu.roll(owned, 2 * CY - 1, 0), 0.0)
    near += jnp.where(lane > 0, pltpu.roll(owned, 1, 1), 0.0)
    near += jnp.where(lane < CX - 1, pltpu.roll(owned, 127, 1), 0.0)
    smooth = (0.5 * smooth_weight) * (6.0 * owned - near)
    out[...] = contracted(planes, back[half[0]], xt) * scale
    out[CY : 3 * CY] += smooth
    first = base[...]

    def total(value):
        return jnp.sum(jnp.sum(value, axis=0, keepdims=True), axis=1, keepdims=True)

    whole_square = total(square) * scale + total(smooth * owned)
    lines = [
        0.5 * total(first * first),
        0.5 * total(first * owned),
        0.5 * total(owned * owned),
        whole_square,
    ]
    which = lax.broadcasted_iota(jnp.int32, (8, 128), 0)
    tile = jnp.zeros((8, 128), F32)
    for j, line in enumerate(lines):
        tile = jnp.where(which == j, line, tile)
    sums[...] = tile


VMEM_SPEC = pl.BlockSpec(memory_space=pltpu.VMEM)
SMEM_SPEC = pl.BlockSpec(memory_space=pltpu.SMEM)
PARAMS = pltpu.CompilerParams(vmem_limit_bytes=24 * 1024 * 1024)
SMALL_PARAMS = pltpu.CompilerParams(vmem_limit_bytes=8 * 1024 * 1024)


GRAD_SHAPE = jax.ShapeDtypeStruct((3, NZ, NY, NX), F32)
PLANES_SHAPE = jax.ShapeDtypeStruct((PLANES, NY, 3 * NX), F32)
CTL_SHAPE = jax.ShapeDtypeStruct((CTL, 128), F32)


def interior_pass(half, moving, fixed):
    return pl.pallas_call(
        interior_kernel,
        in_specs=[SMEM_SPEC] + [VMEM_SPEC] * 2,
        out_specs=[VMEM_SPEC] * 4,
        out_shape=[
            GRAD_SHAPE,
            PLANES_SHAPE,
            jax.ShapeDtypeStruct((len(EDGES), NY, NX), F32),
            jax.ShapeDtypeStruct((NZ, 8, NX), F32),
        ],
        compiler_params=SMALL_PARAMS,
        cost_estimate=pl.CostEstimate(flops=100_000_000, bytes_accessed=40_000_000, transcendentals=0),
        name="interior",
    )(half, moving, fixed)


def edge_pass(half, z_low, z_high, y_rows, z_edges, y_edges, back_table, x_table, grad, planes):
    grad, _, part = pl.pallas_call(
        edge_kernel,
        in_specs=[SMEM_SPEC] + [VMEM_SPEC] * 9,
        out_specs=[VMEM_SPEC] * 3,
        out_shape=[GRAD_SHAPE, PLANES_SHAPE, CTL_SHAPE],
        input_output_aliases={8: 0, 9: 1},
        compiler_params=PARAMS,
        name="edge",
    )(half, z_low, z_high, y_rows, z_edges, y_edges, back_table, x_table, grad, planes)
    return grad, part


def hessian_pass(half, ctl, base, grad, front_table, back_table, x_table):
    return pl.pallas_call(
        hessian_kernel,
        in_specs=[SMEM_SPEC] + [VMEM_SPEC] * 6,
        out_specs=[VMEM_SPEC] * 2,
        scratch_shapes=[
            pltpu.VMEM((4 * KPAD, 3 * NX), BF),
            pltpu.VMEM((ROWS, 3 * NX), F32),
            pltpu.VMEM((PLANES, NY, 3 * NX), F32),
        ],
        out_shape=[
            jax.ShapeDtypeStruct((CTL, 128), F32),
            jax.ShapeDtypeStruct((8, 128), F32),
        ],
        compiler_params=PARAMS,
        name="hessian",
    )(half, ctl, base, grad, front_table, back_table, x_table)


def rims_kernel(*refs):
    for source, target in zip(refs[: len(refs) // 2], refs[len(refs) // 2 :]):
        target[...] = source[...]


def rims_pass(*rims):
    return pl.pallas_call(
        rims_kernel,
        in_specs=[VMEM_SPEC] * len(rims),
        out_specs=[VMEM_SPEC] * len(rims),
        out_shape=[jax.ShapeDtypeStruct(rim.shape, F32) for rim in rims],
        compiler_params=SMALL_PARAMS,
        cost_estimate=pl.CostEstimate(flops=20_000_000_000, bytes_accessed=60_000_000, transcendentals=0),
        name="rims",
    )(*rims)


def passed_along(value, axis, steps):
    count = lax.axis_size(axis)
    initial, last = (max(0, -steps), min(count, count - steps))
    return lax.ppermute(value, axis, [(source, source + steps) for source in range(initial, last)])


def swapped(value):
    return lax.ppermute(value, "gy", [(0, 1), (1, 0)])


def paired(value, mask):
    count = lax.axis_size("gz")
    return lax.ppermute(value, "gz", [(i, i ^ mask) for i in range(count)])


def stage(value, *masks):
    return value + sum(paired(value, mask) for mask in masks)


def outer_paired(value):
    count = lax.axis_size("gz")
    pairs = [(i, i + 1) for i in range(1, count - 1, 2)]
    return lax.ppermute(value, "gz", pairs + [(j, i) for i, j in pairs])


def pair_sum(lower, own, other):
    first, second = jnp.where(lower, own, other), jnp.where(lower, other, own)
    widths = ((0, 2 * CY), (0, 0)), ((2 * CY, 0), (0, 0))
    return jnp.pad(first, widths[0]) + jnp.pad(second, widths[1])


def outer_terms(lower, seven):
    return outer_paired(jnp.where(lower, seven[: 3 * CY], seven[4 * CY :]))


def all_planes(lower, inside, part):
    part = part + swapped(part)
    seven = pair_sum(lower, part, paired(part, 1))
    three = outer_terms(lower, seven)
    one = paired(jnp.where(lower, three[2 * CY :], three[:CY]), 1)
    low = jnp.concatenate([three, jnp.zeros((CY, 128), F32), one], 0) + seven[: 5 * CY]
    high = jnp.concatenate([one, jnp.zeros((CY, 128), F32), three], 0) + seven[2 * CY :]
    return inside * jnp.where(lower, low, high)


def local(moving, fixed):
    half_id = lax.axis_index("gy").astype(jnp.int32)
    half = half_id.reshape(1)
    slab = lax.axis_index("gz")
    lower = slab % 2 == 0
    at = slab * (2 * CY) - CY + lax.broadcasted_iota(jnp.int32, (CTL, 128), 0)
    inside = ((at >= 0) & (at < lax.axis_size("gz") * (2 * CY))).astype(F32)
    moving, half_id, half, lower, inside = lax.optimization_barrier(
        (moving, half_id, half, lower, inside)
    )
    front, back, xt = (jnp.asarray(a) for a in tables())

    y_rim = jnp.where(half_id == 0, moving[:, -2:], moving[:, :2])
    top, bottom, y_rim = rims_pass(moving[-2:], moving[:2], y_rim)
    z_low = passed_along(top, "gz", 1)
    z_high = passed_along(bottom, "gz", -1)
    y_rows = swapped(y_rim)

    grad, planes, z_edges, y_edges = interior_pass(half, moving, fixed)
    grad, part = edge_pass(
        half, z_low, z_high, y_rows, z_edges, y_edges, back, xt, grad, planes
    )
    b_planes = all_planes(lower, inside, part)
    b = b_planes[CY : 3 * CY]
    part, _ = hessian_pass(half, b_planes, b, grad, front, back, xt)
    u_planes = all_planes(lower, inside, part)
    u = u_planes[CY : 3 * CY]
    part, sums = hessian_pass(half, u_planes, b, grad, front, back, xt)
    both = jnp.concatenate([part, sums], 0)
    both = both + swapped(both)
    other = paired(both, 1)
    seven = pair_sum(lower, both[:CTL], other[:CTL])
    sums = both[CTL:] + other[CTL:]
    three = outer_terms(lower, seven)
    sums = stage(sums, 2, 4, 6)
    sums, three = lax.optimization_barrier((sums, three))
    sums = stage(stage(sums, 8), 16, 32, 48)
    v_low = seven[CY : 3 * CY] + three[CY:]
    v_high = seven[3 * CY : 5 * CY] + jnp.pad(three[:CY], ((CY, 0), (0, 0)))
    v = jnp.where(lower, v_low, v_high)

    bb, bu, uu, uv = (sums[j : j + 1] for j in range(4))
    a0 = bb / bu
    rr1 = bb - 2.0 * a0 * bu + a0 * a0 * uu
    beta = rr1 / bb
    more = 1.0 + beta
    a1 = rr1 / (more * more * bu - 2.0 * more * a0 * uu + a0 * a0 * uv)
    solution = a0 * b + a1 * (more * b - a0 * u)
    residual = (b - a0 * u) - a1 * (more * u - a0 * v)

    def placed(value):
        turned = value.reshape(2, CY, 128)[:, :, : 3 * CX].reshape(2, CY, 3, CX)
        return turned.transpose(2, 0, 1, 3)

    return placed(solution), placed(residual)


def solution(mesh):
    in_specs = (P("gz", "gy", None), P("gz", "gy", None))
    out_specs = (P(None, "gz", None, None), P(None, "gz", None, None))
    return jax.shard_map(local, mesh=mesh, in_specs=in_specs, out_specs=out_specs, check_vma=False)
```

```python
import jax
import jax.numpy as jnp
import ml_dtypes
import numpy as np
from jax import lax
from jax.experimental import pallas as pl
from jax.experimental.pallas import tpu as pltpu
from jax.sharding import PartitionSpec as P

KNOT = 16
data_weight = 1.0 / 256.0
smooth_weight = 0.1

BF = jnp.bfloat16
F32 = jnp.float32
NZ, NY, NX = 32, 64, 512
ROWS = KNOT * NY
PLANES, CY, CX = 5, 8, 32
CTL = PLANES * CY
KPAD = 48
TILE = 16
WIDE = 128
EDGES = (0, 1, NZ - 2, NZ - 1)


def split(array):
    high = array.astype(ml_dtypes.bfloat16)
    low = (array - high.astype(np.float64)).astype(ml_dtypes.bfloat16)
    return high, low


def spline_weights():
    t = (np.arange(KNOT) + 0.5) / KNOT
    return np.stack(
        [
            (1 - t) ** 3 / 6,
            (3 * t**3 - 6 * t**2 + 4) / 6,
            (-3 * t**3 + 3 * t**2 + 3 * t + 1) / 6,
            t**3 / 6,
        ]
    )


def tables():
    weights = spline_weights()

    def along(blocks, first_block, points, first_point):
        out = np.zeros((blocks * KNOT, points))
        for block in range(blocks):
            for j in range(4):
                point = first_block + block + j - 1 - first_point
                if 0 <= point < points:
                    out[block * KNOT : (block + 1) * KNOT, point] = weights[j]
        return out

    along_z = along(NZ // KNOT, 0, PLANES, -1)
    halves = []
    for half in range(2):
        along_y = along(NY // KNOT, half * (NY // KNOT), CY, 0)
        halves.append(np.einsum("zp,yq->zypq", along_z, along_y).reshape(NZ * NY, CTL))
    high, low = split(np.stack(halves))
    widths = ((0, 0), (0, 0), (0, KPAD - CTL))
    high48, low48 = (np.pad(a, widths) for a in (high, low))
    out_table = np.concatenate([high48, low48, high48, low48], axis=2)
    backs = []
    for half in range(2):
        along_y = along(NY // KNOT, half * (NY // KNOT), CY, 0)
        backs.append(np.concatenate(split(np.kron(np.eye(PLANES), along_y).T), axis=0))
    back_table = np.stack(backs)
    along_x = along(NX // KNOT, 0, CX, 0)
    rows = np.zeros((128, 3 * NX))
    for c in range(3):
        rows[c * CX : (c + 1) * CX, c * NX : (c + 1) * NX] = along_x.T
    x_table = np.concatenate(split(rows), axis=0)
    return out_table, back_table, x_table


def halves_of(value):
    high = value.astype(BF)
    return high, (value - high.astype(F32)).astype(BF)


def block_terms(block, grad, weight_at, planes):
    weights = spline_weights()
    even = (weights[:2] + weights[:2, ::-1]) / 2
    odd = (weights[:2] - weights[:2, ::-1]) / 2

    def strip(y, carry):
        rows = pl.ds(pl.multiple_of(y * 8, 8), 8)
        for x in range(0, NX, WIDE):
            lanes = slice(x, x + WIDE)
            sums = [[[0.0, 0.0], [0.0, 0.0]] for _ in range(3)]
            for i in range(KNOT // 2):
                pair = []
                for z in (i, KNOT - 1 - i):
                    slopes = [grad[c, block * KNOT + z, rows, lanes] for c in range(3)]
                    weight, carry = weight_at(block * KNOT + z, y, lanes, slopes, carry)
                    pair.append([slope * weight for slope in slopes])
                for c in range(3):
                    both, apart = pair[0][c] + pair[1][c], pair[0][c] - pair[1][c]
                    for j in range(2):
                        sums[c][0][j] = sums[c][0][j] + float(even[j, i]) * both
                        sums[c][1][j] = sums[c][1][j] + float(odd[j, i]) * apart
            for c in range(3):
                (e0, e1), (o0, o1) = sums[c]
                at = slice(c * NX + x, c * NX + x + WIDE)
                for j, value in enumerate((e0 + o0, e1 + o1, e1 - o1, e0 - o0)):
                    if block == 0 or j == 3:
                        planes[block + j, rows, at] = value
                    else:
                        planes[block + j, rows, at] += value
        return carry

    return strip


def contracted(planes, back, x_table):
    high, low = halves_of(planes[...].reshape(PLANES * NY, 3 * NX))
    terms = jnp.dot(back, high, preferred_element_type=F32)
    rest = jnp.dot(back[:CTL], low, preferred_element_type=F32)
    high, low = halves_of(terms[:CTL] + (terms[CTL:] + rest))
    both = lax.dot_general(
        jnp.concatenate([high, low], 0),
        x_table[...],
        (((1,), (1,)), ((), ())),
        preferred_element_type=F32,
    )
    return both[:CTL, :128] + (both[:CTL, 128:] + both[CTL:, :128])


def interior_kernel(half, moving, fixed, grad, planes, z_edges, y_edges):
    lane = lax.broadcasted_iota(jnp.int32, (TILE, NX), 1)
    two = jnp.zeros((2, NX), F32)

    def plane(z, shifts):
        center = moving.at[z]
        for y in range(0, NY, TILE):
            here = slice(y, y + TILE)
            value = center[here]

            def at_z(k):
                return moving[z + k, here] if k in shifts else 0.0

            def at_y(k):
                first = y + k
                if first < 0:
                    return jnp.concatenate([two[: -first], center[0 : TILE + first]], 0)
                if first + TILE > NY:
                    return jnp.concatenate([center[first:NY], two[: first + TILE - NY]], 0)
                return center[first : first + TILE]

            def at_x(k):
                moved = pltpu.roll(value, (-k) % NX, 1)
                inside = lane < NX - k if k > 0 else lane >= -k
                return jnp.where(inside, moved, 0.0)

            for c, near in enumerate((at_z, at_y, at_x)):
                grad[c, z, here] = 8.0 * (near(1) - near(-1)) - (near(2) - near(-2))

    every = (-2, -1, 1, 2)

    def body(z, carry):
        plane(z, every)
        return carry

    plane(0, (1, 2))
    plane(1, (-1, 1, 2))
    lax.fori_loop(2, NZ - 2, body, 0, unroll=2)
    plane(NZ - 2, (-2, -1, 1))
    plane(NZ - 1, (-2, -1))

    def weight_at(z, y, lanes, slopes, carry):
        rows = pl.ds(pl.multiple_of(y * 8, 8), 8)
        return moving[z, rows, lanes] - fixed[z, rows, lanes], carry

    for block in range(NZ // KNOT):
        lax.fori_loop(0, NY // 8, block_terms(block, grad, weight_at, planes), 0, unroll=2)
    for e, z in enumerate(EDGES):
        z_edges[e] = moving[z] - fixed[z]
    rows = pl.ds(pl.multiple_of((1 - half[0]) * (NY - 8), 8), 8)
    y_edges[...] = moving[:, rows, :] - fixed[:, rows, :]


def edge_kernel(
    half, inner, outer, y_rows, z_edges, y_edges, back, xt, grad_in, planes_in, grad, planes, out
):
    del grad_in, planes_in
    lower = half[1] == 0
    weights = spline_weights()

    def strip(y, carry):
        rows = pl.ds(pl.multiple_of(y * 8, 8), 8)
        near, far = (jnp.where(lower, outer[z, rows], inner[z, rows]) for z in (1, 0))
        above, beyond = (jnp.where(lower, inner[z, rows], outer[z, rows]) for z in (0, 1))
        slopes = (far - 8.0 * near, near, -above, 8.0 * above - beyond)
        for e, z in enumerate(EDGES):
            grad[0, z, rows] += slopes[e]
            term = slopes[e] * z_edges[e, rows]
            for j in range(4):
                at = z // KNOT + j
                planes[at, rows, 0:NX] += float(weights[j, z % KNOT]) * term
        return carry

    lax.fori_loop(0, NY // 8, strip, 0)

    upper = half[0] == 0
    rows = pl.ds(pl.multiple_of((1 - half[0]) * (NY - 8), 8), 8)
    sub = lax.broadcasted_iota(jnp.int32, (8, NX), 0)

    def coefficient(when_upper, otherwise):
        def column(entries):
            value = jnp.zeros((8, NX), F32)
            for row, entry in entries.items():
                value = jnp.where(sub == row, entry, value)
            return value

        return jnp.where(upper, column(when_upper), column(otherwise))

    on_first = coefficient({6: -1.0, 7: 8.0}, {0: 1.0})
    on_second = coefficient({7: -1.0}, {0: -8.0, 1: 1.0})
    for block in range(NZ // KNOT):
        sums = [0.0] * 4
        for i in range(KNOT):
            z = block * KNOT + i
            slope = on_first * y_rows[z, 0:1] + on_second * y_rows[z, 1:2]
            grad[1, z, rows] += slope
            term = slope * y_edges[z]
            sums = [total + float(weights[j, i]) * term for j, total in enumerate(sums)]
        for j, total in enumerate(sums):
            planes[block + j, rows, NX : 2 * NX] += total
    out[...] = contracted(planes, back[half[0]], xt) * (-data_weight / 12.0)


def hessian_kernel(half, ctl, base, grad, front, back, xt, out, sums, spread, field, planes):
    high, low = halves_of(ctl[...])
    first, second = xt[:128], xt[128:]
    value = jnp.dot(high, first, preferred_element_type=F32)
    value += jnp.dot(low, first, preferred_element_type=F32)
    value += jnp.dot(high, second, preferred_element_type=F32)
    value = jnp.concatenate([value, jnp.zeros((KPAD - CTL, 3 * NX), F32)], 0)
    high, low = halves_of(value)
    for j, part in enumerate((high, high, low, low)):
        spread[j * KPAD : (j + 1) * KPAD] = part
    square = jnp.zeros((8, WIDE), F32)

    for block in range(NZ // KNOT):
        at_rows = slice(block * ROWS, (block + 1) * ROWS)
        field[...] = jnp.dot(front[half[0], at_rows], spread[...], preferred_element_type=F32)

        def weight_at(z, y, lanes, slopes, carry):
            rows = pl.ds(pl.multiple_of(z % KNOT * NY + y * 8, 8), 8)
            weight = 0.0
            for c in range(3):
                at = slice(c * NX + lanes.start, c * NX + lanes.stop)
                weight = weight + slopes[c] * field[rows, at]
            return weight, carry + weight * weight

        strip = block_terms(block, grad, weight_at, planes)
        square = lax.fori_loop(0, NY // 8, strip, square, unroll=2)

    scale = data_weight / 144.0
    whole = ctl[...]
    owned = whole[CY : 3 * CY]
    sub = lax.broadcasted_iota(jnp.int32, (2 * CY, 128), 0) % CY
    lane = lax.broadcasted_iota(jnp.int32, (2 * CY, 128), 1) % CX
    near = whole[0 : 2 * CY] + whole[2 * CY : 4 * CY]
    near += jnp.where(sub > 0, pltpu.roll(owned, 1, 0), 0.0)
    near += jnp.where(sub < CY - 1, pltpu.roll(owned, 2 * CY - 1, 0), 0.0)
    near += jnp.where(lane > 0, pltpu.roll(owned, 1, 1), 0.0)
    near += jnp.where(lane < CX - 1, pltpu.roll(owned, 127, 1), 0.0)
    smooth = (0.5 * smooth_weight) * (6.0 * owned - near)
    out[...] = contracted(planes, back[half[0]], xt) * scale
    out[CY : 3 * CY] += smooth
    first = base[...]

    def total(value):
        return jnp.sum(jnp.sum(value, axis=0, keepdims=True), axis=1, keepdims=True)

    whole_square = total(square) * scale + total(smooth * owned)
    lines = [
        0.5 * total(first * first),
        0.5 * total(first * owned),
        0.5 * total(owned * owned),
        whole_square,
    ]
    which = lax.broadcasted_iota(jnp.int32, (8, 128), 0)
    tile = jnp.zeros((8, 128), F32)
    for j, line in enumerate(lines):
        tile = jnp.where(which == j, line, tile)
    sums[...] = tile


VMEM_SPEC = pl.BlockSpec(memory_space=pltpu.VMEM)
HBM_SPEC = pl.BlockSpec(memory_space=pltpu.HBM)
SMEM_SPEC = pl.BlockSpec(memory_space=pltpu.SMEM)
PARAMS = pltpu.CompilerParams(vmem_limit_bytes=24 * 1024 * 1024)
RIMS_MIB = 52
SMALL_PARAMS = pltpu.CompilerParams(vmem_limit_bytes=8 * 1024 * 1024)


GRAD_SHAPE = jax.ShapeDtypeStruct((3, NZ, NY, NX), F32)
PLANES_SHAPE = jax.ShapeDtypeStruct((PLANES, NY, 3 * NX), F32)
CTL_SHAPE = jax.ShapeDtypeStruct((CTL, 128), F32)


def interior_pass(half, moving, fixed):
    return pl.pallas_call(
        interior_kernel,
        in_specs=[SMEM_SPEC] + [VMEM_SPEC] * 2,
        out_specs=[VMEM_SPEC] * 4,
        out_shape=[
            GRAD_SHAPE,
            PLANES_SHAPE,
            jax.ShapeDtypeStruct((len(EDGES), NY, NX), F32),
            jax.ShapeDtypeStruct((NZ, 8, NX), F32),
        ],
        compiler_params=SMALL_PARAMS,
        cost_estimate=pl.CostEstimate(flops=100_000_000, bytes_accessed=40_000_000, transcendentals=0),
        name="interior",
    )(half, moving, fixed)


def edge_pass(half, inner, outer, y_rows, z_edges, y_edges, back_table, x_table, grad, planes):
    grad, _, part = pl.pallas_call(
        edge_kernel,
        in_specs=[SMEM_SPEC] + [VMEM_SPEC] * 9,
        out_specs=[VMEM_SPEC] * 3,
        out_shape=[GRAD_SHAPE, PLANES_SHAPE, CTL_SHAPE],
        input_output_aliases={8: 0, 9: 1},
        compiler_params=PARAMS,
        name="edge",
    )(half, inner, outer, y_rows, z_edges, y_edges, back_table, x_table, grad, planes)
    return grad, part


def hessian_pass(half, ctl, base, grad, front_table, back_table, x_table):
    return pl.pallas_call(
        hessian_kernel,
        in_specs=[SMEM_SPEC] + [VMEM_SPEC] * 6,
        out_specs=[VMEM_SPEC] * 2,
        scratch_shapes=[
            pltpu.VMEM((4 * KPAD, 3 * NX), BF),
            pltpu.VMEM((ROWS, 3 * NX), F32),
            pltpu.VMEM((PLANES, NY, 3 * NX), F32),
        ],
        out_shape=[
            jax.ShapeDtypeStruct((CTL, 128), F32),
            jax.ShapeDtypeStruct((8, 128), F32),
        ],
        compiler_params=PARAMS,
        name="hessian",
    )(half, ctl, base, grad, front_table, back_table, x_table)


def rims_kernel(place, moving, inner, outer, y_rim, tile, sems):
    half, parity = place[0], place[1]
    top, bottom = NZ - 2, 0
    copies = [
        pltpu.make_async_copy(
            moving.at[pl.ds(jnp.where(parity == 0, top, bottom), 2)], inner, sems.at[0]
        ),
        pltpu.make_async_copy(
            moving.at[pl.ds(jnp.where(parity == 0, bottom, top), 2)], outer, sems.at[1]
        ),
        pltpu.make_async_copy(
            moving.at[:, pl.ds(pl.multiple_of((1 - half) * (NY - 8), 8), 8)], tile, sems.at[2]
        ),
    ]
    for copy in copies:
        copy.start()
    for copy in copies:
        copy.wait()
    y_rim[...] = jnp.where(half == 0, tile[:, 6:8, :], tile[:, 0:2, :])


def rims_pass(place, moving):
    return pl.pallas_call(
        rims_kernel,
        in_specs=[SMEM_SPEC, HBM_SPEC],
        out_specs=[VMEM_SPEC] * 3,
        out_shape=[jax.ShapeDtypeStruct(shape, F32) for shape in ((2, NY, NX), (2, NY, NX), (NZ, 2, NX))],
        scratch_shapes=[pltpu.VMEM((NZ, 8, NX), F32), pltpu.SemaphoreType.DMA((3,))],
        compiler_params=pltpu.CompilerParams(vmem_limit_bytes=RIMS_MIB * 1024 * 1024),
        name="rims",
    )(place, moving)


def held_kernel(*refs):
    for source, target in zip(refs[: len(refs) // 2], refs[len(refs) // 2 :]):
        target[...] = source[...]


def held(*rims):
    return pl.pallas_call(
        held_kernel,
        in_specs=[VMEM_SPEC] * len(rims),
        out_specs=[VMEM_SPEC] * len(rims),
        out_shape=[jax.ShapeDtypeStruct(rim.shape, F32) for rim in rims],
        compiler_params=SMALL_PARAMS,
        cost_estimate=pl.CostEstimate(flops=20_000_000_000, bytes_accessed=60_000_000, transcendentals=0),
        name="held",
    )(*rims)


def placed_kernel(solution, residual, solution_out, residual_out):
    for value, out in ((solution[...], solution_out), (residual[...], residual_out)):
        for c in range(3):
            moved = pltpu.roll(value, (-c * CX) % 128, 1) if c else value
            for plane in range(2):
                out[c, plane] = moved[plane * CY : (plane + 1) * CY, :CX]


def placed(solution, residual):
    return pl.pallas_call(
        placed_kernel,
        in_specs=[VMEM_SPEC] * 2,
        out_specs=[VMEM_SPEC] * 2,
        out_shape=[jax.ShapeDtypeStruct((3, 2, CY, CX), F32)] * 2,
        compiler_params=SMALL_PARAMS,
        name="placed",
    )(solution, residual)


def swapped(value):
    return lax.ppermute(value, "gy", [(0, 1), (1, 0)])


def paired(value, mask):
    count = lax.axis_size("gz")
    return lax.ppermute(value, "gz", [(i, i ^ mask) for i in range(count)])


def stage(value, *masks):
    return value + sum(paired(value, mask) for mask in masks)


def outer_paired(value):
    count = lax.axis_size("gz")
    pairs = [(i, i + 1) for i in range(1, count - 1, 2)]
    return lax.ppermute(value, "gz", pairs + [(j, i) for i, j in pairs])


def pair_sum(lower, own, other):
    first, second = jnp.where(lower, own, other), jnp.where(lower, other, own)
    widths = ((0, 2 * CY), (0, 0)), ((2 * CY, 0), (0, 0))
    return jnp.pad(first, widths[0]) + jnp.pad(second, widths[1])


def outer_terms(lower, seven):
    return outer_paired(jnp.where(lower, seven[: 3 * CY], seven[4 * CY :]))


def all_planes(lower, inside, part):
    part = part + swapped(part)
    seven = pair_sum(lower, part, paired(part, 1))
    three = outer_terms(lower, seven)
    one = paired(jnp.where(lower, three[2 * CY :], three[:CY]), 1)
    low = jnp.concatenate([three, jnp.zeros((CY, 128), F32), one], 0) + seven[: 5 * CY]
    high = jnp.concatenate([one, jnp.zeros((CY, 128), F32), three], 0) + seven[2 * CY :]
    return inside * jnp.where(lower, low, high)


def local(moving, fixed):
    slab = lax.axis_index("gz").astype(jnp.int32)
    half = jnp.stack([lax.axis_index("gy").astype(jnp.int32), slab % 2])
    lower = slab % 2 == 0
    at = slab * (2 * CY) - CY + lax.broadcasted_iota(jnp.int32, (CTL, 128), 0)
    inside = ((at >= 0) & (at < lax.axis_size("gz") * (2 * CY))).astype(F32)
    moving, half, lower, inside = lax.optimization_barrier((moving, half, lower, inside))
    front, back, xt = (jnp.asarray(a) for a in tables())

    inner, outer, y_rim = held(*rims_pass(half, moving))
    inner = paired(inner, 1)
    outer = outer_paired(outer)
    y_rows = swapped(y_rim)

    grad, planes, z_edges, y_edges = interior_pass(half, moving, fixed)
    grad, part = edge_pass(
        half, inner, outer, y_rows, z_edges, y_edges, back, xt, grad, planes
    )
    b_planes = all_planes(lower, inside, part)
    b = b_planes[CY : 3 * CY]
    part, _ = hessian_pass(half, b_planes, b, grad, front, back, xt)
    u_planes = all_planes(lower, inside, part)
    u = u_planes[CY : 3 * CY]
    part, sums = hessian_pass(half, u_planes, b, grad, front, back, xt)
    both = jnp.concatenate([part, sums], 0)
    both = both + swapped(both)
    other = paired(both, 1)
    seven = pair_sum(lower, both[:CTL], other[:CTL])
    sums = both[CTL:] + other[CTL:]
    three = outer_terms(lower, seven)
    sums = stage(sums, 2, 4, 6)
    sums, three = lax.optimization_barrier((sums, three))
    sums = stage(stage(sums, 8), 16, 32, 48)
    v_low = seven[CY : 3 * CY] + three[CY:]
    v_high = seven[3 * CY : 5 * CY] + jnp.pad(three[:CY], ((CY, 0), (0, 0)))
    v = jnp.where(lower, v_low, v_high)

    bb, bu, uu, uv = (sums[j : j + 1] for j in range(4))
    a0 = bb / bu
    rr1 = bb - 2.0 * a0 * bu + a0 * a0 * uu
    beta = rr1 / bb
    more = 1.0 + beta
    a1 = rr1 / (more * more * bu - 2.0 * more * a0 * uu + a0 * a0 * uv)
    solution = a0 * b + a1 * (more * b - a0 * u)
    residual = (b - a0 * u) - a1 * (more * u - a0 * v)

    return tuple(placed(solution, residual))


def solution(mesh):
    in_specs = (P("gz", "gy", None), P("gz", "gy", None))
    out_specs = (P(None, "gz", None, None), P(None, "gz", None, None))
    return jax.shard_map(local, mesh=mesh, in_specs=in_specs, out_specs=out_specs, check_vma=False)
```

```python
import jax
import jax.numpy as jnp
import ml_dtypes
import numpy as np
from jax import lax
from jax.experimental import pallas as pl
from jax.experimental.pallas import tpu as pltpu
from jax.sharding import PartitionSpec as P

KNOT = 16
data_weight = 1.0 / 256.0
smooth_weight = 0.1

BF = jnp.bfloat16
F32 = jnp.float32
NZ, NY, NX = 32, 64, 512
ROWS = KNOT * NY
PLANES, CY, CX = 5, 8, 32
CTL = PLANES * CY
KPAD = 48
TILE = 16
WIDE = 128
EDGES = (0, 1, NZ - 2, NZ - 1)


def split(array):
    high = array.astype(ml_dtypes.bfloat16)
    low = (array - high.astype(np.float64)).astype(ml_dtypes.bfloat16)
    return high, low


def spline_weights():
    t = (np.arange(KNOT) + 0.5) / KNOT
    return np.stack(
        [
            (1 - t) ** 3 / 6,
            (3 * t**3 - 6 * t**2 + 4) / 6,
            (-3 * t**3 + 3 * t**2 + 3 * t + 1) / 6,
            t**3 / 6,
        ]
    )


def tables():
    weights = spline_weights()

    def along(blocks, first_block, points, first_point):
        out = np.zeros((blocks * KNOT, points))
        for block in range(blocks):
            for j in range(4):
                point = first_block + block + j - 1 - first_point
                if 0 <= point < points:
                    out[block * KNOT : (block + 1) * KNOT, point] = weights[j]
        return out

    along_z = along(NZ // KNOT, 0, PLANES, -1)
    halves = []
    for half in range(2):
        along_y = along(NY // KNOT, half * (NY // KNOT), CY, 0)
        halves.append(np.einsum("zp,yq->zypq", along_z, along_y).reshape(NZ * NY, CTL))
    high, low = split(np.stack(halves))
    widths = ((0, 0), (0, 0), (0, KPAD - CTL))
    high48, low48 = (np.pad(a, widths) for a in (high, low))
    out_table = np.concatenate([high48, low48, high48, low48], axis=2)
    backs = []
    for half in range(2):
        along_y = along(NY // KNOT, half * (NY // KNOT), CY, 0)
        backs.append(np.concatenate(split(np.kron(np.eye(PLANES), along_y).T), axis=0))
    back_table = np.stack(backs)
    along_x = along(NX // KNOT, 0, CX, 0)
    rows = np.zeros((128, 3 * NX))
    for c in range(3):
        rows[c * CX : (c + 1) * CX, c * NX : (c + 1) * NX] = along_x.T
    x_table = np.concatenate(split(rows), axis=0)
    return out_table, back_table, x_table


def halves_of(value):
    high = value.astype(BF)
    return high, (value - high.astype(F32)).astype(BF)


def block_terms(block, grad, weight_at, planes):
    weights = spline_weights()
    even = (weights[:2] + weights[:2, ::-1]) / 2
    odd = (weights[:2] - weights[:2, ::-1]) / 2

    def strip(y, carry):
        rows = pl.ds(pl.multiple_of(y * 8, 8), 8)
        for x in range(0, NX, WIDE):
            lanes = slice(x, x + WIDE)
            sums = [[[0.0, 0.0], [0.0, 0.0]] for _ in range(3)]
            for i in range(KNOT // 2):
                pair = []
                for z in (i, KNOT - 1 - i):
                    slopes = [grad[c, block * KNOT + z, rows, lanes] for c in range(3)]
                    weight, carry = weight_at(block * KNOT + z, y, lanes, slopes, carry)
                    pair.append([slope * weight for slope in slopes])
                for c in range(3):
                    both, apart = pair[0][c] + pair[1][c], pair[0][c] - pair[1][c]
                    for j in range(2):
                        sums[c][0][j] = sums[c][0][j] + float(even[j, i]) * both
                        sums[c][1][j] = sums[c][1][j] + float(odd[j, i]) * apart
            for c in range(3):
                (e0, e1), (o0, o1) = sums[c]
                at = slice(c * NX + x, c * NX + x + WIDE)
                for j, value in enumerate((e0 + o0, e1 + o1, e1 - o1, e0 - o0)):
                    if block == 0 or j == 3:
                        planes[block + j, rows, at] = value
                    else:
                        planes[block + j, rows, at] += value
        return carry

    return strip


def contracted(planes, back, x_table):
    high, low = halves_of(planes[...].reshape(PLANES * NY, 3 * NX))
    terms = jnp.dot(back, high, preferred_element_type=F32)
    rest = jnp.dot(back[:CTL], low, preferred_element_type=F32)
    high, low = halves_of(terms[:CTL] + (terms[CTL:] + rest))
    both = lax.dot_general(
        jnp.concatenate([high, low], 0),
        x_table[...],
        (((1,), (1,)), ((), ())),
        preferred_element_type=F32,
    )
    return both[:CTL, :128] + (both[:CTL, 128:] + both[CTL:, :128])


def interior_kernel(half, moving, fixed, grad, planes, z_edges, y_edges):
    lane = lax.broadcasted_iota(jnp.int32, (TILE, NX), 1)
    two = jnp.zeros((2, NX), F32)

    def plane(z, shifts):
        center = moving.at[z]
        for y in range(0, NY, TILE):
            here = slice(y, y + TILE)
            value = center[here]

            def at_z(k):
                return moving[z + k, here] if k in shifts else 0.0

            def at_y(k):
                first = y + k
                if first < 0:
                    return jnp.concatenate([two[: -first], center[0 : TILE + first]], 0)
                if first + TILE > NY:
                    return jnp.concatenate([center[first:NY], two[: first + TILE - NY]], 0)
                return center[first : first + TILE]

            def at_x(k):
                moved = pltpu.roll(value, (-k) % NX, 1)
                inside = lane < NX - k if k > 0 else lane >= -k
                return jnp.where(inside, moved, 0.0)

            for c, near in enumerate((at_z, at_y, at_x)):
                grad[c, z, here] = 8.0 * (near(1) - near(-1)) - (near(2) - near(-2))

    every = (-2, -1, 1, 2)

    def body(z, carry):
        plane(z, every)
        return carry

    plane(0, (1, 2))
    plane(1, (-1, 1, 2))
    lax.fori_loop(2, NZ - 2, body, 0, unroll=2)
    plane(NZ - 2, (-2, -1, 1))
    plane(NZ - 1, (-2, -1))

    def weight_at(z, y, lanes, slopes, carry):
        rows = pl.ds(pl.multiple_of(y * 8, 8), 8)
        return moving[z, rows, lanes] - fixed[z, rows, lanes], carry

    for block in range(NZ // KNOT):
        lax.fori_loop(0, NY // 8, block_terms(block, grad, weight_at, planes), 0, unroll=2)
    for e, z in enumerate(EDGES):
        z_edges[e] = moving[z] - fixed[z]
    rows = pl.ds(pl.multiple_of((1 - half[0]) * (NY - 8), 8), 8)
    y_edges[...] = moving[:, rows, :] - fixed[:, rows, :]


def edge_kernel(
    half, parity, inner, outer, y_rows, z_edges, y_edges, back, xt, grad_in, planes_in, grad, planes, out
):
    del grad_in, planes_in
    lower = parity[0] == 0
    weights = spline_weights()

    def strip(y, carry):
        rows = pl.ds(pl.multiple_of(y * 8, 8), 8)
        near, far = (jnp.where(lower, outer[z, rows], inner[z, rows]) for z in (1, 0))
        above, beyond = (jnp.where(lower, inner[z, rows], outer[z, rows]) for z in (0, 1))
        slopes = (far - 8.0 * near, near, -above, 8.0 * above - beyond)
        for e, z in enumerate(EDGES):
            grad[0, z, rows] += slopes[e]
            term = slopes[e] * z_edges[e, rows]
            for j in range(4):
                at = z // KNOT + j
                planes[at, rows, 0:NX] += float(weights[j, z % KNOT]) * term
        return carry

    lax.fori_loop(0, NY // 8, strip, 0)

    upper = half[0] == 0
    rows = pl.ds(pl.multiple_of((1 - half[0]) * (NY - 8), 8), 8)
    sub = lax.broadcasted_iota(jnp.int32, (8, NX), 0)

    def coefficient(when_upper, otherwise):
        def column(entries):
            value = jnp.zeros((8, NX), F32)
            for row, entry in entries.items():
                value = jnp.where(sub == row, entry, value)
            return value

        return jnp.where(upper, column(when_upper), column(otherwise))

    on_first = coefficient({6: -1.0, 7: 8.0}, {0: 1.0})
    on_second = coefficient({7: -1.0}, {0: -8.0, 1: 1.0})
    for block in range(NZ // KNOT):
        sums = [0.0] * 4
        for i in range(KNOT):
            z = block * KNOT + i
            slope = on_first * y_rows[z, 0:1] + on_second * y_rows[z, 1:2]
            grad[1, z, rows] += slope
            term = slope * y_edges[z]
            sums = [total + float(weights[j, i]) * term for j, total in enumerate(sums)]
        for j, total in enumerate(sums):
            planes[block + j, rows, NX : 2 * NX] += total
    out[...] = contracted(planes, back[half[0]], xt) * (-data_weight / 12.0)


def hessian_kernel(half, ctl, base, grad, front, back, xt, out, spread, field, planes):
    high, low = halves_of(ctl[...])
    first, second = xt[:128], xt[128:]
    value = jnp.dot(high, first, preferred_element_type=F32)
    value += jnp.dot(low, first, preferred_element_type=F32)
    value += jnp.dot(high, second, preferred_element_type=F32)
    value = jnp.concatenate([value, jnp.zeros((KPAD - CTL, 3 * NX), F32)], 0)
    high, low = halves_of(value)
    for j, part in enumerate((high, high, low, low)):
        spread[j * KPAD : (j + 1) * KPAD] = part
    square = jnp.zeros((8, WIDE), F32)

    for block in range(NZ // KNOT):
        at_rows = slice(block * ROWS, (block + 1) * ROWS)
        field[...] = jnp.dot(front[half[0], at_rows], spread[...], preferred_element_type=F32)

        def weight_at(z, y, lanes, slopes, carry):
            rows = pl.ds(pl.multiple_of(z % KNOT * NY + y * 8, 8), 8)
            weight = 0.0
            for c in range(3):
                at = slice(c * NX + lanes.start, c * NX + lanes.stop)
                weight = weight + slopes[c] * field[rows, at]
            return weight, carry + weight * weight

        strip = block_terms(block, grad, weight_at, planes)
        square = lax.fori_loop(0, NY // 8, strip, square, unroll=2)

    scale = data_weight / 144.0
    whole = ctl[...]
    owned = whole[CY : 3 * CY]
    sub = lax.broadcasted_iota(jnp.int32, (2 * CY, 128), 0) % CY
    lane = lax.broadcasted_iota(jnp.int32, (2 * CY, 128), 1) % CX
    near = whole[0 : 2 * CY] + whole[2 * CY : 4 * CY]
    near += jnp.where(sub > 0, pltpu.roll(owned, 1, 0), 0.0)
    near += jnp.where(sub < CY - 1, pltpu.roll(owned, 2 * CY - 1, 0), 0.0)
    near += jnp.where(lane > 0, pltpu.roll(owned, 1, 1), 0.0)
    near += jnp.where(lane < CX - 1, pltpu.roll(owned, 127, 1), 0.0)
    smooth = (0.5 * smooth_weight) * (6.0 * owned - near)
    out[:CTL] = contracted(planes, back[half[0]], xt) * scale
    out[CY : 3 * CY] += smooth
    first = base[...]

    def total(value):
        return jnp.sum(jnp.sum(value, axis=0, keepdims=True), axis=1, keepdims=True)

    whole_square = total(square) * scale + total(smooth * owned)
    lines = [
        0.5 * total(first * first),
        0.5 * total(first * owned),
        0.5 * total(owned * owned),
        whole_square,
    ]
    which = lax.broadcasted_iota(jnp.int32, (8, 128), 0)
    tile = jnp.zeros((8, 128), F32)
    for j, line in enumerate(lines):
        tile = jnp.where(which == j, line, tile)
    out[CTL:] = tile


VMEM_SPEC = pl.BlockSpec(memory_space=pltpu.VMEM)
HBM_SPEC = pl.BlockSpec(memory_space=pltpu.HBM)
SMEM_SPEC = pl.BlockSpec(memory_space=pltpu.SMEM)
PARAMS = pltpu.CompilerParams(vmem_limit_bytes=24 * 1024 * 1024)
RIMS_MIB = 52
SMALL_PARAMS = pltpu.CompilerParams(vmem_limit_bytes=8 * 1024 * 1024)


GRAD_SHAPE = jax.ShapeDtypeStruct((3, NZ, NY, NX), F32)
PLANES_SHAPE = jax.ShapeDtypeStruct((PLANES, NY, 3 * NX), F32)
CTL_SHAPE = jax.ShapeDtypeStruct((CTL, 128), F32)


def interior_pass(half, moving, fixed):
    return pl.pallas_call(
        interior_kernel,
        in_specs=[SMEM_SPEC] + [VMEM_SPEC] * 2,
        out_specs=[VMEM_SPEC] * 4,
        out_shape=[
            GRAD_SHAPE,
            PLANES_SHAPE,
            jax.ShapeDtypeStruct((len(EDGES), NY, NX), F32),
            jax.ShapeDtypeStruct((NZ, 8, NX), F32),
        ],
        compiler_params=SMALL_PARAMS,
        cost_estimate=pl.CostEstimate(flops=100_000_000, bytes_accessed=40_000_000, transcendentals=0),
        name="interior",
    )(half, moving, fixed)


def edge_pass(half, parity, inner, outer, y_rows, z_edges, y_edges, back_table, x_table, grad, planes):
    grad, _, part = pl.pallas_call(
        edge_kernel,
        in_specs=[SMEM_SPEC] * 2 + [VMEM_SPEC] * 9,
        out_specs=[VMEM_SPEC] * 3,
        out_shape=[GRAD_SHAPE, PLANES_SHAPE, CTL_SHAPE],
        input_output_aliases={9: 0, 10: 1},
        compiler_params=PARAMS,
        name="edge",
    )(half, parity, inner, outer, y_rows, z_edges, y_edges, back_table, x_table, grad, planes)
    return grad, part


def hessian_pass(half, ctl, base, grad, front_table, back_table, x_table):
    return pl.pallas_call(
        hessian_kernel,
        in_specs=[SMEM_SPEC] + [VMEM_SPEC] * 6,
        out_specs=VMEM_SPEC,
        scratch_shapes=[
            pltpu.VMEM((4 * KPAD, 3 * NX), BF),
            pltpu.VMEM((ROWS, 3 * NX), F32),
            pltpu.VMEM((PLANES, NY, 3 * NX), F32),
        ],
        out_shape=jax.ShapeDtypeStruct((CTL + 8, 128), F32),
        compiler_params=PARAMS,
        name="hessian",
    )(half, ctl, base, grad, front_table, back_table, x_table)


def rims_kernel(half, parity, moving, inner, outer, y_rim, tile, sems):
    half, parity = half[0], parity[0]
    top, bottom = NZ - 2, 0
    copies = [
        pltpu.make_async_copy(
            moving.at[pl.ds(jnp.where(parity == 0, top, bottom), 2)], inner, sems.at[0]
        ),
        pltpu.make_async_copy(
            moving.at[pl.ds(jnp.where(parity == 0, bottom, top), 2)], outer, sems.at[1]
        ),
        pltpu.make_async_copy(
            moving.at[:, pl.ds(pl.multiple_of((1 - half) * (NY - 8), 8), 8)], tile, sems.at[2]
        ),
    ]
    for copy in copies:
        copy.start()
    for copy in copies:
        copy.wait()
    y_rim[...] = jnp.where(half == 0, tile[:, 6:8, :], tile[:, 0:2, :])


def rims_pass(half, parity, moving):
    return pl.pallas_call(
        rims_kernel,
        in_specs=[SMEM_SPEC, SMEM_SPEC, HBM_SPEC],
        out_specs=[VMEM_SPEC] * 3,
        out_shape=[jax.ShapeDtypeStruct(shape, F32) for shape in ((2, NY, NX), (2, NY, NX), (NZ, 2, NX))],
        scratch_shapes=[pltpu.VMEM((NZ, 8, NX), F32), pltpu.SemaphoreType.DMA((3,))],
        compiler_params=pltpu.CompilerParams(vmem_limit_bytes=RIMS_MIB * 1024 * 1024),
        name="rims",
    )(half, parity, moving)


def held_kernel(*refs):
    for source, target in zip(refs[: len(refs) // 2], refs[len(refs) // 2 :]):
        target[...] = source[...]


def held(*rims):
    return pl.pallas_call(
        held_kernel,
        in_specs=[VMEM_SPEC] * len(rims),
        out_specs=[VMEM_SPEC] * len(rims),
        out_shape=[jax.ShapeDtypeStruct(rim.shape, F32) for rim in rims],
        compiler_params=SMALL_PARAMS,
        cost_estimate=pl.CostEstimate(flops=20_000_000_000, bytes_accessed=60_000_000, transcendentals=0),
        name="held",
    )(*rims)


def placed_kernel(solution, residual, solution_out, residual_out):
    for value, out in ((solution[...], solution_out), (residual[...], residual_out)):
        for c in range(3):
            moved = pltpu.roll(value, (-c * CX) % 128, 1) if c else value
            for plane in range(2):
                out[c, plane] = moved[plane * CY : (plane + 1) * CY, :CX]


def placed(solution, residual):
    return pl.pallas_call(
        placed_kernel,
        in_specs=[VMEM_SPEC] * 2,
        out_specs=[VMEM_SPEC] * 2,
        out_shape=[jax.ShapeDtypeStruct((3, 2, CY, CX), F32)] * 2,
        compiler_params=SMALL_PARAMS,
        name="placed",
    )(solution, residual)


def swapped(value):
    return lax.ppermute(value, "gy", [(0, 1), (1, 0)])


def paired(value, mask):
    count = lax.axis_size("gz")
    return lax.ppermute(value, "gz", [(i, i ^ mask) for i in range(count)])


def stage(value, *masks):
    return value + sum(paired(value, mask) for mask in masks)


def outer_paired(value):
    count = lax.axis_size("gz")
    pairs = [(i, i + 1) for i in range(1, count - 1, 2)]
    return lax.ppermute(value, "gz", pairs + [(j, i) for i, j in pairs])


def pair_sum(lower, own, other):
    first, second = jnp.where(lower, own, other), jnp.where(lower, other, own)
    widths = ((0, 2 * CY), (0, 0)), ((2 * CY, 0), (0, 0))
    return jnp.pad(first, widths[0]) + jnp.pad(second, widths[1])


def outer_terms(lower, seven):
    return outer_paired(jnp.where(lower, seven[: 3 * CY], seven[4 * CY :]))


def all_planes(lower, inside, part):
    part = (part + swapped(part))[:CTL]
    seven = pair_sum(lower, part, paired(part, 1))
    three = outer_terms(lower, seven)
    one = paired(jnp.where(lower, three[2 * CY :], three[:CY]), 1)
    low = jnp.concatenate([three, jnp.zeros((CY, 128), F32), one], 0) + seven[: 5 * CY]
    high = jnp.concatenate([one, jnp.zeros((CY, 128), F32), three], 0) + seven[2 * CY :]
    return inside * jnp.where(lower, low, high)


def local(moving, fixed):
    slab = lax.axis_index("gz").astype(jnp.int32)
    half = lax.axis_index("gy").astype(jnp.int32).reshape(1)
    parity = (slab % 2).reshape(1)
    lower = slab % 2 == 0
    at = slab * (2 * CY) - CY + lax.broadcasted_iota(jnp.int32, (CTL, 128), 0)
    inside = ((at >= 0) & (at < lax.axis_size("gz") * (2 * CY))).astype(F32)
    moving, half, parity, lower, inside = lax.optimization_barrier(
        (moving, half, parity, lower, inside)
    )
    front, back, xt = (jnp.asarray(a) for a in tables())

    inner, outer, y_rim = held(*rims_pass(half, parity, moving))
    inner = paired(inner, 1)
    outer = outer_paired(outer)
    y_rows = swapped(y_rim)

    grad, planes, z_edges, y_edges = interior_pass(half, moving, fixed)
    grad, part = edge_pass(
        half, parity, inner, outer, y_rows, z_edges, y_edges, back, xt, grad, planes
    )
    b_planes = all_planes(lower, inside, part)
    b = b_planes[CY : 3 * CY]
    part = hessian_pass(half, b_planes, b, grad, front, back, xt)
    u_planes = all_planes(lower, inside, part)
    u = u_planes[CY : 3 * CY]
    both = hessian_pass(half, u_planes, b, grad, front, back, xt)
    both = both + swapped(both)
    other = paired(both, 1)
    seven = pair_sum(lower, both[:CTL], other[:CTL])
    sums = both[CTL:] + other[CTL:]
    three = outer_terms(lower, seven)
    sums = stage(sums, 2, 4, 6)
    sums, three = lax.optimization_barrier((sums, three))
    sums = stage(stage(sums, 8), 16, 32, 48)
    v_low = seven[CY : 3 * CY] + three[CY:]
    v_high = seven[3 * CY : 5 * CY] + jnp.pad(three[:CY], ((CY, 0), (0, 0)))
    v = jnp.where(lower, v_low, v_high)

    bb, bu, uu, uv = (sums[j : j + 1] for j in range(4))
    a0 = bb / bu
    rr1 = bb - 2.0 * a0 * bu + a0 * a0 * uu
    beta = rr1 / bb
    more = 1.0 + beta
    a1 = rr1 / (more * more * bu - 2.0 * more * a0 * uu + a0 * a0 * uv)
    solution = a0 * b + a1 * (more * b - a0 * u)
    residual = (b - a0 * u) - a1 * (more * u - a0 * v)

    return tuple(placed(solution, residual))


def solution(mesh):
    in_specs = (P("gz", "gy", None), P("gz", "gy", None))
    out_specs = (P(None, "gz", None, None), P(None, "gz", None, None))
    return jax.shard_map(local, mesh=mesh, in_specs=in_specs, out_specs=out_specs, check_vma=False)
```

```python
import jax
import jax.numpy as jnp
import ml_dtypes
import numpy as np
from jax import lax
from jax.experimental import pallas as pl
from jax.experimental.pallas import tpu as pltpu
from jax.sharding import PartitionSpec as P

KNOT = 16
data_weight = 1.0 / 256.0
smooth_weight = 0.1

BF = jnp.bfloat16
F32 = jnp.float32
NZ, NY, NX = 32, 64, 512
ROWS = KNOT * NY
PLANES, CY, CX = 5, 8, 32
CTL = PLANES * CY
KPAD = 48
TILE = 16
WIDE = 128
EDGES = (0, 1, NZ - 2, NZ - 1)


def split(array):
    high = array.astype(ml_dtypes.bfloat16)
    low = (array - high.astype(np.float64)).astype(ml_dtypes.bfloat16)
    return high, low


def spline_weights():
    t = (np.arange(KNOT) + 0.5) / KNOT
    return np.stack(
        [
            (1 - t) ** 3 / 6,
            (3 * t**3 - 6 * t**2 + 4) / 6,
            (-3 * t**3 + 3 * t**2 + 3 * t + 1) / 6,
            t**3 / 6,
        ]
    )


def tables():
    weights = spline_weights()

    def along(blocks, first_block, points, first_point):
        out = np.zeros((blocks * KNOT, points))
        for block in range(blocks):
            for j in range(4):
                point = first_block + block + j - 1 - first_point
                if 0 <= point < points:
                    out[block * KNOT : (block + 1) * KNOT, point] = weights[j]
        return out

    along_z = along(NZ // KNOT, 0, PLANES, -1)
    halves = []
    for half in range(2):
        along_y = along(NY // KNOT, half * (NY // KNOT), CY, 0)
        halves.append(np.einsum("zp,yq->zypq", along_z, along_y).reshape(NZ * NY, CTL))
    high, low = split(np.stack(halves))
    widths = ((0, 0), (0, 0), (0, KPAD - CTL))
    high48, low48 = (np.pad(a, widths) for a in (high, low))
    out_table = np.concatenate([high48, low48, high48, low48], axis=2)
    backs = []
    for half in range(2):
        along_y = along(NY // KNOT, half * (NY // KNOT), CY, 0)
        backs.append(np.concatenate(split(np.kron(np.eye(PLANES), along_y).T), axis=0))
    back_table = np.stack(backs)
    along_x = along(NX // KNOT, 0, CX, 0)
    rows = np.zeros((128, 3 * NX))
    for c in range(3):
        rows[c * CX : (c + 1) * CX, c * NX : (c + 1) * NX] = along_x.T
    x_table = np.concatenate(split(rows), axis=0)
    return out_table, back_table, x_table


def halves_of(value):
    high = value.astype(BF)
    return high, (value - high.astype(F32)).astype(BF)


def block_terms(block, grad, weight_at, planes):
    weights = spline_weights()
    even = (weights[:2] + weights[:2, ::-1]) / 2
    odd = (weights[:2] - weights[:2, ::-1]) / 2

    def strip(y, carry):
        rows = pl.ds(pl.multiple_of(y * 8, 8), 8)
        for x in range(0, NX, WIDE):
            lanes = slice(x, x + WIDE)
            sums = [[[0.0, 0.0], [0.0, 0.0]] for _ in range(3)]
            for i in range(KNOT // 2):
                pair = []
                for z in (i, KNOT - 1 - i):
                    slopes = [grad[c, block * KNOT + z, rows, lanes] for c in range(3)]
                    weight, carry = weight_at(block * KNOT + z, y, lanes, slopes, carry)
                    pair.append([slope * weight for slope in slopes])
                for c in range(3):
                    both, apart = pair[0][c] + pair[1][c], pair[0][c] - pair[1][c]
                    for j in range(2):
                        sums[c][0][j] = sums[c][0][j] + float(even[j, i]) * both
                        sums[c][1][j] = sums[c][1][j] + float(odd[j, i]) * apart
            for c in range(3):
                (e0, e1), (o0, o1) = sums[c]
                at = slice(c * NX + x, c * NX + x + WIDE)
                for j, value in enumerate((e0 + o0, e1 + o1, e1 - o1, e0 - o0)):
                    if block == 0 or j == 3:
                        planes[block + j, rows, at] = value
                    else:
                        planes[block + j, rows, at] += value
        return carry

    return strip


def contracted(planes, back, x_table):
    high, low = halves_of(planes[...].reshape(PLANES * NY, 3 * NX))
    terms = jnp.dot(back, high, preferred_element_type=F32)
    rest = jnp.dot(back[:CTL], low, preferred_element_type=F32)
    high, low = halves_of(terms[:CTL] + (terms[CTL:] + rest))
    both = lax.dot_general(
        jnp.concatenate([high, low], 0),
        x_table[...],
        (((1,), (1,)), ((), ())),
        preferred_element_type=F32,
    )
    return both[:CTL, :128] + (both[:CTL, 128:] + both[CTL:, :128])


def interior_kernel(half, moving, fixed, grad, planes, z_edges, y_edges):
    lane = lax.broadcasted_iota(jnp.int32, (TILE, NX), 1)
    two = jnp.zeros((2, NX), F32)

    def plane(z, shifts):
        center = moving.at[z]
        for y in range(0, NY, TILE):
            here = slice(y, y + TILE)
            value = center[here]

            def at_z(k):
                return moving[z + k, here] if k in shifts else 0.0

            def at_y(k):
                first = y + k
                if first < 0:
                    return jnp.concatenate([two[: -first], center[0 : TILE + first]], 0)
                if first + TILE > NY:
                    return jnp.concatenate([center[first:NY], two[: first + TILE - NY]], 0)
                return center[first : first + TILE]

            def at_x(k):
                moved = pltpu.roll(value, (-k) % NX, 1)
                inside = lane < NX - k if k > 0 else lane >= -k
                return jnp.where(inside, moved, 0.0)

            for c, near in enumerate((at_z, at_y, at_x)):
                grad[c, z, here] = 8.0 * (near(1) - near(-1)) - (near(2) - near(-2))

    every = (-2, -1, 1, 2)

    def body(z, carry):
        plane(z, every)
        return carry

    plane(0, (1, 2))
    plane(1, (-1, 1, 2))
    lax.fori_loop(2, NZ - 2, body, 0, unroll=4)
    plane(NZ - 2, (-2, -1, 1))
    plane(NZ - 1, (-2, -1))

    def weight_at(z, y, lanes, slopes, carry):
        rows = pl.ds(pl.multiple_of(y * 8, 8), 8)
        return moving[z, rows, lanes] - fixed[z, rows, lanes], carry

    for block in range(NZ // KNOT):
        lax.fori_loop(0, NY // 8, block_terms(block, grad, weight_at, planes), 0, unroll=2)
    for e, z in enumerate(EDGES):
        z_edges[e] = moving[z] - fixed[z]
    rows = pl.ds(pl.multiple_of((1 - half[0]) * (NY - 8), 8), 8)
    y_edges[...] = moving[:, rows, :] - fixed[:, rows, :]


def edge_kernel(
    half, parity, inner, outer, y_rows, z_edges, y_edges, back, xt, grad_in, planes_in, grad, planes, out
):
    del grad_in, planes_in
    lower = parity[0] == 0
    weights = spline_weights()

    def strip(y, carry):
        rows = pl.ds(pl.multiple_of(y * 8, 8), 8)
        near, far = (jnp.where(lower, outer[z, rows], inner[z, rows]) for z in (1, 0))
        above, beyond = (jnp.where(lower, inner[z, rows], outer[z, rows]) for z in (0, 1))
        slopes = (far - 8.0 * near, near, -above, 8.0 * above - beyond)
        for e, z in enumerate(EDGES):
            grad[0, z, rows] += slopes[e]
            term = slopes[e] * z_edges[e, rows]
            for j in range(4):
                at = z // KNOT + j
                planes[at, rows, 0:NX] += float(weights[j, z % KNOT]) * term
        return carry

    lax.fori_loop(0, NY // 8, strip, 0)

    upper = half[0] == 0
    rows = pl.ds(pl.multiple_of((1 - half[0]) * (NY - 8), 8), 8)
    sub = lax.broadcasted_iota(jnp.int32, (8, NX), 0)

    def coefficient(when_upper, otherwise):
        def column(entries):
            value = jnp.zeros((8, NX), F32)
            for row, entry in entries.items():
                value = jnp.where(sub == row, entry, value)
            return value

        return jnp.where(upper, column(when_upper), column(otherwise))

    on_first = coefficient({6: -1.0, 7: 8.0}, {0: 1.0})
    on_second = coefficient({7: -1.0}, {0: -8.0, 1: 1.0})
    for block in range(NZ // KNOT):
        sums = [0.0] * 4
        for i in range(KNOT):
            z = block * KNOT + i
            slope = on_first * y_rows[z, 0:1] + on_second * y_rows[z, 1:2]
            grad[1, z, rows] += slope
            term = slope * y_edges[z]
            sums = [total + float(weights[j, i]) * term for j, total in enumerate(sums)]
        for j, total in enumerate(sums):
            planes[block + j, rows, NX : 2 * NX] += total
    out[...] = contracted(planes, back[half[0]], xt) * (-data_weight / 12.0)


def hessian_kernel(half, ctl, base, grad, front, back, xt, out, spread, field, planes):
    high, low = halves_of(ctl[...])
    first, second = xt[:128], xt[128:]
    value = jnp.dot(jnp.concatenate([high, low], 0), first, preferred_element_type=F32)
    value = value[:CTL] + (value[CTL:] + jnp.dot(high, second, preferred_element_type=F32))
    value = jnp.concatenate([value, jnp.zeros((KPAD - CTL, 3 * NX), F32)], 0)
    high, low = halves_of(value)
    for j, part in enumerate((high, high, low, low)):
        spread[j * KPAD : (j + 1) * KPAD] = part
    square = jnp.zeros((8, WIDE), F32)

    for block in range(NZ // KNOT):
        at_rows = slice(block * ROWS, (block + 1) * ROWS)
        field[...] = jnp.dot(front[half[0], at_rows], spread[...], preferred_element_type=F32)

        def weight_at(z, y, lanes, slopes, carry):
            rows = pl.ds(pl.multiple_of(z % KNOT * NY + y * 8, 8), 8)
            weight = 0.0
            for c in range(3):
                at = slice(c * NX + lanes.start, c * NX + lanes.stop)
                weight = weight + slopes[c] * field[rows, at]
            return weight, carry + weight * weight

        strip = block_terms(block, grad, weight_at, planes)
        square = lax.fori_loop(0, NY // 8, strip, square, unroll=True)

    scale = data_weight / 144.0
    whole = ctl[...]
    owned = whole[CY : 3 * CY]
    sub = lax.broadcasted_iota(jnp.int32, (2 * CY, 128), 0) % CY
    lane = lax.broadcasted_iota(jnp.int32, (2 * CY, 128), 1) % CX
    near = whole[0 : 2 * CY] + whole[2 * CY : 4 * CY]
    near += jnp.where(sub > 0, pltpu.roll(owned, 1, 0), 0.0)
    near += jnp.where(sub < CY - 1, pltpu.roll(owned, 2 * CY - 1, 0), 0.0)
    near += jnp.where(lane > 0, pltpu.roll(owned, 1, 1), 0.0)
    near += jnp.where(lane < CX - 1, pltpu.roll(owned, 127, 1), 0.0)
    smooth = (0.5 * smooth_weight) * (6.0 * owned - near)
    out[:CTL] = contracted(planes, back[half[0]], xt) * scale
    out[CY : 3 * CY] += smooth
    first = base[...]

    def total(value):
        return jnp.sum(jnp.sum(value, axis=0, keepdims=True), axis=1, keepdims=True)

    whole_square = total(square) * scale + total(smooth * owned)
    lines = [
        0.5 * total(first * first),
        0.5 * total(first * owned),
        0.5 * total(owned * owned),
        whole_square,
    ]
    which = lax.broadcasted_iota(jnp.int32, (8, 128), 0)
    tile = jnp.zeros((8, 128), F32)
    for j, line in enumerate(lines):
        tile = jnp.where(which == j, line, tile)
    out[CTL:] = tile


VMEM_SPEC = pl.BlockSpec(memory_space=pltpu.VMEM)
HBM_SPEC = pl.BlockSpec(memory_space=pltpu.HBM)
SMEM_SPEC = pl.BlockSpec(memory_space=pltpu.SMEM)
PARAMS = pltpu.CompilerParams(vmem_limit_bytes=24 * 1024 * 1024)
RIMS_MIB = 52
SMALL_PARAMS = pltpu.CompilerParams(vmem_limit_bytes=8 * 1024 * 1024)


GRAD_SHAPE = jax.ShapeDtypeStruct((3, NZ, NY, NX), F32)
PLANES_SHAPE = jax.ShapeDtypeStruct((PLANES, NY, 3 * NX), F32)
CTL_SHAPE = jax.ShapeDtypeStruct((CTL, 128), F32)


def interior_pass(half, moving, fixed):
    return pl.pallas_call(
        interior_kernel,
        in_specs=[SMEM_SPEC] + [VMEM_SPEC] * 2,
        out_specs=[VMEM_SPEC] * 4,
        out_shape=[
            GRAD_SHAPE,
            PLANES_SHAPE,
            jax.ShapeDtypeStruct((len(EDGES), NY, NX), F32),
            jax.ShapeDtypeStruct((NZ, 8, NX), F32),
        ],
        compiler_params=SMALL_PARAMS,
        cost_estimate=pl.CostEstimate(flops=100_000_000, bytes_accessed=40_000_000, transcendentals=0),
        name="interior",
    )(half, moving, fixed)


def edge_pass(half, parity, inner, outer, y_rows, z_edges, y_edges, back_table, x_table, grad, planes):
    grad, _, part = pl.pallas_call(
        edge_kernel,
        in_specs=[SMEM_SPEC] * 2 + [VMEM_SPEC] * 9,
        out_specs=[VMEM_SPEC] * 3,
        out_shape=[GRAD_SHAPE, PLANES_SHAPE, CTL_SHAPE],
        input_output_aliases={9: 0, 10: 1},
        compiler_params=PARAMS,
        name="edge",
    )(half, parity, inner, outer, y_rows, z_edges, y_edges, back_table, x_table, grad, planes)
    return grad, part


def hessian_pass(half, ctl, base, grad, front_table, back_table, x_table):
    return pl.pallas_call(
        hessian_kernel,
        in_specs=[SMEM_SPEC] + [VMEM_SPEC] * 6,
        out_specs=VMEM_SPEC,
        scratch_shapes=[
            pltpu.VMEM((4 * KPAD, 3 * NX), BF),
            pltpu.VMEM((ROWS, 3 * NX), F32),
            pltpu.VMEM((PLANES, NY, 3 * NX), F32),
        ],
        out_shape=jax.ShapeDtypeStruct((CTL + 8, 128), F32),
        compiler_params=PARAMS,
        name="hessian",
    )(half, ctl, base, grad, front_table, back_table, x_table)


def rims_kernel(half, parity, moving, inner, outer, y_rim, tile, sems):
    half, parity = half[0], parity[0]
    top, bottom = NZ - 2, 0
    copies = [
        pltpu.make_async_copy(
            moving.at[pl.ds(jnp.where(parity == 0, top, bottom), 2)], inner, sems.at[0]
        ),
        pltpu.make_async_copy(
            moving.at[pl.ds(jnp.where(parity == 0, bottom, top), 2)], outer, sems.at[1]
        ),
        pltpu.make_async_copy(
            moving.at[:, pl.ds(pl.multiple_of((1 - half) * (NY - 8), 8), 8)], tile, sems.at[2]
        ),
    ]
    for copy in copies:
        copy.start()
    for copy in copies:
        copy.wait()
    y_rim[...] = jnp.where(half == 0, tile[:, 6:8, :], tile[:, 0:2, :])


def rims_pass(half, parity, moving):
    return pl.pallas_call(
        rims_kernel,
        in_specs=[SMEM_SPEC, SMEM_SPEC, HBM_SPEC],
        out_specs=[VMEM_SPEC] * 3,
        out_shape=[jax.ShapeDtypeStruct(shape, F32) for shape in ((2, NY, NX), (2, NY, NX), (NZ, 2, NX))],
        scratch_shapes=[pltpu.VMEM((NZ, 8, NX), F32), pltpu.SemaphoreType.DMA((3,))],
        compiler_params=pltpu.CompilerParams(vmem_limit_bytes=RIMS_MIB * 1024 * 1024),
        name="rims",
    )(half, parity, moving)


def held_kernel(*refs):
    for source, target in zip(refs[: len(refs) // 2], refs[len(refs) // 2 :]):
        target[...] = source[...]


def held(*rims):
    return pl.pallas_call(
        held_kernel,
        in_specs=[VMEM_SPEC] * len(rims),
        out_specs=[VMEM_SPEC] * len(rims),
        out_shape=[jax.ShapeDtypeStruct(rim.shape, F32) for rim in rims],
        compiler_params=SMALL_PARAMS,
        cost_estimate=pl.CostEstimate(flops=20_000_000_000, bytes_accessed=60_000_000, transcendentals=0),
        name="held",
    )(*rims)


def placed_kernel(solution, residual, solution_out, residual_out):
    for value, out in ((solution[...], solution_out), (residual[...], residual_out)):
        for c in range(3):
            moved = pltpu.roll(value, (-c * CX) % 128, 1) if c else value
            for plane in range(2):
                out[c, plane] = moved[plane * CY : (plane + 1) * CY, :CX]


def placed(solution, residual):
    return pl.pallas_call(
        placed_kernel,
        in_specs=[VMEM_SPEC] * 2,
        out_specs=[VMEM_SPEC] * 2,
        out_shape=[jax.ShapeDtypeStruct((3, 2, CY, CX), F32)] * 2,
        compiler_params=SMALL_PARAMS,
        name="placed",
    )(solution, residual)


def swapped(value):
    return lax.ppermute(value, "gy", [(0, 1), (1, 0)])


def paired(value, mask):
    count = lax.axis_size("gz")
    return lax.ppermute(value, "gz", [(i, i ^ mask) for i in range(count)])


def stage(value, *masks):
    return value + sum(paired(value, mask) for mask in masks)


def outer_paired(value):
    count = lax.axis_size("gz")
    pairs = [(i, i + 1) for i in range(1, count - 1, 2)]
    return lax.ppermute(value, "gz", pairs + [(j, i) for i, j in pairs])


def pair_sum(lower, own, other):
    first, second = jnp.where(lower, own, other), jnp.where(lower, other, own)
    widths = ((0, 2 * CY), (0, 0)), ((2 * CY, 0), (0, 0))
    return jnp.pad(first, widths[0]) + jnp.pad(second, widths[1])


def outer_terms(lower, seven):
    return outer_paired(jnp.where(lower, seven[: 3 * CY], seven[4 * CY :]))


def all_planes(lower, inside, part):
    part = (part + swapped(part))[:CTL]
    seven = pair_sum(lower, part, paired(part, 1))
    three = outer_terms(lower, seven)
    one = paired(jnp.where(lower, three[2 * CY :], three[:CY]), 1)
    low = jnp.concatenate([three, jnp.zeros((CY, 128), F32), one], 0) + seven[: 5 * CY]
    high = jnp.concatenate([one, jnp.zeros((CY, 128), F32), three], 0) + seven[2 * CY :]
    return inside * jnp.where(lower, low, high)


def local(moving, fixed):
    slab = lax.axis_index("gz").astype(jnp.int32)
    half = lax.axis_index("gy").astype(jnp.int32).reshape(1)
    parity = (slab % 2).reshape(1)
    lower = slab % 2 == 0
    at = slab * (2 * CY) - CY + lax.broadcasted_iota(jnp.int32, (CTL, 128), 0)
    inside = ((at >= 0) & (at < lax.axis_size("gz") * (2 * CY))).astype(F32)
    moving, half, parity, lower, inside = lax.optimization_barrier(
        (moving, half, parity, lower, inside)
    )
    front, back, xt = (jnp.asarray(a) for a in tables())

    inner, outer, y_rim = held(*rims_pass(half, parity, moving))
    inner = paired(inner, 1)
    outer = outer_paired(outer)
    y_rows = swapped(y_rim)

    grad, planes, z_edges, y_edges = interior_pass(half, moving, fixed)
    grad, part = edge_pass(
        half, parity, inner, outer, y_rows, z_edges, y_edges, back, xt, grad, planes
    )
    b_planes = all_planes(lower, inside, part)
    b = b_planes[CY : 3 * CY]
    part = hessian_pass(half, b_planes, b, grad, front, back, xt)
    u_planes = all_planes(lower, inside, part)
    u = u_planes[CY : 3 * CY]
    both = hessian_pass(half, u_planes, b, grad, front, back, xt)
    both = both + swapped(both)
    other = paired(both, 1)
    seven = pair_sum(lower, both[:CTL], other[:CTL])
    sums = both[CTL:] + other[CTL:]
    three = outer_terms(lower, seven)
    sums = stage(sums, 2, 4, 6)
    sums, three = lax.optimization_barrier((sums, three))
    sums = stage(stage(sums, 8), 16, 32, 48)
    v_low = seven[CY : 3 * CY] + three[CY:]
    v_high = seven[3 * CY : 5 * CY] + jnp.pad(three[:CY], ((CY, 0), (0, 0)))
    v = jnp.where(lower, v_low, v_high)

    bb, bu, uu, uv = (sums[j : j + 1] for j in range(4))
    a0 = bb / bu
    rr1 = bb - 2.0 * a0 * bu + a0 * a0 * uu
    beta = rr1 / bb
    more = 1.0 + beta
    a1 = rr1 / (more * more * bu - 2.0 * more * a0 * uu + a0 * a0 * uv)
    solution = a0 * b + a1 * (more * b - a0 * u)
    residual = (b - a0 * u) - a1 * (more * u - a0 * v)

    return tuple(placed(solution, residual))


def solution(mesh):
    in_specs = (P("gz", "gy", None), P("gz", "gy", None))
    out_specs = (P(None, "gz", None, None), P(None, "gz", None, None))
    return jax.shard_map(local, mesh=mesh, in_specs=in_specs, out_specs=out_specs, check_vma=False)
```

```python
import jax
import jax.numpy as jnp
import ml_dtypes
import numpy as np
from jax import lax
from jax.experimental import pallas as pl
from jax.experimental.pallas import tpu as pltpu
from jax.sharding import PartitionSpec as P

KNOT = 16
data_weight = 1.0 / 256.0
smooth_weight = 0.1

BF = jnp.bfloat16
F32 = jnp.float32
NZ, NY, NX = 32, 64, 512
ROWS = KNOT * NY
PLANES, CY, CX = 5, 8, 32
CTL = PLANES * CY
KPAD = 48
TILE = 16
WIDE = 128
EDGES = (0, 1, NZ - 2, NZ - 1)


def split(array):
    high = array.astype(ml_dtypes.bfloat16)
    low = (array - high.astype(np.float64)).astype(ml_dtypes.bfloat16)
    return high, low


def spline_weights():
    t = (np.arange(KNOT) + 0.5) / KNOT
    return np.stack(
        [
            (1 - t) ** 3 / 6,
            (3 * t**3 - 6 * t**2 + 4) / 6,
            (-3 * t**3 + 3 * t**2 + 3 * t + 1) / 6,
            t**3 / 6,
        ]
    )


def tables():
    weights = spline_weights()

    def along(blocks, first_block, points, first_point):
        out = np.zeros((blocks * KNOT, points))
        for block in range(blocks):
            for j in range(4):
                point = first_block + block + j - 1 - first_point
                if 0 <= point < points:
                    out[block * KNOT : (block + 1) * KNOT, point] = weights[j]
        return out

    along_z = along(NZ // KNOT, 0, PLANES, -1)
    halves = []
    for half in range(2):
        along_y = along(NY // KNOT, half * (NY // KNOT), CY, 0)
        halves.append(np.einsum("zp,yq->zypq", along_z, along_y).reshape(NZ * NY, CTL))
    high, low = split(np.stack(halves))
    widths = ((0, 0), (0, 0), (0, KPAD - CTL))
    high48, low48 = (np.pad(a, widths) for a in (high, low))
    out_table = np.concatenate([high48, low48, high48, low48], axis=2)
    backs = []
    for half in range(2):
        along_y = along(NY // KNOT, half * (NY // KNOT), CY, 0)
        backs.append(np.concatenate(split(np.kron(np.eye(PLANES), along_y).T), axis=0))
    back_table = np.stack(backs)
    along_x = along(NX // KNOT, 0, CX, 0)
    rows = np.zeros((128, 3 * NX))
    for c in range(3):
        rows[c * CX : (c + 1) * CX, c * NX : (c + 1) * NX] = along_x.T
    x_table = np.concatenate(split(rows), axis=0)
    return out_table, back_table, x_table


def halves_of(value):
    high = value.astype(BF)
    return high, (value - high.astype(F32)).astype(BF)


def block_terms(block, grad, weight_at, planes):
    weights = spline_weights()
    even = (weights[:2] + weights[:2, ::-1]) / 2
    odd = (weights[:2] - weights[:2, ::-1]) / 2

    def strip(y, carry):
        rows = pl.ds(pl.multiple_of(y * 8, 8), 8)
        for x in range(0, NX, WIDE):
            lanes = slice(x, x + WIDE)
            sums = [[[0.0, 0.0], [0.0, 0.0]] for _ in range(3)]
            for i in range(KNOT // 2):
                pair = []
                for z in (i, KNOT - 1 - i):
                    slopes = [grad[c, block * KNOT + z, rows, lanes] for c in range(3)]
                    weight, carry = weight_at(block * KNOT + z, y, lanes, slopes, carry)
                    pair.append([slope * weight for slope in slopes])
                for c in range(3):
                    both, apart = pair[0][c] + pair[1][c], pair[0][c] - pair[1][c]
                    for j in range(2):
                        sums[c][0][j] = sums[c][0][j] + float(even[j, i]) * both
                        sums[c][1][j] = sums[c][1][j] + float(odd[j, i]) * apart
            for c in range(3):
                (e0, e1), (o0, o1) = sums[c]
                at = slice(c * NX + x, c * NX + x + WIDE)
                for j, value in enumerate((e0 + o0, e1 + o1, e1 - o1, e0 - o0)):
                    if block == 0 or j == 3:
                        planes[block + j, rows, at] = value
                    else:
                        planes[block + j, rows, at] += value
        return carry

    return strip


def contracted(planes, back, x_table):
    high, low = halves_of(planes[...].reshape(PLANES * NY, 3 * NX))
    terms = jnp.dot(back, high, preferred_element_type=F32)
    rest = jnp.dot(back[:CTL], low, preferred_element_type=F32)
    high, low = halves_of(terms[:CTL] + (terms[CTL:] + rest))
    both = lax.dot_general(
        jnp.concatenate([high, low], 0),
        x_table[...],
        (((1,), (1,)), ((), ())),
        preferred_element_type=F32,
    )
    return both[:CTL, :128] + (both[:CTL, 128:] + both[CTL:, :128])


def interior_kernel(half, moving, fixed, grad, planes, z_edges, y_edges):
    lane = lax.broadcasted_iota(jnp.int32, (TILE, NX), 1)
    two = jnp.zeros((2, NX), F32)

    def plane(z, shifts):
        center = moving.at[z]
        for y in range(0, NY, TILE):
            here = slice(y, y + TILE)
            value = center[here]

            def at_z(k):
                return moving[z + k, here] if k in shifts else 0.0

            def at_y(k):
                first = y + k
                if first < 0:
                    return jnp.concatenate([two[: -first], center[0 : TILE + first]], 0)
                if first + TILE > NY:
                    return jnp.concatenate([center[first:NY], two[: first + TILE - NY]], 0)
                return center[first : first + TILE]

            def at_x(k):
                moved = pltpu.roll(value, (-k) % NX, 1)
                inside = lane < NX - k if k > 0 else lane >= -k
                return jnp.where(inside, moved, 0.0)

            for c, near in enumerate((at_z, at_y, at_x)):
                grad[c, z, here] = 8.0 * (near(1) - near(-1)) - (near(2) - near(-2))

    every = (-2, -1, 1, 2)

    def body(z, carry):
        plane(z, every)
        return carry

    plane(0, (1, 2))
    plane(1, (-1, 1, 2))
    lax.fori_loop(2, NZ - 2, body, 0, unroll=2)
    plane(NZ - 2, (-2, -1, 1))
    plane(NZ - 1, (-2, -1))

    def weight_at(z, y, lanes, slopes, carry):
        rows = pl.ds(pl.multiple_of(y * 8, 8), 8)
        return moving[z, rows, lanes] - fixed[z, rows, lanes], carry

    for block in range(NZ // KNOT):
        lax.fori_loop(0, NY // 8, block_terms(block, grad, weight_at, planes), 0, unroll=2)
    for e, z in enumerate(EDGES):
        z_edges[e] = moving[z] - fixed[z]
    rows = pl.ds(pl.multiple_of((1 - half[0]) * (NY - 8), 8), 8)
    y_edges[...] = moving[:, rows, :] - fixed[:, rows, :]


def edge_kernel(
    half, parity, inner, outer, y_rows, z_edges, y_edges, back, xt, grad_in, planes_in, grad, planes, out
):
    del grad_in, planes_in
    lower = parity[0] == 0
    weights = spline_weights()

    def strip(y, carry):
        rows = pl.ds(pl.multiple_of(y * 8, 8), 8)
        near, far = (jnp.where(lower, outer[z, rows], inner[z, rows]) for z in (1, 0))
        above, beyond = (jnp.where(lower, inner[z, rows], outer[z, rows]) for z in (0, 1))
        slopes = (far - 8.0 * near, near, -above, 8.0 * above - beyond)
        for e, z in enumerate(EDGES):
            grad[0, z, rows] += slopes[e]
            term = slopes[e] * z_edges[e, rows]
            for j in range(4):
                at = z // KNOT + j
                planes[at, rows, 0:NX] += float(weights[j, z % KNOT]) * term
        return carry

    lax.fori_loop(0, NY // 8, strip, 0)

    upper = half[0] == 0
    rows = pl.ds(pl.multiple_of((1 - half[0]) * (NY - 8), 8), 8)
    sub = lax.broadcasted_iota(jnp.int32, (8, NX), 0)

    def coefficient(when_upper, otherwise):
        def column(entries):
            value = jnp.zeros((8, NX), F32)
            for row, entry in entries.items():
                value = jnp.where(sub == row, entry, value)
            return value

        return jnp.where(upper, column(when_upper), column(otherwise))

    on_first = coefficient({6: -1.0, 7: 8.0}, {0: 1.0})
    on_second = coefficient({7: -1.0}, {0: -8.0, 1: 1.0})
    for block in range(NZ // KNOT):
        sums = [0.0] * 4
        for i in range(KNOT):
            z = block * KNOT + i
            slope = on_first * y_rows[z, 0:1] + on_second * y_rows[z, 1:2]
            grad[1, z, rows] += slope
            term = slope * y_edges[z]
            sums = [total + float(weights[j, i]) * term for j, total in enumerate(sums)]
        for j, total in enumerate(sums):
            planes[block + j, rows, NX : 2 * NX] += total
    out[...] = contracted(planes, back[half[0]], xt) * (-data_weight / 12.0)


def hessian_kernel(half, ctl, base, grad, front, back, xt, out, spread, field, planes):
    high, low = halves_of(ctl[...])
    first, second = xt[:128], xt[128:]
    value = jnp.dot(high, first, preferred_element_type=F32)
    value += jnp.dot(low, first, preferred_element_type=F32)
    value += jnp.dot(high, second, preferred_element_type=F32)
    value = jnp.concatenate([value, jnp.zeros((KPAD - CTL, 3 * NX), F32)], 0)
    high, low = halves_of(value)
    for j, part in enumerate((high, high, low, low)):
        spread[j * KPAD : (j + 1) * KPAD] = part
    square = jnp.zeros((8, WIDE), F32)

    for block in range(NZ // KNOT):
        at_rows = slice(block * ROWS, (block + 1) * ROWS)
        field[...] = jnp.dot(front[half[0], at_rows], spread[...], preferred_element_type=F32)

        def weight_at(z, y, lanes, slopes, carry):
            rows = pl.ds(pl.multiple_of(z % KNOT * NY + y * 8, 8), 8)
            weight = 0.0
            for c in range(3):
                at = slice(c * NX + lanes.start, c * NX + lanes.stop)
                weight = weight + slopes[c] * field[rows, at]
            return weight, carry + weight * weight

        strip = block_terms(block, grad, weight_at, planes)
        square = lax.fori_loop(0, NY // 8, strip, square, unroll=2)

    scale = data_weight / 144.0
    whole = ctl[...]
    owned = whole[CY : 3 * CY]
    sub = lax.broadcasted_iota(jnp.int32, (2 * CY, 128), 0) % CY
    lane = lax.broadcasted_iota(jnp.int32, (2 * CY, 128), 1) % CX
    near = whole[0 : 2 * CY] + whole[2 * CY : 4 * CY]
    near += jnp.where(sub > 0, pltpu.roll(owned, 1, 0), 0.0)
    near += jnp.where(sub < CY - 1, pltpu.roll(owned, 2 * CY - 1, 0), 0.0)
    near += jnp.where(lane > 0, pltpu.roll(owned, 1, 1), 0.0)
    near += jnp.where(lane < CX - 1, pltpu.roll(owned, 127, 1), 0.0)
    smooth = (0.5 * smooth_weight) * (6.0 * owned - near)
    out[:CTL] = contracted(planes, back[half[0]], xt) * scale
    out[CY : 3 * CY] += smooth
    first = base[...]

    def total(value):
        return jnp.sum(jnp.sum(value, axis=0, keepdims=True), axis=1, keepdims=True)

    whole_square = total(square) * scale + total(smooth * owned)
    lines = [
        0.5 * total(first * first),
        0.5 * total(first * owned),
        0.5 * total(owned * owned),
        whole_square,
    ]
    which = lax.broadcasted_iota(jnp.int32, (8, 128), 0)
    tile = jnp.zeros((8, 128), F32)
    for j, line in enumerate(lines):
        tile = jnp.where(which == j, line, tile)
    out[CTL:] = tile


VMEM_SPEC = pl.BlockSpec(memory_space=pltpu.VMEM)
HBM_SPEC = pl.BlockSpec(memory_space=pltpu.HBM)
SMEM_SPEC = pl.BlockSpec(memory_space=pltpu.SMEM)
PARAMS = pltpu.CompilerParams(vmem_limit_bytes=24 * 1024 * 1024)
RIMS_MIB = 52
SMALL_PARAMS = pltpu.CompilerParams(vmem_limit_bytes=8 * 1024 * 1024)


GRAD_SHAPE = jax.ShapeDtypeStruct((3, NZ, NY, NX), F32)
PLANES_SHAPE = jax.ShapeDtypeStruct((PLANES, NY, 3 * NX), F32)
CTL_SHAPE = jax.ShapeDtypeStruct((CTL, 128), F32)


def interior_pass(half, moving, fixed):
    return pl.pallas_call(
        interior_kernel,
        in_specs=[SMEM_SPEC] + [VMEM_SPEC] * 2,
        out_specs=[VMEM_SPEC] * 4,
        out_shape=[
            GRAD_SHAPE,
            PLANES_SHAPE,
            jax.ShapeDtypeStruct((len(EDGES), NY, NX), F32),
            jax.ShapeDtypeStruct((NZ, 8, NX), F32),
        ],
        compiler_params=SMALL_PARAMS,
        cost_estimate=pl.CostEstimate(flops=100_000_000, bytes_accessed=40_000_000, transcendentals=0),
        name="interior",
    )(half, moving, fixed)


def edge_pass(half, parity, inner, outer, y_rows, z_edges, y_edges, back_table, x_table, grad, planes):
    grad, _, part = pl.pallas_call(
        edge_kernel,
        in_specs=[SMEM_SPEC] * 2 + [VMEM_SPEC] * 9,
        out_specs=[VMEM_SPEC] * 3,
        out_shape=[GRAD_SHAPE, PLANES_SHAPE, CTL_SHAPE],
        input_output_aliases={9: 0, 10: 1},
        compiler_params=PARAMS,
        name="edge",
    )(half, parity, inner, outer, y_rows, z_edges, y_edges, back_table, x_table, grad, planes)
    return grad, part


def hessian_pass(half, ctl, base, grad, front_table, back_table, x_table):
    return pl.pallas_call(
        hessian_kernel,
        in_specs=[SMEM_SPEC] + [VMEM_SPEC] * 6,
        out_specs=VMEM_SPEC,
        scratch_shapes=[
            pltpu.VMEM((4 * KPAD, 3 * NX), BF),
            pltpu.VMEM((ROWS, 3 * NX), F32),
            pltpu.VMEM((PLANES, NY, 3 * NX), F32),
        ],
        out_shape=jax.ShapeDtypeStruct((CTL + 8, 128), F32),
        compiler_params=PARAMS,
        name="hessian",
    )(half, ctl, base, grad, front_table, back_table, x_table)


def rims_kernel(half, parity, moving, inner, outer, y_rim, tile, sems):
    half, parity = half[0], parity[0]
    top, bottom = NZ - 2, 0
    copies = [
        pltpu.make_async_copy(
            moving.at[pl.ds(jnp.where(parity == 0, top, bottom), 2)], inner, sems.at[0]
        ),
        pltpu.make_async_copy(
            moving.at[pl.ds(jnp.where(parity == 0, bottom, top), 2)], outer, sems.at[1]
        ),
        pltpu.make_async_copy(
            moving.at[:, pl.ds(pl.multiple_of((1 - half) * (NY - 8), 8), 8)], tile, sems.at[2]
        ),
    ]
    for copy in copies:
        copy.start()
    for copy in copies:
        copy.wait()
    y_rim[...] = jnp.where(half == 0, tile[:, 6:8, :], tile[:, 0:2, :])


def rims_pass(half, parity, moving):
    return pl.pallas_call(
        rims_kernel,
        in_specs=[SMEM_SPEC, SMEM_SPEC, HBM_SPEC],
        out_specs=[VMEM_SPEC] * 3,
        out_shape=[jax.ShapeDtypeStruct(shape, F32) for shape in ((2, NY, NX), (2, NY, NX), (NZ, 2, NX))],
        scratch_shapes=[pltpu.VMEM((NZ, 8, NX), F32), pltpu.SemaphoreType.DMA((3,))],
        compiler_params=pltpu.CompilerParams(vmem_limit_bytes=RIMS_MIB * 1024 * 1024),
        name="rims",
    )(half, parity, moving)


def held_kernel(*refs):
    for source, target in zip(refs[: len(refs) // 2], refs[len(refs) // 2 :]):
        target[...] = source[...]


def held(*rims):
    return pl.pallas_call(
        held_kernel,
        in_specs=[VMEM_SPEC] * len(rims),
        out_specs=[VMEM_SPEC] * len(rims),
        out_shape=[jax.ShapeDtypeStruct(rim.shape, F32) for rim in rims],
        compiler_params=SMALL_PARAMS,
        cost_estimate=pl.CostEstimate(flops=20_000_000_000, bytes_accessed=60_000_000, transcendentals=0),
        name="held",
    )(*rims)


def placed_kernel(solution, residual, solution_out, residual_out):
    for value, out in ((solution[...], solution_out), (residual[...], residual_out)):
        for c in range(3):
            moved = pltpu.roll(value, (-c * CX) % 128, 1) if c else value
            for plane in range(2):
                out[c, plane] = moved[plane * CY : (plane + 1) * CY, :CX]


def placed(solution, residual):
    return pl.pallas_call(
        placed_kernel,
        in_specs=[VMEM_SPEC] * 2,
        out_specs=[VMEM_SPEC] * 2,
        out_shape=[jax.ShapeDtypeStruct((3, 2, CY, CX), F32)] * 2,
        compiler_params=SMALL_PARAMS,
        name="placed",
    )(solution, residual)


def swapped(value):
    return lax.ppermute(value, "gy", [(0, 1), (1, 0)])


def paired(value, mask):
    count = lax.axis_size("gz")
    return lax.ppermute(value, "gz", [(i, i ^ mask) for i in range(count)])


def stage(value, *masks):
    return value + sum(paired(value, mask) for mask in masks)


def outer_paired(value):
    count = lax.axis_size("gz")
    pairs = [(i, i + 1) for i in range(1, count - 1, 2)]
    return lax.ppermute(value, "gz", pairs + [(j, i) for i, j in pairs])


def far_paired(value):
    count = lax.axis_size("gz")
    pairs = [(i, i + 3) for i in range(0, count - 3, 2)]
    return lax.ppermute(value, "gz", pairs + [(j, i) for i, j in pairs])


def pair_sum(lower, own, other):
    first, second = jnp.where(lower, own, other), jnp.where(lower, other, own)
    widths = ((0, 2 * CY), (0, 0)), ((2 * CY, 0), (0, 0))
    return jnp.pad(first, widths[0]) + jnp.pad(second, widths[1])


def outer_terms(lower, seven):
    return outer_paired(jnp.where(lower, seven[: 3 * CY], seven[4 * CY :]))


def all_planes(lower, inside, part):
    part = (part + swapped(part))[:CTL]
    seven = pair_sum(lower, part, paired(part, 1))
    three = outer_terms(lower, seven)
    one = far_paired(jnp.where(lower, seven[6 * CY :], seven[:CY]))
    low = jnp.concatenate([three, jnp.zeros((CY, 128), F32), one], 0) + seven[: 5 * CY]
    high = jnp.concatenate([one, jnp.zeros((CY, 128), F32), three], 0) + seven[2 * CY :]
    return inside * jnp.where(lower, low, high)


def local(moving, fixed):
    slab = lax.axis_index("gz").astype(jnp.int32)
    half = lax.axis_index("gy").astype(jnp.int32).reshape(1)
    parity = (slab % 2).reshape(1)
    lower = slab % 2 == 0
    at = slab * (2 * CY) - CY + lax.broadcasted_iota(jnp.int32, (CTL, 128), 0)
    inside = ((at >= 0) & (at < lax.axis_size("gz") * (2 * CY))).astype(F32)
    moving, half, parity, lower, inside = lax.optimization_barrier(
        (moving, half, parity, lower, inside)
    )
    front, back, xt = (jnp.asarray(a) for a in tables())

    inner, outer, y_rim = held(*rims_pass(half, parity, moving))
    inner = paired(inner, 1)
    outer = outer_paired(outer)
    y_rows = swapped(y_rim)

    grad, planes, z_edges, y_edges = interior_pass(half, moving, fixed)
    grad, part = edge_pass(
        half, parity, inner, outer, y_rows, z_edges, y_edges, back, xt, grad, planes
    )
    b_planes = all_planes(lower, inside, part)
    b = b_planes[CY : 3 * CY]
    part = hessian_pass(half, b_planes, b, grad, front, back, xt)
    u_planes = all_planes(lower, inside, part)
    u = u_planes[CY : 3 * CY]
    both = hessian_pass(half, u_planes, b, grad, front, back, xt)
    both = both + swapped(both)
    other = paired(both, 1)
    seven = pair_sum(lower, both[:CTL], other[:CTL])
    sums = both[CTL:] + other[CTL:]
    three = outer_terms(lower, seven)
    sums = stage(sums, 2, 4, 6)
    sums, three = lax.optimization_barrier((sums, three))
    sums = stage(stage(sums, 8), 16, 32, 48)
    v_low = seven[CY : 3 * CY] + three[CY:]
    v_high = seven[3 * CY : 5 * CY] + jnp.pad(three[:CY], ((CY, 0), (0, 0)))
    v = jnp.where(lower, v_low, v_high)

    bb, bu, uu, uv = (sums[j : j + 1] for j in range(4))
    a0 = bb / bu
    rr1 = bb - 2.0 * a0 * bu + a0 * a0 * uu
    beta = rr1 / bb
    more = 1.0 + beta
    a1 = rr1 / (more * more * bu - 2.0 * more * a0 * uu + a0 * a0 * uv)
    solution = a0 * b + a1 * (more * b - a0 * u)
    residual = (b - a0 * u) - a1 * (more * u - a0 * v)

    return tuple(placed(solution, residual))


def solution(mesh):
    in_specs = (P("gz", "gy", None), P("gz", "gy", None))
    out_specs = (P(None, "gz", None, None), P(None, "gz", None, None))
    return jax.shard_map(local, mesh=mesh, in_specs=in_specs, out_specs=out_specs, check_vma=False)
```

```python
import jax
import jax.numpy as jnp
import ml_dtypes
import numpy as np
from jax import lax
from jax.experimental import pallas as pl
from jax.experimental.pallas import tpu as pltpu
from jax.sharding import PartitionSpec as P

KNOT = 16
data_weight = 1.0 / 256.0
smooth_weight = 0.1

BF = jnp.bfloat16
F32 = jnp.float32
NZ, NY, NX = 32, 64, 512
ROWS = KNOT * NY
PLANES, CY, CX = 5, 8, 32
CTL = PLANES * CY
KPAD = 48
TILE = 16
WIDE = 128
EDGES = (0, 1, NZ - 2, NZ - 1)


def split(array):
    high = array.astype(ml_dtypes.bfloat16)
    low = (array - high.astype(np.float64)).astype(ml_dtypes.bfloat16)
    return high, low


def spline_weights():
    t = (np.arange(KNOT) + 0.5) / KNOT
    return np.stack(
        [
            (1 - t) ** 3 / 6,
            (3 * t**3 - 6 * t**2 + 4) / 6,
            (-3 * t**3 + 3 * t**2 + 3 * t + 1) / 6,
            t**3 / 6,
        ]
    )


def tables():
    weights = spline_weights()

    def along(blocks, first_block, points, first_point):
        out = np.zeros((blocks * KNOT, points))
        for block in range(blocks):
            for j in range(4):
                point = first_block + block + j - 1 - first_point
                if 0 <= point < points:
                    out[block * KNOT : (block + 1) * KNOT, point] = weights[j]
        return out

    along_z = along(NZ // KNOT, 0, PLANES, -1)
    halves = []
    for half in range(2):
        along_y = along(NY // KNOT, half * (NY // KNOT), CY, 0)
        halves.append(np.einsum("zp,yq->zypq", along_z, along_y).reshape(NZ * NY, CTL))
    high, low = split(np.stack(halves))
    widths = ((0, 0), (0, 0), (0, KPAD - CTL))
    high48, low48 = (np.pad(a, widths) for a in (high, low))
    out_table = np.concatenate([high48, low48, high48, low48], axis=2)
    backs = []
    for half in range(2):
        along_y = along(NY // KNOT, half * (NY // KNOT), CY, 0)
        backs.append(np.concatenate(split(np.kron(np.eye(PLANES), along_y).T), axis=0))
    back_table = np.stack(backs)
    along_x = along(NX // KNOT, 0, CX, 0)
    rows = np.zeros((128, 3 * NX))
    for c in range(3):
        rows[c * CX : (c + 1) * CX, c * NX : (c + 1) * NX] = along_x.T
    x_table = np.concatenate(split(rows), axis=0)
    return out_table, back_table, x_table


def halves_of(value):
    high = value.astype(BF)
    return high, (value - high.astype(F32)).astype(BF)


def block_terms(block, grad, weight_at, planes):
    weights = spline_weights()
    even = (weights[:2] + weights[:2, ::-1]) / 2
    odd = (weights[:2] - weights[:2, ::-1]) / 2

    def strip(y, carry):
        rows = pl.ds(pl.multiple_of(y * 8, 8), 8)
        for x in range(0, NX, WIDE):
            lanes = slice(x, x + WIDE)
            sums = [[[0.0, 0.0], [0.0, 0.0]] for _ in range(3)]
            for i in range(KNOT // 2):
                pair = []
                for z in (i, KNOT - 1 - i):
                    slopes = [grad[c, block * KNOT + z, rows, lanes] for c in range(3)]
                    weight, carry = weight_at(block * KNOT + z, y, lanes, slopes, carry)
                    pair.append([slope * weight for slope in slopes])
                for c in range(3):
                    both, apart = pair[0][c] + pair[1][c], pair[0][c] - pair[1][c]
                    for j in range(2):
                        sums[c][0][j] = sums[c][0][j] + float(even[j, i]) * both
                        sums[c][1][j] = sums[c][1][j] + float(odd[j, i]) * apart
            for c in range(3):
                (e0, e1), (o0, o1) = sums[c]
                at = slice(c * NX + x, c * NX + x + WIDE)
                for j, value in enumerate((e0 + o0, e1 + o1, e1 - o1, e0 - o0)):
                    if block == 0 or j == 3:
                        planes[block + j, rows, at] = value
                    else:
                        planes[block + j, rows, at] += value
        return carry

    return strip


def contracted(planes, back, x_table):
    high, low = halves_of(planes[...].reshape(PLANES * NY, 3 * NX))
    terms = jnp.dot(back, high, preferred_element_type=F32)
    rest = jnp.dot(back[:CTL], low, preferred_element_type=F32)
    high, low = halves_of(terms[:CTL] + (terms[CTL:] + rest))
    both = lax.dot_general(
        jnp.concatenate([high, low], 0),
        x_table[...],
        (((1,), (1,)), ((), ())),
        preferred_element_type=F32,
    )
    return both[:CTL, :128] + (both[:CTL, 128:] + both[CTL:, :128])


def interior_kernel(half, moving, fixed, grad, planes, z_edges, y_edges):
    lane = lax.broadcasted_iota(jnp.int32, (TILE, NX), 1)
    two = jnp.zeros((2, NX), F32)

    def plane(z, shifts):
        center = moving.at[z]
        for y in range(0, NY, TILE):
            here = slice(y, y + TILE)
            value = center[here]

            def at_z(k):
                return moving[z + k, here] if k in shifts else 0.0

            def at_y(k):
                first = y + k
                if first < 0:
                    return jnp.concatenate([two[: -first], center[0 : TILE + first]], 0)
                if first + TILE > NY:
                    return jnp.concatenate([center[first:NY], two[: first + TILE - NY]], 0)
                return center[first : first + TILE]

            def at_x(k):
                moved = pltpu.roll(value, (-k) % NX, 1)
                inside = lane < NX - k if k > 0 else lane >= -k
                return jnp.where(inside, moved, 0.0)

            for c, near in enumerate((at_z, at_y, at_x)):
                grad[c, z, here] = 8.0 * (near(1) - near(-1)) - (near(2) - near(-2))

    every = (-2, -1, 1, 2)

    def body(z, carry):
        plane(z, every)
        return carry

    plane(0, (1, 2))
    plane(1, (-1, 1, 2))
    lax.fori_loop(2, NZ - 2, body, 0, unroll=4)
    plane(NZ - 2, (-2, -1, 1))
    plane(NZ - 1, (-2, -1))

    def weight_at(z, y, lanes, slopes, carry):
        rows = pl.ds(pl.multiple_of(y * 8, 8), 8)
        return moving[z, rows, lanes] - fixed[z, rows, lanes], carry

    for block in range(NZ // KNOT):
        lax.fori_loop(0, NY // 8, block_terms(block, grad, weight_at, planes), 0, unroll=2)
    for e, z in enumerate(EDGES):
        z_edges[e] = moving[z] - fixed[z]
    rows = pl.ds(pl.multiple_of((1 - half[0]) * (NY - 8), 8), 8)
    y_edges[...] = moving[:, rows, :] - fixed[:, rows, :]


def edge_kernel(
    half, parity, inner, outer, y_rows, z_edges, y_edges, back, xt, grad_in, planes_in, grad, planes, out
):
    del grad_in, planes_in
    lower = parity[0] == 0
    weights = spline_weights()

    def strip(y, carry):
        rows = pl.ds(pl.multiple_of(y * 8, 8), 8)
        near, far = (jnp.where(lower, outer[z, rows], inner[z, rows]) for z in (1, 0))
        above, beyond = (jnp.where(lower, inner[z, rows], outer[z, rows]) for z in (0, 1))
        slopes = (far - 8.0 * near, near, -above, 8.0 * above - beyond)
        for e, z in enumerate(EDGES):
            grad[0, z, rows] += slopes[e]
            term = slopes[e] * z_edges[e, rows]
            for j in range(4):
                at = z // KNOT + j
                planes[at, rows, 0:NX] += float(weights[j, z % KNOT]) * term
        return carry

    lax.fori_loop(0, NY // 8, strip, 0)

    upper = half[0] == 0
    rows = pl.ds(pl.multiple_of((1 - half[0]) * (NY - 8), 8), 8)
    sub = lax.broadcasted_iota(jnp.int32, (8, NX), 0)

    def coefficient(when_upper, otherwise):
        def column(entries):
            value = jnp.zeros((8, NX), F32)
            for row, entry in entries.items():
                value = jnp.where(sub == row, entry, value)
            return value

        return jnp.where(upper, column(when_upper), column(otherwise))

    on_first = coefficient({6: -1.0, 7: 8.0}, {0: 1.0})
    on_second = coefficient({7: -1.0}, {0: -8.0, 1: 1.0})
    for block in range(NZ // KNOT):
        sums = [0.0] * 4
        for i in range(KNOT):
            z = block * KNOT + i
            slope = on_first * y_rows[z, 0:1] + on_second * y_rows[z, 1:2]
            grad[1, z, rows] += slope
            term = slope * y_edges[z]
            sums = [total + float(weights[j, i]) * term for j, total in enumerate(sums)]
        for j, total in enumerate(sums):
            planes[block + j, rows, NX : 2 * NX] += total
    out[...] = contracted(planes, back[half[0]], xt) * (-data_weight / 12.0)


def hessian_kernel(half, ctl, base, grad, front, back, xt, out, spread, field, planes):
    high, low = halves_of(ctl[...])
    first, second = xt[:128], xt[128:]
    value = jnp.dot(jnp.concatenate([high, low], 0), first, preferred_element_type=F32)
    value = value[:CTL] + (value[CTL:] + jnp.dot(high, second, preferred_element_type=F32))
    value = jnp.concatenate([value, jnp.zeros((KPAD - CTL, 3 * NX), F32)], 0)
    high, low = halves_of(value)
    for j, part in enumerate((high, high, low, low)):
        spread[j * KPAD : (j + 1) * KPAD] = part
    square = jnp.zeros((8, WIDE), F32)

    for block in range(NZ // KNOT):
        at_rows = slice(block * ROWS, (block + 1) * ROWS)
        field[...] = jnp.dot(front[half[0], at_rows], spread[...], preferred_element_type=F32)

        def weight_at(z, y, lanes, slopes, carry):
            rows = pl.ds(pl.multiple_of(z % KNOT * NY + y * 8, 8), 8)
            weight = 0.0
            for c in range(3):
                at = slice(c * NX + lanes.start, c * NX + lanes.stop)
                weight = weight + slopes[c] * field[rows, at]
            return weight, carry + weight * weight

        strip = block_terms(block, grad, weight_at, planes)
        square = lax.fori_loop(0, NY // 8, strip, square, unroll=2)

    scale = data_weight / 144.0
    whole = ctl[...]
    owned = whole[CY : 3 * CY]
    sub = lax.broadcasted_iota(jnp.int32, (2 * CY, 128), 0) % CY
    lane = lax.broadcasted_iota(jnp.int32, (2 * CY, 128), 1) % CX
    near = whole[0 : 2 * CY] + whole[2 * CY : 4 * CY]
    near += jnp.where(sub > 0, pltpu.roll(owned, 1, 0), 0.0)
    near += jnp.where(sub < CY - 1, pltpu.roll(owned, 2 * CY - 1, 0), 0.0)
    near += jnp.where(lane > 0, pltpu.roll(owned, 1, 1), 0.0)
    near += jnp.where(lane < CX - 1, pltpu.roll(owned, 127, 1), 0.0)
    smooth = (0.5 * smooth_weight) * (6.0 * owned - near)
    out[:CTL] = contracted(planes, back[half[0]], xt) * scale
    out[CY : 3 * CY] += smooth
    first = base[...]

    def total(value):
        return jnp.sum(jnp.sum(value, axis=0, keepdims=True), axis=1, keepdims=True)

    whole_square = total(square) * scale + total(smooth * owned)
    lines = [
        0.5 * total(first * first),
        0.5 * total(first * owned),
        0.5 * total(owned * owned),
        whole_square,
    ]
    which = lax.broadcasted_iota(jnp.int32, (8, 128), 0)
    tile = jnp.zeros((8, 128), F32)
    for j, line in enumerate(lines):
        tile = jnp.where(which == j, line, tile)
    out[CTL:] = tile


VMEM_SPEC = pl.BlockSpec(memory_space=pltpu.VMEM)
HBM_SPEC = pl.BlockSpec(memory_space=pltpu.HBM)
SMEM_SPEC = pl.BlockSpec(memory_space=pltpu.SMEM)
PARAMS = pltpu.CompilerParams(vmem_limit_bytes=24 * 1024 * 1024)
RIMS_MIB = 52
SMALL_PARAMS = pltpu.CompilerParams(vmem_limit_bytes=8 * 1024 * 1024)


GRAD_SHAPE = jax.ShapeDtypeStruct((3, NZ, NY, NX), F32)
PLANES_SHAPE = jax.ShapeDtypeStruct((PLANES, NY, 3 * NX), F32)
CTL_SHAPE = jax.ShapeDtypeStruct((CTL, 128), F32)


def interior_pass(half, moving, fixed):
    return pl.pallas_call(
        interior_kernel,
        in_specs=[SMEM_SPEC] + [VMEM_SPEC] * 2,
        out_specs=[VMEM_SPEC] * 4,
        out_shape=[
            GRAD_SHAPE,
            PLANES_SHAPE,
            jax.ShapeDtypeStruct((len(EDGES), NY, NX), F32),
            jax.ShapeDtypeStruct((NZ, 8, NX), F32),
        ],
        compiler_params=SMALL_PARAMS,
        cost_estimate=pl.CostEstimate(flops=100_000_000, bytes_accessed=40_000_000, transcendentals=0),
        name="interior",
    )(half, moving, fixed)


def edge_pass(half, parity, inner, outer, y_rows, z_edges, y_edges, back_table, x_table, grad, planes):
    grad, _, part = pl.pallas_call(
        edge_kernel,
        in_specs=[SMEM_SPEC] * 2 + [VMEM_SPEC] * 9,
        out_specs=[VMEM_SPEC] * 3,
        out_shape=[GRAD_SHAPE, PLANES_SHAPE, CTL_SHAPE],
        input_output_aliases={9: 0, 10: 1},
        compiler_params=PARAMS,
        name="edge",
    )(half, parity, inner, outer, y_rows, z_edges, y_edges, back_table, x_table, grad, planes)
    return grad, part


def hessian_pass(half, ctl, base, grad, front_table, back_table, x_table):
    return pl.pallas_call(
        hessian_kernel,
        in_specs=[SMEM_SPEC] + [VMEM_SPEC] * 6,
        out_specs=VMEM_SPEC,
        scratch_shapes=[
            pltpu.VMEM((4 * KPAD, 3 * NX), BF),
            pltpu.VMEM((ROWS, 3 * NX), F32),
            pltpu.VMEM((PLANES, NY, 3 * NX), F32),
        ],
        out_shape=jax.ShapeDtypeStruct((CTL + 8, 128), F32),
        compiler_params=PARAMS,
        name="hessian",
    )(half, ctl, base, grad, front_table, back_table, x_table)


def rims_kernel(half, parity, moving, inner, outer, y_rim, tile, sems):
    half, parity = half[0], parity[0]
    top, bottom = NZ - 2, 0
    copies = [
        pltpu.make_async_copy(
            moving.at[pl.ds(jnp.where(parity == 0, top, bottom), 2)], inner, sems.at[0]
        ),
        pltpu.make_async_copy(
            moving.at[pl.ds(jnp.where(parity == 0, bottom, top), 2)], outer, sems.at[1]
        ),
        pltpu.make_async_copy(
            moving.at[:, pl.ds(pl.multiple_of((1 - half) * (NY - 8), 8), 8)], tile, sems.at[2]
        ),
    ]
    for copy in copies:
        copy.start()
    for copy in copies:
        copy.wait()
    y_rim[...] = jnp.where(half == 0, tile[:, 6:8, :], tile[:, 0:2, :])


def rims_pass(half, parity, moving):
    return pl.pallas_call(
        rims_kernel,
        in_specs=[SMEM_SPEC, SMEM_SPEC, HBM_SPEC],
        out_specs=[VMEM_SPEC] * 3,
        out_shape=[jax.ShapeDtypeStruct(shape, F32) for shape in ((2, NY, NX), (2, NY, NX), (NZ, 2, NX))],
        scratch_shapes=[pltpu.VMEM((NZ, 8, NX), F32), pltpu.SemaphoreType.DMA((3,))],
        compiler_params=pltpu.CompilerParams(vmem_limit_bytes=RIMS_MIB * 1024 * 1024),
        name="rims",
    )(half, parity, moving)


def held_kernel(*refs):
    for source, target in zip(refs[: len(refs) // 2], refs[len(refs) // 2 :]):
        target[...] = source[...]


def held(*rims):
    return pl.pallas_call(
        held_kernel,
        in_specs=[VMEM_SPEC] * len(rims),
        out_specs=[VMEM_SPEC] * len(rims),
        out_shape=[jax.ShapeDtypeStruct(rim.shape, F32) for rim in rims],
        compiler_params=SMALL_PARAMS,
        cost_estimate=pl.CostEstimate(flops=20_000_000_000, bytes_accessed=60_000_000, transcendentals=0),
        name="held",
    )(*rims)


def placed_kernel(solution, residual, solution_out, residual_out):
    for value, out in ((solution[...], solution_out), (residual[...], residual_out)):
        for c in range(3):
            moved = pltpu.roll(value, (-c * CX) % 128, 1) if c else value
            for plane in range(2):
                out[c, plane] = moved[plane * CY : (plane + 1) * CY, :CX]


def placed(solution, residual):
    return pl.pallas_call(
        placed_kernel,
        in_specs=[VMEM_SPEC] * 2,
        out_specs=[VMEM_SPEC] * 2,
        out_shape=[jax.ShapeDtypeStruct((3, 2, CY, CX), F32)] * 2,
        compiler_params=SMALL_PARAMS,
        name="placed",
    )(solution, residual)


def swapped(value):
    return lax.ppermute(value, "gy", [(0, 1), (1, 0)])


def paired(value, mask):
    count = lax.axis_size("gz")
    return lax.ppermute(value, "gz", [(i, i ^ mask) for i in range(count)])


def stage(value, *masks):
    return value + sum(paired(value, mask) for mask in masks)


def outer_paired(value):
    count = lax.axis_size("gz")
    pairs = [(i, i + 1) for i in range(1, count - 1, 2)]
    return lax.ppermute(value, "gz", pairs + [(j, i) for i, j in pairs])


def far_paired(value):
    count = lax.axis_size("gz")
    pairs = [(i, i + 3) for i in range(0, count - 3, 2)]
    return lax.ppermute(value, "gz", pairs + [(j, i) for i, j in pairs])


def pair_sum(lower, own, other):
    first, second = jnp.where(lower, own, other), jnp.where(lower, other, own)
    widths = ((0, 2 * CY), (0, 0)), ((2 * CY, 0), (0, 0))
    return jnp.pad(first, widths[0]) + jnp.pad(second, widths[1])


def outer_terms(lower, seven):
    return outer_paired(jnp.where(lower, seven[: 3 * CY], seven[4 * CY :]))


def all_planes(lower, inside, part):
    part = (part + swapped(part))[:CTL]
    seven = pair_sum(lower, part, paired(part, 1))
    three = outer_terms(lower, seven)
    one = far_paired(jnp.where(lower, seven[6 * CY :], seven[:CY]))
    low = jnp.concatenate([three, jnp.zeros((CY, 128), F32), one], 0) + seven[: 5 * CY]
    high = jnp.concatenate([one, jnp.zeros((CY, 128), F32), three], 0) + seven[2 * CY :]
    return inside * jnp.where(lower, low, high)


def local(moving, fixed):
    slab = lax.axis_index("gz").astype(jnp.int32)
    half = lax.axis_index("gy").astype(jnp.int32).reshape(1)
    parity = (slab % 2).reshape(1)
    lower = slab % 2 == 0
    at = slab * (2 * CY) - CY + lax.broadcasted_iota(jnp.int32, (CTL, 128), 0)
    inside = ((at >= 0) & (at < lax.axis_size("gz") * (2 * CY))).astype(F32)
    moving, half, parity, lower, inside = lax.optimization_barrier(
        (moving, half, parity, lower, inside)
    )
    front, back, xt = (jnp.asarray(a) for a in tables())

    inner, outer, y_rim = held(*rims_pass(half, parity, moving))
    inner = paired(inner, 1)
    outer = outer_paired(outer)
    y_rows = swapped(y_rim)

    grad, planes, z_edges, y_edges = interior_pass(half, moving, fixed)
    grad, part = edge_pass(
        half, parity, inner, outer, y_rows, z_edges, y_edges, back, xt, grad, planes
    )
    b_planes = all_planes(lower, inside, part)
    b = b_planes[CY : 3 * CY]
    part = hessian_pass(half, b_planes, b, grad, front, back, xt)
    u_planes = all_planes(lower, inside, part)
    u = u_planes[CY : 3 * CY]
    both = hessian_pass(half, u_planes, b, grad, front, back, xt)
    both = both + swapped(both)
    other = paired(both, 1)
    seven = pair_sum(lower, both[:CTL], other[:CTL])
    sums = both[CTL:] + other[CTL:]
    three = outer_terms(lower, seven)
    sums = stage(sums, 2, 4, 6)
    sums, three = lax.optimization_barrier((sums, three))
    sums = stage(stage(sums, 8), 16, 32, 48)
    v_low = seven[CY : 3 * CY] + three[CY:]
    v_high = seven[3 * CY : 5 * CY] + jnp.pad(three[:CY], ((CY, 0), (0, 0)))
    v = jnp.where(lower, v_low, v_high)

    bb, bu, uu, uv = (sums[j : j + 1] for j in range(4))
    a0 = bb / bu
    rr1 = bb - 2.0 * a0 * bu + a0 * a0 * uu
    beta = rr1 / bb
    more = 1.0 + beta
    a1 = rr1 / (more * more * bu - 2.0 * more * a0 * uu + a0 * a0 * uv)
    solution = a0 * b + a1 * (more * b - a0 * u)
    residual = (b - a0 * u) - a1 * (more * u - a0 * v)

    return tuple(placed(solution, residual))


def solution(mesh):
    in_specs = (P("gz", "gy", None), P("gz", "gy", None))
    out_specs = (P(None, "gz", None, None), P(None, "gz", None, None))
    return jax.shard_map(local, mesh=mesh, in_specs=in_specs, out_specs=out_specs, check_vma=False)
```
